256 devices in a mesh: dp: 16 (over y, x_hi, core), seq: 16 (over x_lo, z).
Axes of the slice: x: 4 (x_hi: 2, x_lo: 2; x = x_hi * 2 + x_lo), y: 4, z: 8, core: 2. Of those that a mesh axis runs over, the one named last changes fastest.
Arguments:
- stored: bfloat16 [16, 2048, 6144], P('dp', 'seq'), may hold values from -6 to 6
- source_row: int32 [16, 256, 1], P(None, 'seq'), may hold values from 0 to 15; in each aligned block of 16 rows (0 to 15, 16 to 31, ..., all dimensions but the last counted through in order) at most 2 rows name the same one
- source_span: int32 [16, 256], P(None, 'seq'), may hold values from 0 to 15
- segments: int32 [16, 2048], P('dp', 'seq'), may hold values from 0 to 127, never falling along the last dimension, each value on 1 to 256 neighbouring positions
- short_weight: float32 [3, 3, 2048], replicated, may hold values from -3 to 3
- filter_taps: float32 [2048, 2048], P('seq'), may hold values from -2 to 2
- cotangent: bfloat16 [16, 2048, 2048], P('dp', 'seq'), may hold values from -6 to 6
Outputs:
- mixed: bfloat16 [16, 2048, 2048], P('dp', 'seq')
- grad_stored: bfloat16 [16, 2048, 6144], P('dp', 'seq')
- grad_filter: float32 [2048, 2048], P('seq')
- grad_short: float32 [3, 3, 2048], replicated
The draws below stay inside these ranges and needn't reach their ends.
Inputs may be any that keep to these rules, and one draw needn't show every extreme that they name: `source_row`: within the 16 slots of one sequence that share one value of j // 16, no source sequence is named more than 2 times, and some such group names one exactly 2 times.
All inputs are finite; a program needn't handle non-finite values.
Results may differ from the reference program's by a relative error of at most 0.018.
Values may be sent and summed in bfloat16 or wider, within the bound.
No kernel may reach another device: no remote copies, remote signals or barrier semaphores. Data moves between devices by JAX's collectives and lax.ppermute only.
A program may use at most 128 MiB of HBM per device.

```python
import math
import jax
import jax.numpy as jnp
import numpy as np
from jax import lax

C = 2048
TOK_DEV = 128
SPANS = 16
MOST = 2
BATCH = 16
LENGTH = 2048
N_DP = 16
N_SEQ = 16


def draw_filter_taps(key, part):
    tau_key = jax.random.fold_in(key, 11)
    noise_key = jax.random.fold_in(key, 12)
    position = jnp.arange(LENGTH, dtype=jnp.float32)[:, None]
    tau = jnp.exp(jax.random.uniform(tau_key, (C,), jnp.float32, math.log(24.0), math.log(4.0 * LENGTH)))
    noise = jnp.clip(jax.random.normal(noise_key, (LENGTH, C), jnp.float32), -6.0, 6.0)
    amplitude = jnp.sqrt(1.0 - jnp.exp(-2.0 / tau))[None, :]
    return (noise * amplitude * jnp.exp(-position / tau[None, :])).astype(jnp.float32)


def set_ends(drawn, rng, least, top_value):
    place = [jax.random.randint(jax.random.fold_in(rng, axis), (), 0, length) for axis, length in enumerate(drawn.shape)]
    widest = drawn.shape.index(max(drawn.shape))
    neighbour = place[:widest] + [(place[widest] + 1) % drawn.shape[widest]] + place[widest + 1:]
    return drawn.at[tuple(place)].set(least).at[tuple(neighbour)].set(top_value)


def block_levels(stream_key, dims, split, least, high):
    loudness = 1.0
    for dim, shards_of in split:
        draws = jax.random.uniform(jax.random.fold_in(jax.random.fold_in(stream_key, 6), dim), (shards_of,), jnp.float32, least / len(split), high / len(split))
        loudness = loudness * jnp.repeat(jnp.exp(draws), dims[dim] // shards_of).reshape((-1,) + (1,) * (len(dims) - 1 - dim))
    return loudness


def length_profile(number_of, total, reach, skew):
    weights = [(1 << 20) // math.isqrt(standing ** skew) + 1 for standing in range(2, number_of + 1)]
    rest, holding = total - reach - (number_of - 1), [1] * (number_of - 1)
    while rest > 0:
        movable = [i for i in range(number_of - 1) if holding[i] < reach]
        pool, left = sum([weights[i] for i in movable]), rest
        for i in movable:
            addition = min(reach - holding[i], max(1, left * weights[i] // pool), rest)
            holding[i] = holding[i] + addition
            rest = rest - addition
    return np.array([reach] + holding)


def ragged(own_key, amount, total, reach, lean):
    if amount == 2:
        one = jax.random.randint(own_key, (), max(1, total - reach), min(reach, total - 1) + 1)
        return jnp.stack([one, total - one])
    tallies = jnp.asarray(length_profile(amount, total, reach, lean), jnp.int32)
    couples = (amount - 1) // 2
    giver, sink = tallies[1:1 + 2 * couples:2], tallies[2:2 + 2 * couples:2]
    slack = jnp.minimum(giver - 1, reach - sink)
    shifted = jax.random.randint(jax.random.fold_in(own_key, 1), (couples,), 0, 1 << 20) % (slack + 1)
    tallies = tallies.at[1:1 + 2 * couples:2].set(giver - shifted).at[2:2 + 2 * couples:2].set(sink + shifted)
    return tallies[jax.random.permutation(jax.random.fold_in(own_key, 2), amount)]


def assign_block(stream_key, own, number, rows, number_of, top, bound, skew):
    ranking = jax.random.permutation(stream_key, number_of)
    crowded, usual = shares(number_of, rows * top, bound, skew, True), shares(number_of, rows * top, bound, skew, False)
    places = jnp.arange(number_of)

    def named(lengths, rotation):
        used = int((lengths > 0).sum())
        fixed = max(1, used // 4)
        passed = fixed + (places - fixed + rotation * (used - fixed)) % max(1, number_of - fixed)
        return jnp.zeros((number_of,), jnp.int32).at[ranking[jnp.where(places < fixed, places, passed)]].set(jnp.asarray(lengths, jnp.int32))

    lengths = jnp.where(number % 4 == 0, named(crowded, number // 4), named(usual, number - number // 4 - 1))
    mixed = jax.random.permutation(jax.random.fold_in(own, 3), number_of)
    giver, taker = mixed[0:number_of // 2 * 2:2], mixed[1:number_of // 2 * 2:2]
    room = jnp.minimum(lengths[giver] - 1, bound - lengths[taker]) // 2
    room = jnp.where((giver == ranking[0]) | (taker == ranking[0]) | (lengths[taker] == 0), 0, jnp.maximum(room, 0))
    passed = jax.random.randint(jax.random.fold_in(own, 4), (number_of // 2,), 0, 1 << 20) % (room + 1)
    lengths = lengths.at[giver].add(-passed).at[taker].add(passed)
    labels = jnp.searchsorted(jnp.cumsum(lengths), jnp.arange(rows * top), side="right").astype(jnp.int32)
    grid = labels.reshape(top, rows).T
    grid = grid[jax.random.permutation(jax.random.fold_in(own, 1), rows)]
    rotation = jax.random.randint(jax.random.fold_in(own, 2), (rows, 1), 0, top)
    return jnp.take_along_axis(grid, (jnp.arange(top)[None, :] + rotation) % top, axis=1)


def shares(count, total, reach, skew, full):
    portions = [(1 << 20) // math.isqrt(rank ** skew) + 1 for rank in range(1, count + 1)]
    largest = reach if full else min(reach, max(-(-total // count), total * portions[0] // sum(portions)))
    least = 1 if total - largest >= count - 1 else 0
    given, rest = [largest] + [least] * (count - 1), total - largest - least * (count - 1)
    while rest > 0:
        candidates = [i for i in range(1, count) if given[i] < largest] or [i for i in range(1, count) if given[i] < reach]
        pool, remaining = sum([portions[i] for i in candidates]), rest
        for i in candidates:
            extra = min(reach - given[i], max(1, remaining * portions[i] // pool), rest)
            given[i] = given[i] + extra
            rest = rest - extra
    return np.array(given)


def bell_draw(own_key, dims, deviation, reach, pieces=(), kind=jnp.bfloat16):
    level = block_levels(own_key, dims, pieces, -0.22, 0.18) if pieces else 1.0
    drawn = jax.random.normal(own_key, dims, jnp.float32) * deviation * level
    return jnp.minimum(jnp.maximum(drawn, -reach), reach).astype(kind)


def setup_inputs(seed: int = 0) -> dict:
    arg_keys = jax.random.split(jax.random.key(seed), 8)
    stored = bell_draw(arg_keys[0], (BATCH, LENGTH, 3 * C), 1.0, 6.0, ((0, 16), (1, 16)))
    source_row_keys = jax.random.split(jax.random.fold_in(arg_keys[1], 1), BATCH * (N_SEQ * SPANS) // SPANS)
    source_row_turns = jax.random.permutation(jax.random.fold_in(arg_keys[1], 3), BATCH * (N_SEQ * SPANS) // SPANS)
    source_row = jax.vmap(lambda own, number: assign_block(jax.random.fold_in(arg_keys[1], 2), own, number, SPANS, N_DP, 1, MOST, 2))(source_row_keys, source_row_turns).reshape((BATCH, N_SEQ * SPANS, 1))
    source_span = set_ends(jax.random.randint(arg_keys[2], (BATCH, N_SEQ * SPANS), 0, SPANS), jax.random.fold_in(arg_keys[2], 1), 0, SPANS - 1).astype(jnp.int32)
    segments = jax.vmap(lambda own: jnp.searchsorted(jnp.cumsum(ragged(own, LENGTH // 16, LENGTH, min(256, LENGTH // 2), 1)), jnp.arange(LENGTH), side="right"))(jax.random.split(arg_keys[3], BATCH)).reshape((BATCH, LENGTH)).astype(jnp.int32)
    short_weight = bell_draw(arg_keys[4], (3, 3, C), 0.5, 3.0, (), jnp.float32)
    filter_taps = draw_filter_taps(jax.random.fold_in(arg_keys[7], 71), 0)
    cotangent = bell_draw(arg_keys[6], (BATCH, LENGTH, C), 1.0, 6.0, ((0, 16), (1, 16)))
    return dict(stored=stored, source_row=source_row, source_span=source_span, segments=segments, short_weight=short_weight, filter_taps=filter_taps, cotangent=cotangent)


def lagged(values, shift):
    return jnp.concatenate([jnp.zeros((shift, values.shape[1]), values.dtype), values[:-shift]], axis=0)


def leading(values, shift):
    return jnp.concatenate([values[shift:], jnp.zeros((shift, values.shape[1]), values.dtype)], axis=0)


def one_sequence(rows, ids, grad_in, taps, filter_spec):
    values = rows.astype(jnp.float32)
    same_one = jnp.concatenate([jnp.zeros((1,), bool), ids[1:] == ids[:-1]]).astype(jnp.float32)[:, None]
    same_two = jnp.concatenate([jnp.zeros((2,), bool), ids[2:] == ids[:-2]]).astype(jnp.float32)[:, None]
    lag_one = lagged(values, 1) * same_one
    lag_two = lagged(values, 2) * same_two
    hat = taps[0] * values + taps[1] * lag_one + taps[2] * lag_two
    key_hat = hat[:, :C]
    value_hat = hat[:, C:2 * C]
    query_hat = hat[:, 2 * C:]
    product = (key_hat * value_hat).astype(jnp.bfloat16)
    length = 2 * LENGTH
    mix_spec = jnp.fft.rfft(product.astype(jnp.float32), n=length, axis=0)
    conv = jnp.fft.irfft(filter_spec * mix_spec, n=length, axis=0)[:LENGTH].astype(jnp.bfloat16)
    conv_f = conv.astype(jnp.float32)
    mixed = (query_hat * conv_f).astype(jnp.bfloat16)
    grad_out = grad_in.astype(jnp.float32)
    grad_conv = (grad_out * query_hat).astype(jnp.bfloat16)
    grad_query = grad_out * conv_f
    cot_spec = jnp.fft.rfft(grad_conv.astype(jnp.float32), n=length, axis=0)
    grad_product = jnp.fft.irfft(jnp.conj(filter_spec) * cot_spec, n=length, axis=0)[:LENGTH].astype(jnp.bfloat16)
    filter_grad = jnp.fft.irfft(jnp.conj(mix_spec) * cot_spec, n=length, axis=0)[:LENGTH].astype(jnp.float32)
    grad_prod_f = grad_product.astype(jnp.float32)
    grad_hat = jnp.concatenate([grad_prod_f * value_hat, grad_prod_f * key_hat, grad_query], axis=1)
    tap_terms = jnp.stack([jnp.sum(grad_hat * values, axis=0), jnp.sum(grad_hat * lag_one, axis=0),
                           jnp.sum(grad_hat * lag_two, axis=0)])
    grad_rows = taps[0] * grad_hat + taps[1] * leading(grad_hat * same_one, 1) + taps[2] * leading(grad_hat * same_two, 2)
    return mixed, grad_rows.astype(jnp.bfloat16), filter_grad, tap_terms


def reference(stored, source_row, source_span, segments, short_weight, filter_taps, cotangent):
    span_rows = TOK_DEV // SPANS
    slot_count = N_SEQ * SPANS
    taps = jnp.transpose(short_weight, (1, 0, 2)).reshape(3, 3 * C)
    filter_spec = jnp.fft.rfft(filter_taps, n=2 * LENGTH, axis=0)
    blocks = stored.reshape(BATCH, N_SEQ, SPANS, span_rows, 3 * C)
    block_seq = jnp.arange(slot_count, dtype=jnp.int32) // SPANS

    def one(index):
        source = source_row[index, :, 0]
        span = source_span[index]
        rows = blocks[source, block_seq, span].reshape(LENGTH, 3 * C)
        return one_sequence(rows, segments[index], cotangent[index], taps, filter_spec)

    mixed, grad_rows, filter_grads, tap_parts = lax.map(one, jnp.arange(BATCH, dtype=jnp.int32))
    grad_filter = jnp.sum(filter_grads, axis=0)
    grad_short = jnp.transpose(jnp.sum(tap_parts, axis=0).reshape(3, 3, C), (1, 0, 2))
    accum = jnp.zeros((BATCH, N_SEQ, SPANS, span_rows, 3 * C), jnp.float32)
    seq_all = jnp.broadcast_to(block_seq[None, :], (BATCH, slot_count))
    terms = grad_rows.reshape(BATCH, slot_count, span_rows, 3 * C).astype(jnp.float32)
    accum = accum.at[source_row[:, :, 0], seq_all, source_span].add(terms)
    grad_stored = accum.reshape(BATCH, LENGTH, 3 * C).astype(jnp.bfloat16)
    return mixed, grad_stored, grad_filter, grad_short
```

```python
import functools
import math

import jax
import jax.numpy as jnp
import numpy as np
from jax import lax
from jax.experimental import pallas as pl
from jax.experimental.pallas import tpu as pltpu
from jax.sharding import PartitionSpec as P

MOST = 2
CHUNK = 256
LANES = 128
HALO = 8
F32 = jnp.float32
BF16 = jnp.bfloat16


def shifted(value, axis, by):
    length = lax.axis_size(axis)
    pairs = [(i, i + by) for i in range(length) if 0 <= i + by < length]
    return lax.ppermute(value, axis, pairs)


def exchange(value, axis):
    return lax.all_to_all(value, axis, 0, 0, tiled=True)


def dot(left, right):
    return jnp.dot(left, right, preferred_element_type=F32)


def halves(value):
    high = value.astype(BF16)
    return high, (value - high.astype(F32)).astype(BF16)


def dot_three(left_high, left_low, value):
    high, low = halves(value)
    return dot(left_high, high) + (dot(left_high, low) + dot(left_low, high))


def outer_tables():
    blocks = np.arange(16)
    forward = [np.ones(16), np.cos(np.pi * blocks)]
    back = [np.ones(16), np.cos(np.pi * blocks)]
    for k in range(1, 16):
        angle = 2.0 * np.pi * k * blocks / 32.0
        forward += [np.cos(angle), -np.sin(angle)]
        back += [2.0 * np.cos(angle), -2.0 * np.sin(angle)]
    return np.stack(forward), np.stack(back, axis=1) / 4096.0


def numpy_halves(table):
    high = _round(table)
    return high, _round(table - high)


def _round(table):
    return np.asarray(table, np.float32).astype(jnp.bfloat16).astype(np.float64)


def spread(table, by):
    rows, cols = table.shape
    eye = jnp.eye(by, dtype=F32)
    wide = jnp.asarray(table, F32)[:, None, :, None] * eye[None, :, None, :]
    return wide.reshape(rows * by, cols * by).astype(BF16)


def table_kernel(fc_ref, fs_ref, row_ref, col_ref, dh_ref, dl_ref, eh_ref, el_ref):
    fc = fc_ref[...]
    fs = fs_ref[...]

    def put(high_ref, low_ref, r, c, value):
        high, low = halves(value)
        where = (0, pl.ds(r * LANES, LANES), pl.ds(c * LANES, LANES))
        high_ref[where] = high
        low_ref[where] = low

    wc = row_ref[0, 0:1, :]
    ws = row_ref[0, 1:2, :]
    cos = fc * wc - fs * ws
    sin = fs * wc + fc * ws
    put(dh_ref, dl_ref, 0, 0, cos)
    put(dh_ref, dl_ref, 0, 1, sin)
    put(dh_ref, dl_ref, 1, 0, -sin)
    put(dh_ref, dl_ref, 1, 1, cos)
    wc = col_ref[0, :, 0:1]
    ws = col_ref[0, :, 1:2]
    cos = fc * wc - fs * ws
    sin = fs * wc + fc * ws
    put(eh_ref, el_ref, 0, 0, cos)
    put(eh_ref, el_ref, 0, 1, -sin)
    put(eh_ref, el_ref, 1, 0, sin)
    put(eh_ref, el_ref, 1, 1, cos)


def inner_tables():
    inner = jnp.arange(LANES, dtype=jnp.int32)
    turn = (inner[:, None] * inner[None, :] % LANES).astype(F32) * (2.0 * math.pi / LANES)
    order = jnp.asarray([0, 16] + list(range(1, 16)), jnp.int32)
    twist = (order[:, None] * inner[None, :]).astype(F32) * (2.0 * math.pi / 4096)
    rows = jnp.stack([jnp.cos(twist), jnp.sin(twist)], axis=1)
    cols = jnp.stack([jnp.cos(twist), jnp.sin(twist)], axis=2)
    whole = pl.BlockSpec((LANES, LANES), lambda k: (0, 0))
    out = pl.BlockSpec((1, 2 * LANES, 2 * LANES), lambda k: (k, 0, 0))
    shape = jax.ShapeDtypeStruct((17, 2 * LANES, 2 * LANES), BF16)
    return pl.pallas_call(
        table_kernel,
        grid=(17,),
        in_specs=[
            whole,
            whole,
            pl.BlockSpec((1, 2, LANES), lambda k: (k, 0, 0)),
            pl.BlockSpec((1, LANES, 2), lambda k: (k, 0, 0)),
        ],
        out_specs=[out] * 4,
        out_shape=[shape] * 4,
        name="inner_tables",
    )(jnp.cos(turn), jnp.sin(turn), rows, cols)


def gather_kernel(k_ref, v_ref, q_ref, take_ref, pk_ref, pv_ref, pq_ref, mask_ref, w_ref, cot_ref, taps_ref, out_ref, xs):
    take = take_ref[...]
    m1 = mask_ref[0:128, 0:1]
    m2 = mask_ref[0:128, 1:2]
    hats = []
    for s, (ref, prev) in enumerate(((k_ref, pk_ref), (v_ref, pv_ref), (q_ref, pq_ref))):
        x = dot(take, ref[...])
        xs[s, 6:8, :] = prev[...].astype(F32)
        xs[s, 8:136, :] = x
        w = w_ref[:, s, :]
        lag_one = xs[s, 7:135, :] * m1
        lag_two = xs[s, 6:134, :] * m2
        hats.append(w[0:1] * x + w[1:2] * lag_one + w[2:3] * lag_two)
    product = (hats[0] * hats[1]).astype(BF16)
    grad_conv = (cot_ref[...].astype(F32) * hats[2]).astype(BF16)
    filt = taps_ref[...].astype(BF16)
    for h in range(CHUNK // LANES):
        at = slice(h * LANES, (h + 1) * LANES)
        out_ref[h, 0:128, :] = product[:, at]
        out_ref[h, 128:256, :] = grad_conv[:, at]
        out_ref[h, 256:384, :] = filt[:, at]


def stream_specs(rows, chunks):
    return [pl.BlockSpec((rows, CHUNK), lambda c, s=s: (0, s * chunks + c)) for s in range(3)]


def gather_rows(received, take, prev, masks, weights, cot, filter_taps):
    chunks = cot.shape[1] // CHUNK
    per = CHUNK // LANES
    return pl.pallas_call(
        gather_kernel,
        grid=(chunks,),
        in_specs=stream_specs(256, chunks)
        + [pl.BlockSpec((128, 256), lambda c: (0, 0))]
        + stream_specs(2, chunks)
        + [
            pl.BlockSpec((136, 2), lambda c: (0, 0)),
            pl.BlockSpec((3, 3, CHUNK), lambda c: (0, 0, c)),
            pl.BlockSpec((128, CHUNK), lambda c: (0, c)),
            pl.BlockSpec((128, CHUNK), lambda c: (0, c)),
        ],
        out_specs=pl.BlockSpec((per, 384, LANES), lambda c: (c, 0, 0)),
        out_shape=jax.ShapeDtypeStruct((chunks * per, 384, LANES), BF16),
        scratch_shapes=[pltpu.VMEM((3, 136, CHUNK), F32)],
        name="gather_rows",
    )(received, received, received, take, prev, prev, prev, masks, weights, cot, filter_taps)


def conv_kernel(in_ref, dh_ref, dl_ref, eh_ref, el_ref, fh_ref, fl_ref, bh_ref, bl_ref, out_ref, ah, al, zh, zl):
    step = pl.program_id(0)
    wide = 3 * LANES

    @pl.when(step == 0)
    def _():
        nothing = jnp.zeros((LANES, wide), BF16)
        for where in (1, 3):
            ah[where] = nothing
            al[where] = nothing
        for g in range(8):
            at = slice(16 * g, 16 * g + 16)
            data = jnp.concatenate(
                [
                    in_ref[:, 128 * i + 16 * g : 128 * i + 16 * g + 16, :].reshape(256, LANES)
                    for i in range(3)
                ],
                axis=1,
            )
            first = dot(fh_ref[...], data) + dot(fl_ref[...], data)
            high, low = halves(first)
            for ref, value in ((ah, high), (al, low)):
                ref[0, at, :] = value[0:16]
                ref[2, at, :] = value[16:32]
                ref[4:34, at, :] = value[32:512].reshape(30, 16, wide)

    pair = pl.ds(2 * step, 2)
    high = ah[pair].reshape(2 * LANES, wide)
    low = al[pair].reshape(2 * LANES, wide)
    spec = dot(dh_ref[0], high) + (dot(dh_ref[0], low) + dot(dl_ref[0], high))
    xr, xi = spec[:LANES, :LANES], spec[LANES:, :LANES]
    gr, gi = spec[:LANES, LANES : 2 * LANES], spec[LANES:, LANES : 2 * LANES]
    hr, hi = spec[:LANES, 2 * LANES :], spec[LANES:, 2 * LANES :]
    real = jnp.concatenate([hr * xr - hi * xi, hr * gr + hi * gi, xr * gr + xi * gi], axis=1)
    imag = jnp.concatenate([hr * xi + hi * xr, hr * gi - hi * gr, xr * gi - xi * gr], axis=1)
    back = dot_three(eh_ref[0], el_ref[0], jnp.concatenate([real, imag], axis=0))
    high, low = halves(back)
    zh[pair] = high.reshape(2, LANES, wide)
    zl[pair] = low.reshape(2, LANES, wide)

    @pl.when(step == 16)
    def _():
        for g in range(8):
            at = slice(16 * g, 16 * g + 16)

            def picked(ref):
                return jnp.concatenate(
                    [ref[0, at, :], ref[2, at, :], ref[4:34, at, :].reshape(480, wide)], axis=0
                )

            high = picked(zh)
            low = picked(zl)
            last = dot(bh_ref[...], high) + (dot(bh_ref[...], low) + dot(bl_ref[...], high))
            for i in range(3):
                part = last[:, i * LANES : (i + 1) * LANES].reshape(16, 16, LANES)
                out_ref[:, 128 * i + 16 * g : 128 * i + 16 * g + 16, :] = part.astype(BF16)
                if g == 0 and i < 2:
                    lead = part[1:, 0:8, :]
                    lead = jnp.concatenate([lead, jnp.zeros((1, 8, LANES), F32)], axis=0)
                    if i == 0:
                        conv_lead = lead
                    else:
                        both = jnp.concatenate([conv_lead, lead], axis=1)
                        out_ref[:, 384:400, :] = both.astype(BF16)


def conv_all(columns, tables):
    fwd, back = outer_tables()
    fh, fl = (spread(t, 16) for t in numpy_halves(fwd))
    bh, bl = (spread(t, 16) for t in numpy_halves(back))
    table = pl.BlockSpec((1, 2 * LANES, 2 * LANES), lambda k: (k, 0, 0))

    def whole(*shape):
        return pl.BlockSpec(shape, lambda k: (0,) * len(shape))

    return pl.pallas_call(
        conv_kernel,
        grid=(17,),
        in_specs=[whole(16, 384, LANES)]
        + [table] * 4
        + [whole(512, 256), whole(512, 256), whole(256, 512), whole(256, 512)],
        out_specs=whole(16, 400, LANES),
        out_shape=jax.ShapeDtypeStruct((16, 400, LANES), BF16),
        scratch_shapes=[pltpu.VMEM((34, LANES, 3 * LANES), BF16) for _ in range(4)],
        name="conv_all",
    )(columns, *tables, fh, fl, bh, bl)


def back_kernel(
    k_ref, v_ref, q_ref, take_ref, give_ref, pk_ref, pv_ref, pq_ref, nk_ref, nv_ref, nq_ref,
    mask_ref, w_ref, cot_ref, next_cot_ref, conv_ref, mixed_ref, back_ref, taps_ref, xs, one, two,
):
    take = take_ref[...]
    give = give_ref[...]
    m1 = mask_ref[:, 0:1]
    m2 = mask_ref[:, 1:2]
    streams = ((k_ref, pk_ref, nk_ref), (v_ref, pv_ref, nv_ref), (q_ref, pq_ref, nq_ref))
    for s, (ref, prev, after) in enumerate(streams):
        xs[s, 6:8, :] = prev[...].astype(F32)
        xs[s, 8:136, :] = dot(take, ref[...])
        xs[s, 136:144, :] = jnp.zeros((8, CHUNK), F32)
        xs[s, 136:138, :] = after[...].astype(F32)
    for h in range(CHUNK // LANES):
        at = slice(h * LANES, (h + 1) * LANES)
        hats = []
        for s in range(3):
            w = w_ref[:, s, at]
            hats.append(
                w[0:1] * xs[s, 8:144, at]
                + w[1:2] * (xs[s, 7:143, at] * m1)
                + w[2:3] * (xs[s, 6:142, at] * m2)
            )
        tail = conv_ref[h, 384:400, :].astype(F32)
        conv = jnp.concatenate([conv_ref[h, 0:128, :].astype(F32), tail[0:8]], axis=0)
        grad_product = jnp.concatenate([conv_ref[h, 128:256, :].astype(F32), tail[8:16]], axis=0)
        cot = jnp.concatenate([cot_ref[:, at].astype(F32), next_cot_ref[:, at].astype(F32)], axis=0)
        mixed_ref[:, at] = (hats[2] * conv)[0:128].astype(BF16)
        grads = (grad_product * hats[1], grad_product * hats[0], cot * conv)
        for s in range(3):
            w = w_ref[:, s, at]
            grad = grads[s]
            here = grad[0:128]
            one[...] = grad * m1
            two[...] = grad * m2
            taps_ref[3 * s : 3 * s + 1, at] = jnp.sum(here * xs[s, 8:136, at], axis=0, keepdims=True)
            taps_ref[3 * s + 1 : 3 * s + 2, at] = jnp.sum(one[0:128] * xs[s, 7:135, at], axis=0, keepdims=True)
            taps_ref[3 * s + 2 : 3 * s + 3, at] = jnp.sum(two[0:128] * xs[s, 6:134, at], axis=0, keepdims=True)
            rows = w[0:1] * here + w[1:2] * one[1:129] + w[2:3] * two[2:130]
            sent = dot(give, rows.astype(BF16)).astype(BF16)
            back_ref[:, 16 * s : 16 * s + 16, at] = sent.reshape(16, 16, LANES)
        lags = conv_ref[h, 256:384, :].astype(F32).reshape(16, 8, LANES)
        back_ref[:, 48:56, at] = lags.astype(BF16)


def back_rows(received, take, give, prev, after, masks, weights, cot, next_cot, columns):
    channels = cot.shape[1]
    chunks = channels // CHUNK
    per = CHUNK // LANES
    return pl.pallas_call(
        back_kernel,
        grid=(chunks,),
        in_specs=stream_specs(256, chunks)
        + [pl.BlockSpec((128, 256), lambda c: (0, 0)), pl.BlockSpec((256, 128), lambda c: (0, 0))]
        + stream_specs(2, chunks)
        + stream_specs(2, chunks)
        + [
            pl.BlockSpec((136, 2), lambda c: (0, 0)),
            pl.BlockSpec((3, 3, CHUNK), lambda c: (0, 0, c)),
            pl.BlockSpec((128, CHUNK), lambda c: (0, c)),
            pl.BlockSpec((8, CHUNK), lambda c: (0, c)),
            pl.BlockSpec((per, 400, LANES), lambda c: (c, 0, 0)),
        ],
        out_specs=[
            pl.BlockSpec((128, CHUNK), lambda c: (0, c)),
            pl.BlockSpec((16, 56, CHUNK), lambda c: (0, 0, c)),
            pl.BlockSpec((9, CHUNK), lambda c: (0, c)),
        ],
        out_shape=[
            jax.ShapeDtypeStruct((128, channels), BF16),
            jax.ShapeDtypeStruct((16, 56, channels), BF16),
            jax.ShapeDtypeStruct((9, channels), F32),
        ],
        scratch_shapes=[
            pltpu.VMEM((3, 144, CHUNK), F32),
            pltpu.VMEM((136, LANES), F32),
            pltpu.VMEM((136, LANES), F32),
        ],
        name="back_rows",
    )(
        received, received, received, take, give, prev, prev, prev, after, after, after,
        masks, weights, cot, next_cot, columns,
    )


def store_kernel(select_ref, in_ref, out_ref):
    width = in_ref.shape[2]
    out_ref[...] = dot(select_ref[...], in_ref[...].reshape(256, width)).astype(BF16)


def store_grads(select, returned, channels):
    width = 512
    chunks = channels // width
    return pl.pallas_call(
        store_kernel,
        grid=(3, chunks),
        in_specs=[
            pl.BlockSpec((128, 256), lambda s, c: (0, 0)),
            pl.BlockSpec((16, 16, width), lambda s, c: (0, s, c)),
        ],
        out_specs=pl.BlockSpec((128, width), lambda s, c: (0, s * chunks + c)),
        out_shape=jax.ShapeDtypeStruct((128, 3 * channels), BF16),
        name="store_grads",
    )(select, returned)


def total_over(value, axis):
    length = lax.axis_size(axis)
    step = 1
    while step < length:
        value = value + lax.ppermute(value, axis, [(i, i ^ step) for i in range(length)])
        step *= 2
    return value


def shards(stored, source_row, source_span, segments, short_weight, filter_taps, cotangent):
    dp_count = lax.axis_size("dp")
    my_dp = lax.axis_index("dp")
    tok_rows = stored.shape[1]
    width = stored.shape[2]
    channels = width // 3
    span_count = source_span.shape[1]
    span_rows = tok_rows // span_count
    slot_ids = jnp.arange(MOST, dtype=jnp.int32)
    span_ids = jnp.arange(span_count, dtype=jnp.int32)
    sources = source_row[:, :, 0]
    mine = (sources == my_dp).astype(jnp.int32)
    earlier = jnp.cumsum(mine, axis=1) - mine
    picked = mine[:, None, :] * (earlier[:, None, :] == slot_ids[None, :, None]).astype(jnp.int32)
    span_hot = (source_span[:, :, None] == span_ids[None, None, :]).astype(F32)
    select = jnp.einsum("dmj,djk->dmk", picked.astype(F32), span_hot).reshape(dp_count * MOST, span_count)
    my_sources = lax.dynamic_index_in_dim(sources, my_dp, 0, keepdims=False)
    same_source = my_sources[:, None] == my_sources[None, :]
    lower_slot = span_ids[:, None] > span_ids[None, :]
    my_order = jnp.sum((same_source & lower_slot).astype(jnp.int32), axis=1)
    place = my_sources * MOST + my_order
    take = (place[:, None] == jnp.arange(dp_count * MOST, dtype=jnp.int32)[None, :]).astype(F32)

    send_rows = spread(select, span_rows)
    select_rows = spread(jnp.transpose(select), span_rows)
    take_rows = spread(take, span_rows)
    give_rows = spread(jnp.transpose(take), span_rows)

    sent = dot(send_rows, stored[0]).astype(BF16)
    received = exchange(sent.reshape(dp_count, MOST * span_rows, width), "dp")
    received = received.reshape(dp_count * MOST * span_rows, width)

    ids = segments[0] + 1
    before_ids = shifted(ids[-2:], "seq", 1)
    after_ids = shifted(ids[:2], "seq", -1)
    all_ids = jnp.concatenate([before_ids, ids, after_ids])
    masks = jnp.stack(
        [all_ids[1 : tok_rows + 3] == all_ids[2 : tok_rows + 4], all_ids[: tok_rows + 2] == all_ids[2 : tok_rows + 4]],
        axis=1,
    ).astype(F32)
    masks = jnp.pad(masks, ((0, 6), (0, 0)))
    cot = cotangent[0]
    next_cot = jnp.pad(shifted(cot[:2], "seq", -1), ((0, 6), (0, 0)))
    weights = jnp.transpose(short_weight, (1, 0, 2))
    tables = inner_tables()

    last = lax.dynamic_slice(received, (place[-1] * span_rows, 0), (span_rows, width))[-2:]
    first = lax.dynamic_slice(received, (place[0] * span_rows, 0), (span_rows, width))[:2]
    prev = shifted(last, "seq", 1)
    after = shifted(first, "seq", -1)

    outgoing = gather_rows(received, take_rows, prev, masks, weights, cot, filter_taps)
    columns = exchange(outgoing, "seq")
    results = conv_all(columns, tables)
    local = exchange(results, "seq")
    mixed, back, taps = back_rows(
        received, take_rows, give_rows, prev, after, masks, weights, cot, next_cot, local
    )
    returned = exchange(back, "dp")
    taps = total_over(taps, "seq")
    grad_stored = store_grads(select_rows, returned, channels)
    lags = jnp.sum(returned[:, 48:56].astype(F32), axis=0)
    final = jnp.concatenate([lags, taps], axis=0).astype(BF16)
    final = exchange(jnp.broadcast_to(final[None], (dp_count, *final.shape)), "dp").astype(F32)
    grad_filter = final[:, :8].reshape(tok_rows, channels)
    grad_short = jnp.sum(final[:, 8:], axis=0).reshape(3, 3, channels)
    return (mixed[None], grad_stored[None], grad_filter, grad_short)


def solution(mesh):
    return jax.shard_map(
        shards,
        mesh=mesh,
        in_specs=(
            P("dp", "seq", None),
            P(None, "seq", None),
            P(None, "seq"),
            P("dp", "seq"),
            P(),
            P("seq", None),
            P("dp", "seq", None),
        ),
        out_specs=(P("dp", "seq", None), P("dp", "seq", None), P("seq", None), P()),
        check_vma=False,
    )
```

```python
import functools
import math

import jax
import jax.numpy as jnp
import numpy as np
from jax import lax
from jax.experimental import pallas as pl
from jax.experimental.pallas import tpu as pltpu
from jax.sharding import PartitionSpec as P

MOST = 2
CHUNK = 512
LANES = 128
HALO = 8
F32 = jnp.float32
BF16 = jnp.bfloat16


def shifted(value, axis, by):
    length = lax.axis_size(axis)
    pairs = [(i, i + by) for i in range(length) if 0 <= i + by < length]
    return lax.ppermute(value, axis, pairs)


def exchange(value, axis):
    return lax.all_to_all(value, axis, 0, 0, tiled=True)


def dot(left, right):
    return jnp.dot(left, right, preferred_element_type=F32)


def dot_t(left, right):
    return lax.dot_general(left, right, (((0,), (0,)), ((), ())), preferred_element_type=F32)


def iota(shape, axis):
    return lax.broadcasted_iota(jnp.int32, shape, axis)


def whole(*shape):
    return pl.BlockSpec(shape, lambda *ids: (0,) * len(shape))


SMEM = pl.BlockSpec(memory_space=pltpu.SMEM)


def outer_tables():
    blocks = np.arange(16)
    forward = [np.ones(16), np.cos(np.pi * blocks)]
    back = [np.ones(16), np.cos(np.pi * blocks)]
    for k in range(1, 16):
        angle = 2.0 * np.pi * k * blocks / 32.0
        forward += [np.cos(angle), -np.sin(angle)]
        back += [2.0 * np.cos(angle), -2.0 * np.sin(angle)]
    return np.stack(forward), np.stack(back, axis=1) / 4096.0


def numpy_halves(table):
    high = np.asarray(table, np.float32).astype(jnp.bfloat16)
    low = (table - high.astype(np.float64)).astype(np.float32).astype(jnp.bfloat16)
    return jnp.asarray(high), jnp.asarray(low)


def spread_in(table, by):
    rows, cols = table.shape
    tall = (iota((rows * by, rows), 0) // by == iota((rows * by, rows), 1)).astype(BF16)
    wide = (iota((cols, cols * by), 0) == iota((cols, cols * by), 1) // by).astype(BF16)
    value = dot(dot(tall, table).astype(BF16), wide)
    shape = (rows * by, cols * by)
    diagonal = iota(shape, 0) % by == iota(shape, 1) % by
    return jnp.where(diagonal, value, 0.0).astype(BF16)


def dft_constants():
    inner = np.arange(LANES)
    turn = 2.0 * np.pi * (inner[:, None] * inner[None, :] % LANES) / LANES
    order = np.asarray([0, 16] + list(range(1, 16)))
    twist = 2.0 * np.pi * order[:, None] * inner[None, :] / 4096.0
    values = (
        np.cos(turn),
        np.sin(turn),
        np.stack([np.cos(twist), np.sin(twist)], axis=1),
        np.stack([np.cos(twist), np.sin(twist)], axis=2),
    )
    return tuple(jnp.asarray(value, F32) for value in values)


def turned(fc_ref, fs_ref, wc, ws):
    fc = fc_ref[...]
    fs = fs_ref[...]
    return fc * wc - fs * ws, fs * wc + fc * ws


def forward_table(fc_ref, fs_ref, row_ref, k):
    row = row_ref[k]
    cos, sin = turned(fc_ref, fs_ref, row[0:1, :], row[1:2, :])
    cos, sin, minus = cos.astype(BF16), sin.astype(BF16), (-sin).astype(BF16)
    return jnp.concatenate(
        [jnp.concatenate([cos, sin], axis=1), jnp.concatenate([minus, cos], axis=1)], axis=0
    )


def back_table(fc_ref, fs_ref, col_ref, k):
    col = col_ref[k]
    cos, sin = turned(fc_ref, fs_ref, col[:, 0:1], col[:, 1:2])
    cos, sin, minus = cos.astype(BF16), sin.astype(BF16), (-sin).astype(BF16)
    return jnp.concatenate(
        [jnp.concatenate([cos, minus], axis=1), jnp.concatenate([sin, cos], axis=1)], axis=0
    )


def pack_kernel(me_ref, source_ref, span_ref, stored_ref, out_ref, select_ref):
    @pl.when(pl.program_id(0) == 0)
    def _():
        mine = (source_ref[...] == me_ref[0]).astype(F32)
        before = (iota((16, 16), 0) < iota((16, 16), 1)).astype(F32)
        earlier = dot(mine, before)
        tall = (iota((256, 16), 0) // 16 == iota((256, 16), 1)).astype(F32)
        row = iota((256, 16), 0)
        hit = dot(tall, mine) * (dot(tall, earlier) == (row // 8 % 2).astype(F32)).astype(F32)
        start = jnp.sum(hit * (dot(tall, span_ref[...].astype(F32)) * 8.0 + 1.0), axis=1, keepdims=True)
        target = jnp.where(start > 0.5, start - 1.0 + (iota((256, 1), 0) % 8).astype(F32), -1.0)
        select_ref[...] = (iota((256, 128), 1).astype(F32) == target).astype(F32).astype(BF16)

    out_ref[...] = dot(select_ref[...], stored_ref[...]).astype(BF16)


def pack_rows(me, sources, spans, stored):
    width = 1024
    return pl.pallas_call(
        pack_kernel,
        grid=(stored.shape[1] // width,),
        in_specs=[
            SMEM,
            whole(16, 16),
            whole(16, 16),
            pl.BlockSpec((128, width), lambda c: (0, c)),
        ],
        out_specs=[pl.BlockSpec((256, width), lambda c: (0, c)), whole(256, 128)],
        out_shape=[
            jax.ShapeDtypeStruct((256, stored.shape[1]), BF16),
            jax.ShapeDtypeStruct((256, 128), BF16),
        ],
        name="pack_rows",
    )(me, sources, spans, stored)


def filter_blocks_kernel(me_ref, taps_ref, *out_refs):
    for r, out_ref in enumerate(out_refs):
        at = pl.multiple_of((me_ref[0] ^ r) * LANES, LANES)
        out_ref[...] = taps_ref[:, pl.ds(at, LANES)].astype(BF16)


def filter_blocks(me, filter_taps):
    return pl.pallas_call(
        filter_blocks_kernel,
        in_specs=[SMEM, pl.BlockSpec(memory_space=pltpu.VMEM)],
        out_specs=[pl.BlockSpec(memory_space=pltpu.VMEM)] * 16,
        out_shape=[jax.ShapeDtypeStruct((128, LANES), BF16)] * 16,
        name="filter_blocks",
    )(me, filter_taps)


def gather_kernel(k_ref, v_ref, q_ref, take_ref, pk_ref, pv_ref, pq_ref, mask_ref, w_ref, cot_ref, out_ref, xs):
    take = take_ref[...]
    m1 = mask_ref[0:128, 0:1]
    m2 = mask_ref[0:128, 1:2]
    hats = []
    for s, (ref, prev) in enumerate(((k_ref, pk_ref), (v_ref, pv_ref), (q_ref, pq_ref))):
        x = dot(take, ref[...])
        xs[s, 6:8, :] = prev[...].astype(F32)
        xs[s, 8:136, :] = x
        w = w_ref[:, s, :]
        lag_one = xs[s, 7:135, :] * m1
        lag_two = xs[s, 6:134, :] * m2
        hats.append(w[0:1] * x + w[1:2] * lag_one + w[2:3] * lag_two)
    product = (hats[0] * hats[1]).astype(BF16)
    grad_conv = (cot_ref[...].astype(F32) * hats[2]).astype(BF16)
    for h in range(CHUNK // LANES):
        at = slice(h * LANES, (h + 1) * LANES)
        out_ref[h, 0:128, :] = product[:, at]
        out_ref[h, 128:256, :] = grad_conv[:, at]


def stream_specs(rows, chunks):
    return [pl.BlockSpec((rows, CHUNK), lambda c, s=s: (0, s * chunks + c)) for s in range(3)]


def column_spec(rows):
    return pl.BlockSpec((rows, CHUNK), lambda c: (0, c))


WEIGHTS = pl.BlockSpec((3, 3, CHUNK), lambda c: (0, 0, c))


def gather_rows(received, take, prev, masks, weights, cot):
    chunks = cot.shape[1] // CHUNK
    per = CHUNK // LANES
    return pl.pallas_call(
        gather_kernel,
        grid=(chunks,),
        in_specs=stream_specs(256, chunks)
        + [whole(128, 256)]
        + stream_specs(2, chunks)
        + [whole(136, 2), WEIGHTS, column_spec(128)],
        out_specs=pl.BlockSpec((per, 256, LANES), lambda c: (c, 0, 0)),
        out_shape=jax.ShapeDtypeStruct((chunks * per, 256, LANES), BF16),
        scratch_shapes=[pltpu.VMEM((3, 136, CHUNK), F32)],
        name="gather_rows",
    )(received, received, received, take, prev, prev, prev, masks, weights, cot)


def outer_forward(fh_ref, fl_ref, pick, spec):
    nothing = jnp.zeros(spec.shape[1:], BF16)
    for where in (1, 3):
        spec[where] = nothing
    for g in range(8):
        at = slice(16 * g, 16 * g + 16)
        data = pick(g)
        value = (dot(fh_ref[...], data) + dot(fl_ref[...], data)).astype(BF16)
        spec[0, at, :] = value[0:16]
        spec[2, at, :] = value[16:32]
        spec[4:34, at, :] = value[32:512].reshape(30, 16, value.shape[1])


def outer_back(bh_ref, turns, g):
    at = slice(16 * g, 16 * g + 16)
    rest = turns[4:34, at, :].reshape(480, turns.shape[2])
    return dot(bh_ref[...], jnp.concatenate([turns[0, at, :], turns[2, at, :], rest], axis=0))


def pair_of(ref, k):
    return ref[pl.ds(2 * k, 2)].reshape(2 * LANES, ref.shape[2])


def put_pair(ref, k, value):
    ref[pl.ds(2 * k, 2)] = value.astype(BF16).reshape(2, LANES, ref.shape[2])


VMEM_SPEC = pl.BlockSpec(memory_space=pltpu.VMEM)


def filter_kernel(me_ref, fc_ref, fs_ref, row_ref, ofh_ref, ofl_ref, obh_ref, *rest):
    blocks, (out_ref, fh_ref, fl_ref, bh_ref, ordered, spec) = rest[:16], rest[16:]
    fh_ref[...] = spread_in(ofh_ref[...], 16)
    fl_ref[...] = spread_in(ofl_ref[...], 16)
    bh_ref[...] = spread_in(obh_ref[...], 16)
    for r, block in enumerate(blocks):
        ordered[me_ref[0] ^ r] = block[...]
    outer_forward(
        fh_ref, fl_ref, lambda g: ordered[:, 16 * g : 16 * g + 16, :].reshape(256, LANES), spec
    )

    def step(k, carry):
        out_ref[k] = dot(forward_table(fc_ref, fs_ref, row_ref, k), pair_of(spec, k)).astype(BF16)
        return carry

    lax.fori_loop(0, 17, step, 0)


def filter_spectrum(me, constants, blocks):
    fc, fs, row, _ = constants
    forward, back = outer_tables()
    tall = jax.ShapeDtypeStruct((512, 256), BF16)
    return pl.pallas_call(
        filter_kernel,
        in_specs=[SMEM] + [VMEM_SPEC] * 22,
        out_specs=[VMEM_SPEC] * 4,
        out_shape=[
            jax.ShapeDtypeStruct((17, 2 * LANES, LANES), BF16),
            tall,
            tall,
            jax.ShapeDtypeStruct((256, 512), BF16),
        ],
        scratch_shapes=[pltpu.VMEM((16, 128, LANES), BF16), pltpu.VMEM((34, LANES, LANES), BF16)],
        name="filter_spectrum",
    )(me, fc, fs, row, *numpy_halves(forward), numpy_halves(back)[0], *blocks)


def conv_kernel(
    in_ref, h_ref, fc_ref, fs_ref, row_ref, col_ref, fh_ref, fl_ref, bh_ref, out_ref, cross_ref, spec, turns,
):
    def pick(g):
        parts = [in_ref[:, 128 * i + 16 * g : 128 * i + 16 * g + 16, :] for i in range(2)]
        return jnp.concatenate([part.reshape(256, LANES) for part in parts], axis=1)

    outer_forward(fh_ref, fl_ref, pick, spec)

    def step(k, carry):
        value = dot(forward_table(fc_ref, fs_ref, row_ref, k), pair_of(spec, k))
        xr, xi = value[:LANES, :LANES], value[LANES:, :LANES]
        gr, gi = value[:LANES, LANES:], value[LANES:, LANES:]
        h = h_ref[k].astype(F32)
        hr, hi = h[:LANES], h[LANES:]
        cross = jnp.concatenate([xr * gr + xi * gi, xr * gi - xi * gr], axis=0)
        cross_ref[k] = cross.astype(BF16)
        real = jnp.concatenate([hr * xr - hi * xi, hr * gr + hi * gi], axis=1)
        imag = jnp.concatenate([hr * xi + hi * xr, hr * gi - hi * gr], axis=1)
        mixed = jnp.concatenate([real, imag], axis=0).astype(BF16)
        put_pair(turns, k, dot(back_table(fc_ref, fs_ref, col_ref, k), mixed))
        return carry

    lax.fori_loop(0, 17, step, 0)
    for g in range(8):
        last = outer_back(bh_ref, turns, g)
        parts = [last[:, i * LANES : (i + 1) * LANES].reshape(16, 16, LANES) for i in range(2)]
        for i in range(2):
            out_ref[:, 128 * i + 16 * g : 128 * i + 16 * g + 16, :] = parts[i].astype(BF16)
        if g == 0:
            leads = jnp.concatenate([part[1:, 0:8, :] for part in parts], axis=1)
            leads = jnp.concatenate([leads, jnp.zeros((1, 16, LANES), F32)], axis=0)
            out_ref[:, 256:272, :] = leads.astype(BF16)


def conv_both(columns, spectrum, constants):
    h, fh, fl, bh = spectrum
    return pl.pallas_call(
        conv_kernel,
        in_specs=[VMEM_SPEC] * 9,
        out_specs=[VMEM_SPEC] * 2,
        out_shape=[
            jax.ShapeDtypeStruct((16, 272, LANES), BF16),
            jax.ShapeDtypeStruct((17, 2 * LANES, LANES), BF16),
        ],
        scratch_shapes=[pltpu.VMEM((34, LANES, 2 * LANES), BF16) for _ in range(2)],
        name="conv_both",
    )(columns, h, *constants, fh, fl, bh)


def reversed_bits(j):
    return ((j & 1) << 3) | ((j & 2) << 1) | ((j & 4) >> 1) | ((j & 8) >> 3)


def filter_grad_kernel(ids_ref, cross_ref, fc_ref, fs_ref, col_ref, bh_ref, out_ref, turns):
    def step(k, carry):
        put_pair(turns, k, dot(back_table(fc_ref, fs_ref, col_ref, k), cross_ref[k]))
        return carry

    lax.fori_loop(0, 17, step, 0)
    for g in range(8):
        part = outer_back(bh_ref, turns, g).reshape(16, 16, LANES)
        for e in range(2):
            place = reversed_bits((2 * g + e) ^ ids_ref[0])
            for p in range(16):
                out_ref[place, p ^ ids_ref[1]] = part[p, 8 * e : 8 * e + 8].astype(BF16)


def filter_grad(ids, cross, constants, back):
    fc, fs, _, col = constants
    return pl.pallas_call(
        filter_grad_kernel,
        in_specs=[SMEM] + [VMEM_SPEC] * 5,
        out_specs=VMEM_SPEC,
        out_shape=jax.ShapeDtypeStruct((16, 16, 8, LANES), BF16),
        scratch_shapes=[pltpu.VMEM((34, LANES, LANES), BF16)],
        name="filter_grad",
    )(ids, cross, fc, fs, col, back)


def extended(take, streams, xs):
    for s, (ref, prev, after) in enumerate(streams):
        xs[s, 6:8, :] = prev[...].astype(F32)
        xs[s, 8:136, :] = dot(take, ref[...])
        xs[s, 136:144, :] = jnp.zeros((8, xs.shape[2]), F32)
        xs[s, 136:138, :] = after[...].astype(F32)


def hats_kernel(
    k_ref, v_ref, take_ref, pk_ref, pv_ref, nk_ref, nv_ref, mask_ref, w_ref, key_ref, value_ref, xs,
):
    m1 = mask_ref[:, 0:1]
    m2 = mask_ref[:, 1:2]
    extended(take_ref[...], ((k_ref, pk_ref, nk_ref), (v_ref, pv_ref, nv_ref)), xs)
    for s, out_ref in enumerate((key_ref, value_ref)):
        w = w_ref[:, s, :]
        out_ref[...] = (
            w[0:1] * xs[s, 8:144, :] + w[1:2] * (xs[s, 7:143, :] * m1) + w[2:3] * (xs[s, 6:142, :] * m2)
        )


def make_hats(received, take, prev, after, masks, weights):
    channels = weights.shape[2]
    chunks = channels // CHUNK
    return pl.pallas_call(
        hats_kernel,
        grid=(chunks,),
        in_specs=stream_specs(256, chunks)[:2]
        + [whole(128, 256)]
        + stream_specs(2, chunks)[:2]
        + stream_specs(2, chunks)[:2]
        + [whole(136, 2), WEIGHTS],
        out_specs=[column_spec(136)] * 2,
        out_shape=[jax.ShapeDtypeStruct((136, channels), F32)] * 2,
        scratch_shapes=[pltpu.VMEM((2, 144, CHUNK), F32)],
        name="make_hats",
    )(received, received, take, prev, prev, after, after, masks, weights)


def spread_rows(conv_ref, h):
    tail = conv_ref[h, 256:272, :].astype(F32)
    conv = jnp.concatenate([conv_ref[h, 0:128, :].astype(F32), tail[0:8]], axis=0)
    grad_product = jnp.concatenate([conv_ref[h, 128:256, :].astype(F32), tail[8:16]], axis=0)
    return conv, grad_product


def back_kernel(
    key_ref, value_ref, give_ref, mask_ref, w_ref, cot_ref, next_cot_ref, conv_ref, back_ref, one, two,
):
    give = give_ref[...]
    m1 = mask_ref[:, 0:1]
    m2 = mask_ref[:, 1:2]
    for h in range(CHUNK // LANES):
        at = slice(h * LANES, (h + 1) * LANES)
        conv, grad_product = spread_rows(conv_ref, h)
        cot = jnp.concatenate([cot_ref[:, at].astype(F32), next_cot_ref[:, at].astype(F32)], axis=0)
        grads = (grad_product * value_ref[:, at], grad_product * key_ref[:, at], cot * conv)
        for s in range(3):
            w = w_ref[:, s, at]
            grad = grads[s]
            one[s] = grad * m1
            two[s] = grad * m2
            rows = w[0:1] * grad[0:128] + w[1:2] * one[s, 1:129] + w[2:3] * two[s, 2:130]
            sent = dot(give, rows.astype(BF16)).astype(BF16)
            back_ref[:, 16 * s : 16 * s + 16, at] = sent.reshape(16, 16, LANES)


def back_rows(hats, give, masks, weights, cot, next_cot, local):
    channels = cot.shape[1]
    chunks = channels // CHUNK
    per = CHUNK // LANES
    return pl.pallas_call(
        back_kernel,
        grid=(chunks,),
        in_specs=[
            column_spec(136),
            column_spec(136),
            whole(256, 128),
            whole(136, 2),
            WEIGHTS,
            column_spec(128),
            column_spec(8),
            pl.BlockSpec((per, 272, LANES), lambda c: (c, 0, 0)),
        ],
        out_specs=pl.BlockSpec((16, 48, CHUNK), lambda c: (0, 0, c)),
        out_shape=jax.ShapeDtypeStruct((16, 48, channels), BF16),
        scratch_shapes=[pltpu.VMEM((3, 136, LANES), F32) for _ in range(2)],
        name="back_rows",
    )(*hats, give, masks, weights, cot, next_cot, local)


def sums_kernel(
    k_ref, v_ref, q_ref, take_ref, pk_ref, pv_ref, pq_ref, key_ref, value_ref, mask_ref, w_ref, cot_ref, conv_ref,
    mixed_ref, taps_ref, xs,
):
    take = take_ref[...]
    m1 = mask_ref[0:128, 0:1]
    m2 = mask_ref[0:128, 1:2]
    for s, (ref, prev) in enumerate(((k_ref, pk_ref), (v_ref, pv_ref), (q_ref, pq_ref))):
        xs[s, 6:8, :] = prev[...].astype(F32)
        xs[s, 8:136, :] = dot(take, ref[...])
    for h in range(CHUNK // LANES):
        at = slice(h * LANES, (h + 1) * LANES)
        conv = conv_ref[h, 0:128, :].astype(F32)
        grad_product = conv_ref[h, 128:256, :].astype(F32)
        cot = cot_ref[:, at].astype(F32)
        grads = (grad_product * value_ref[0:128, at], grad_product * key_ref[0:128, at], cot * conv)
        for s in range(3):
            parts = (xs[s, 8:136, at], xs[s, 7:135, at] * m1, xs[s, 6:134, at] * m2)
            for k in range(3):
                total = jnp.sum(grads[s] * parts[k], axis=0, keepdims=True)
                taps_ref[3 * s + k, pl.ds((CHUNK // LANES) * pl.program_id(0) + h, 1), :] = total
            if s == 2:
                w = w_ref[:, s, at]
                query = w[0:1] * parts[0] + w[1:2] * parts[1] + w[2:3] * parts[2]
                mixed_ref[:, at] = (query * conv).astype(BF16)


def mixed_and_sums(received, take, prev, hats, masks, weights, cot, local):
    channels = cot.shape[1]
    chunks = channels // CHUNK
    per = CHUNK // LANES
    return pl.pallas_call(
        sums_kernel,
        grid=(chunks,),
        in_specs=stream_specs(256, chunks)
        + [whole(128, 256)]
        + stream_specs(2, chunks)
        + [
            column_spec(136),
            column_spec(136),
            whole(136, 2),
            WEIGHTS,
            column_spec(128),
            pl.BlockSpec((per, 272, LANES), lambda c: (c, 0, 0)),
        ],
        out_specs=[column_spec(128), whole(9, 16, LANES)],
        out_shape=[
            jax.ShapeDtypeStruct((128, channels), BF16),
            jax.ShapeDtypeStruct((9, 16, LANES), F32),
        ],
        scratch_shapes=[pltpu.VMEM((3, 136, CHUNK), F32)],
        name="mixed_and_sums",
    )(received, received, received, take, prev, prev, prev, *hats, masks, weights, cot, local)


def store_kernel(select_ref, in_ref, out_ref):
    width = in_ref.shape[2]
    out_ref[...] = dot_t(select_ref[...], in_ref[...].reshape(256, width)).astype(BF16)


def store_grads(select, returned, channels):
    width = 1024
    chunks = channels // width
    return pl.pallas_call(
        store_kernel,
        grid=(3, chunks),
        in_specs=[
            whole(256, 128),
            pl.BlockSpec((16, 16, width), lambda s, c: (0, s, c)),
        ],
        out_specs=pl.BlockSpec((128, width), lambda s, c: (0, s * chunks + c)),
        out_shape=jax.ShapeDtypeStruct((128, 3 * channels), BF16),
        name="store_grads",
    )(select, returned)


def final_kernel(me_ref, in_ref, grad_ref, taps_ref):
    for j in range(16):
        at = pl.multiple_of((j ^ me_ref[0]) * LANES, LANES)
        grad_ref[:, pl.ds(at, LANES)] = in_ref[:, 8 * j : 8 * j + 8, :].astype(F32).reshape(128, LANES)
    taps_ref[...] = jnp.sum(in_ref[:, 128:272, :].astype(F32), axis=0)


def final_parts(me, final):
    return pl.pallas_call(
        final_kernel,
        in_specs=[SMEM, pl.BlockSpec(memory_space=pltpu.VMEM)],
        out_specs=[pl.BlockSpec(memory_space=pltpu.VMEM)] * 2,
        out_shape=[jax.ShapeDtypeStruct((128, 2048), F32), jax.ShapeDtypeStruct((144, LANES), F32)],
        name="final_parts",
    )(me, final)


def across(value, axis, bit):
    return lax.ppermute(value, axis, [(i, i ^ bit) for i in range(lax.axis_size(axis))])


def halving_sum(value):
    total = value.astype(F32)
    for bit in (1, 2, 4, 8):
        half = total.shape[0] // 2
        total = total[:half] + across(total[half:].astype(BF16), "dp", bit).astype(F32)
    return total[0]


def cube_exchange(value, axis):
    shape = value.shape
    for bit in (1, 2, 4, 8):
        grouped = value.reshape(shape[0] // (2 * bit), 2, bit, *shape[1:])
        other = across(grouped[:, 1], axis, bit)
        value = jnp.stack([grouped[:, 0], other], axis=1).reshape(shape)
    return value


def total_over(value, axis):
    for bit in (1, 2, 4, 8):
        value = value + across(value, axis, bit)
    return value


def shards(stored, source_row, source_span, segments, short_weight, filter_taps, cotangent):
    dp_count = lax.axis_size("dp")
    seq_count = lax.axis_size("seq")
    my_dp = lax.axis_index("dp").astype(jnp.int32)
    my_seq = lax.axis_index("seq").astype(jnp.int32)
    tok_rows = stored.shape[1]
    width = stored.shape[2]
    channels = width // 3
    span_count = source_span.shape[1]
    span_rows = tok_rows // span_count
    sources = source_row[:, :, 0]
    dp_id, seq_id = my_dp[None], my_seq[None]

    sent, select = pack_rows(dp_id, sources, source_span, stored[0])
    received = exchange(sent.reshape(dp_count, MOST * span_rows, width), "dp")
    received = received.reshape(dp_count * MOST * span_rows, width)

    blocks = filter_blocks(seq_id, filter_taps)
    blocks = [blocks[0]] + [
        across(blocks[r], "seq", r) for r in range(1, seq_count)
    ]
    received, blocks = lax.optimization_barrier((received, blocks))
    constants = dft_constants()
    spectrum = filter_spectrum(seq_id, constants, blocks)

    span_ids = jnp.arange(span_count, dtype=jnp.int32)
    my_sources = lax.dynamic_index_in_dim(sources, my_dp, 0, keepdims=False)
    same_source = my_sources[:, None] == my_sources[None, :]
    lower_slot = span_ids[:, None] > span_ids[None, :]
    my_order = jnp.sum((same_source & lower_slot).astype(jnp.int32), axis=1)
    place = (my_sources * MOST + my_order) * span_rows
    target = (place[:, None] + jnp.arange(span_rows, dtype=jnp.int32)[None, :]).reshape(tok_rows)
    slot_rows = jnp.arange(dp_count * MOST * span_rows, dtype=jnp.int32)
    take = (target[:, None] == slot_rows[None, :]).astype(BF16)
    give = (slot_rows[:, None] == target[None, :]).astype(BF16)

    ids = segments[0] + 1
    before_ids = shifted(ids[-2:], "seq", 1)
    after_ids = shifted(ids[:2], "seq", -1)
    all_ids = jnp.concatenate([before_ids, ids, after_ids])
    here = all_ids[2 : tok_rows + 4]
    masks = jnp.stack([all_ids[1 : tok_rows + 3] == here, all_ids[: tok_rows + 2] == here], axis=1)
    masks = jnp.pad(masks.astype(F32), ((0, HALO - 2), (0, 0)))
    cot = cotangent[0]
    next_cot = jnp.pad(shifted(cot[:2], "seq", -1), ((0, HALO - 2), (0, 0)))
    weights = jnp.transpose(short_weight, (1, 0, 2))

    last = lax.dynamic_slice(received, (place[-1], 0), (span_rows, width))[-2:]
    first = lax.dynamic_slice(received, (place[0], 0), (span_rows, width))[:2]
    prev = shifted(last, "seq", 1)
    after = shifted(first, "seq", -1)

    columns = exchange(gather_rows(received, take, prev, masks, weights, cot), "seq")
    hats = make_hats(received, take, prev, after, masks, weights)
    results, cross = conv_both(columns, spectrum, constants)
    local = exchange(results, "seq")
    lags = halving_sum(filter_grad(jnp.stack([my_dp, my_seq]), cross, constants, spectrum[3]))

    back = back_rows(hats, give, masks, weights, cot, next_cot, local)
    back, local, lags = lax.optimization_barrier((back, local, lags))
    returned = exchange(back, "dp")
    mixed, taps = mixed_and_sums(received, take, prev, hats, masks, weights, cot, local)
    lags = cube_exchange(lags.astype(BF16), "seq")
    taps = total_over(taps, "seq")
    final = jnp.concatenate([lags.reshape(128, LANES), taps.astype(BF16).reshape(144, LANES)], axis=0)
    final = jnp.broadcast_to(final[None], (dp_count, *final.shape))
    returned, final = lax.optimization_barrier((returned, final))
    final = exchange(final, "dp")
    grad_stored = store_grads(select, returned, channels)
    grad_filter, grad_short = final_parts(seq_id, final)
    return (mixed[None], grad_stored[None], grad_filter, grad_short.reshape(3, 3, channels))


def solution(mesh):
    return jax.shard_map(
        shards,
        mesh=mesh,
        in_specs=(
            P("dp", "seq", None),
            P(None, "seq", None),
            P(None, "seq"),
            P("dp", "seq"),
            P(),
            P("seq", None),
            P("dp", "seq", None),
        ),
        out_specs=(P("dp", "seq", None), P("dp", "seq", None), P("seq", None), P()),
        check_vma=False,
    )
```

```python
import functools
import math

import jax
import jax.numpy as jnp
import numpy as np
from jax import lax
from jax.experimental import pallas as pl
from jax.experimental.pallas import tpu as pltpu
from jax.sharding import PartitionSpec as P

MOST = 2
CHUNK = 512
LANES = 128
HALO = 8
F32 = jnp.float32
BF16 = jnp.bfloat16


def shifted(value, axis, by):
    length = lax.axis_size(axis)
    pairs = [(i, i + by) for i in range(length) if 0 <= i + by < length]
    return lax.ppermute(value, axis, pairs)


def exchange(value, axis):
    return lax.all_to_all(value, axis, 0, 0, tiled=True)


def dot(left, right):
    return jnp.dot(left, right, preferred_element_type=F32)


def dot_t(left, right):
    return lax.dot_general(left, right, (((0,), (0,)), ((), ())), preferred_element_type=F32)


def iota(shape, axis):
    return lax.broadcasted_iota(jnp.int32, shape, axis)


def whole(*shape):
    return pl.BlockSpec(shape, lambda *ids: (0,) * len(shape))


SMEM = pl.BlockSpec(memory_space=pltpu.SMEM)


def outer_tables():
    blocks = np.arange(16)
    forward = [np.ones(16), np.cos(np.pi * blocks)]
    back = [np.ones(16), np.cos(np.pi * blocks)]
    for k in range(1, 16):
        angle = 2.0 * np.pi * k * blocks / 32.0
        forward += [np.cos(angle), -np.sin(angle)]
        back += [2.0 * np.cos(angle), -2.0 * np.sin(angle)]
    return np.stack(forward), np.stack(back, axis=1) / 4096.0


def spread_in(table, by):
    rows, cols = table.shape
    tall = (iota((rows * by, rows), 0) // by == iota((rows * by, rows), 1)).astype(BF16)
    wide = (iota((cols, cols * by), 0) == iota((cols, cols * by), 1) // by).astype(BF16)
    value = dot(dot(tall, table).astype(BF16), wide)
    shape = (rows * by, cols * by)
    diagonal = iota(shape, 0) % by == iota(shape, 1) % by
    return jnp.where(diagonal, value, 0.0).astype(BF16)


def dft_constants():
    inner = np.arange(LANES)
    turn = 2.0 * np.pi * (inner[:, None] * inner[None, :] % LANES) / LANES
    order = np.asarray([0, 16] + list(range(1, 16)))
    twist = 2.0 * np.pi * order[:, None] * inner[None, :] / 4096.0
    values = (
        np.cos(turn),
        np.sin(turn),
        np.stack([np.cos(twist), np.sin(twist)], axis=1),
        np.stack([np.cos(twist), np.sin(twist)], axis=2),
    )
    return tuple(jnp.asarray(value, F32) for value in values)


def turned(fc_ref, fs_ref, wc, ws):
    fc = fc_ref[...]
    fs = fs_ref[...]
    return fc * wc - fs * ws, fs * wc + fc * ws


def forward_table(fc_ref, fs_ref, row_ref, k):
    row = row_ref[k]
    cos, sin = turned(fc_ref, fs_ref, row[0:1, :], row[1:2, :])
    cos, sin, minus = cos.astype(BF16), sin.astype(BF16), (-sin).astype(BF16)
    return jnp.concatenate(
        [jnp.concatenate([cos, sin], axis=1), jnp.concatenate([minus, cos], axis=1)], axis=0
    )


def back_table(fc_ref, fs_ref, col_ref, k):
    col = col_ref[k]
    cos, sin = turned(fc_ref, fs_ref, col[:, 0:1], col[:, 1:2])
    cos, sin, minus = cos.astype(BF16), sin.astype(BF16), (-sin).astype(BF16)
    return jnp.concatenate(
        [jnp.concatenate([cos, minus], axis=1), jnp.concatenate([sin, cos], axis=1)], axis=0
    )


def pack_kernel(me_ref, source_ref, span_ref, stored_ref, out_ref, select_ref, take_ref, place_ref):
    @pl.when(pl.program_id(0) == 0)
    def _():
        mine = (source_ref[...] == me_ref[0]).astype(F32)
        before = (iota((16, 16), 0) < iota((16, 16), 1)).astype(F32)
        earlier = dot(mine, before)
        tall = (iota((256, 16), 0) // 16 == iota((256, 16), 1)).astype(F32)
        row = iota((256, 16), 0)
        hit = dot(tall, mine) * (dot(tall, earlier) == (row // 8 % 2).astype(F32)).astype(F32)
        start = jnp.sum(hit * (dot(tall, span_ref[...].astype(F32)) * 8.0 + 1.0), axis=1, keepdims=True)
        target = jnp.where(start > 0.5, start - 1.0 + (iota((256, 1), 0) % 8).astype(F32), -1.0)
        select_ref[...] = (iota((256, 128), 1).astype(F32) == target).astype(F32).astype(BF16)

    @pl.when(pl.program_id(0) == pl.num_programs(0) - 1)
    def _():
        sources = source_ref[...].astype(F32)
        row = iota((16, 16), 0)
        col = iota((16, 16), 1)
        ours = jnp.sum(jnp.where(row == me_ref[0], sources, 0.0), axis=0, keepdims=True)
        ours_down = jnp.sum(jnp.where(row == col, ours, 0.0), axis=1, keepdims=True)
        order = jnp.sum(((ours_down == ours) & (col < row)).astype(F32), axis=1, keepdims=True)
        place = (ours_down * MOST + order) * 8.0
        place_ref[...] = place.astype(jnp.int32)
        place_across = jnp.sum(jnp.where(row == col, place, 0.0), axis=0, keepdims=True)
        mine = iota((128, 16), 0) // 8 == iota((128, 16), 1)
        target = jnp.sum(jnp.where(mine, place_across, 0.0), axis=1, keepdims=True)
        target = target + (iota((128, 1), 0) % 8).astype(F32)
        take_ref[...] = (iota((128, 256), 1).astype(F32) == target).astype(F32).astype(BF16)

    out_ref[...] = dot(select_ref[...], stored_ref[...]).astype(BF16)


def pack_rows(me, sources, spans, stored):
    width = 1024
    return pl.pallas_call(
        pack_kernel,
        grid=(stored.shape[1] // width,),
        in_specs=[
            SMEM,
            whole(16, 16),
            whole(16, 16),
            pl.BlockSpec((128, width), lambda c: (0, c)),
        ],
        out_specs=[
            pl.BlockSpec((256, width), lambda c: (0, c)),
            whole(256, 128),
            whole(128, 256),
            whole(16, 1),
        ],
        out_shape=[
            jax.ShapeDtypeStruct((256, stored.shape[1]), BF16),
            jax.ShapeDtypeStruct((256, 128), BF16),
            jax.ShapeDtypeStruct((128, 256), BF16),
            jax.ShapeDtypeStruct((16, 1), jnp.int32),
        ],
        name="pack_rows",
    )(me, sources, spans, stored)


def filter_blocks_kernel(me_ref, taps_ref, *out_refs):
    for r, out_ref in enumerate(out_refs):
        for h in range(4):
            at = pl.multiple_of((me_ref[0] ^ (r | 4 * h)) * LANES, LANES)
            out_ref[h] = taps_ref[:, pl.ds(at, LANES)].astype(BF16)


def filter_blocks(me, filter_taps):
    return pl.pallas_call(
        filter_blocks_kernel,
        in_specs=[SMEM, pl.BlockSpec(memory_space=pltpu.VMEM)],
        out_specs=[pl.BlockSpec(memory_space=pltpu.VMEM)] * 4,
        out_shape=[jax.ShapeDtypeStruct((4, 128, LANES), BF16)] * 4,
        name="filter_blocks",
    )(me, filter_taps)


def masks_of(ids_ref):
    here = ids_ref[8:144, :]
    return (ids_ref[7:143, :] == here).astype(F32), (ids_ref[6:142, :] == here).astype(F32)


def gather_kernel(k_ref, v_ref, q_ref, take_ref, ids_ref, w_ref, cot_ref, out_ref, xs, edge):
    take = take_ref[...]
    m1, m2 = masks_of(ids_ref)
    for s, ref in enumerate((k_ref, v_ref, q_ref)):
        xs[s, 0:8, :] = jnp.zeros((8, CHUNK), F32)
        xs[s, 8:136, :] = dot(take, ref[...])
        xs[s, 136:144, :] = jnp.zeros((8, CHUNK), F32)

    def part(h, carry):
        at = pl.ds(pl.multiple_of(h * LANES, LANES), LANES)
        hats = []
        for s in range(3):
            w = w_ref[:, s, at]
            hats.append(
                w[0:1] * xs[s, 8:144, at]
                + w[1:2] * (xs[s, 7:143, at] * m1)
                + w[2:3] * (xs[s, 6:142, at] * m2)
            )
            edge[2 * s : 2 * s + 2, :] = hats[s][0:2]
            edge[2 * s + 8 : 2 * s + 10, :] = hats[s][128:130]
        cot = cot_ref[:, at].astype(F32)
        edge[6:8, :] = cot[0:2]
        edge[14:16, :] = jnp.zeros((2, LANES), F32)
        out_ref[h, 0:128, :] = (hats[0] * hats[1])[0:128].astype(BF16)
        out_ref[h, 128:256, :] = (cot * hats[2][0:128]).astype(BF16)
        out_ref[h, 256:272, :] = edge[...].astype(BF16)
        return carry

    lax.fori_loop(0, CHUNK // LANES, part, 0)


def stream_specs(rows, chunks):
    return [pl.BlockSpec((rows, CHUNK), lambda c, s=s: (0, s * chunks + c)) for s in range(3)]


def column_spec(rows):
    return pl.BlockSpec((rows, CHUNK), lambda c: (0, c))


WEIGHTS = pl.BlockSpec((3, 3, CHUNK), lambda c: (0, 0, c))


def gather_rows(received, take, ids, weights, cot):
    chunks = cot.shape[1] // CHUNK
    per = CHUNK // LANES
    return pl.pallas_call(
        gather_kernel,
        grid=(chunks,),
        in_specs=stream_specs(256, chunks)
        + [whole(128, 256), whole(144, 1), WEIGHTS, column_spec(128)],
        out_specs=pl.BlockSpec((per, 272, LANES), lambda c: (c, 0, 0)),
        out_shape=jax.ShapeDtypeStruct((chunks * per, 272, LANES), BF16),
        scratch_shapes=[pltpu.VMEM((3, 144, CHUNK), F32), pltpu.VMEM((16, LANES), F32)],
        name="gather_rows",
    )(received, received, received, take, ids, weights, cot)


def outer_forward(fh_ref, pick, spec):
    nothing = jnp.zeros(spec.shape[1:], BF16)
    for where in (1, 3):
        spec[where] = nothing
    for g in range(8):
        at = slice(16 * g, 16 * g + 16)
        data = pick(g)
        value = dot(fh_ref[...], data).astype(BF16)
        spec[0, at, :] = value[0:16]
        spec[2, at, :] = value[16:32]
        spec[4:34, at, :] = value[32:512].reshape(30, 16, value.shape[1])


def outer_back(bh_ref, turns, g):
    at = slice(16 * g, 16 * g + 16)
    rest = turns[4:34, at, :].reshape(480, turns.shape[2])
    return dot(bh_ref[...], jnp.concatenate([turns[0, at, :], turns[2, at, :], rest], axis=0))


def pair_of(ref, k):
    return ref[pl.ds(2 * k, 2)].reshape(2 * LANES, ref.shape[2])


def put_pair(ref, k, value):
    ref[pl.ds(2 * k, 2)] = value.astype(BF16).reshape(2, LANES, ref.shape[2])


VMEM_SPEC = pl.BlockSpec(memory_space=pltpu.VMEM)


def inner_loop(step):
    def four(i, carry):
        for j in range(4):
            step(4 * i + j)
        return carry

    lax.fori_loop(0, 4, four, 0)
    step(16)


def filter_kernel(me_ref, fc_ref, fs_ref, row_ref, of_ref, ob_ref, *rest):
    blocks, (out_ref, f_ref, b_ref, ordered, spec) = rest[:7], rest[7:]
    f_ref[...] = spread_in(of_ref[...], 16)
    b_ref[...] = spread_in(ob_ref[...], 16)
    for r in range(4):
        ordered[me_ref[0] ^ r] = blocks[r][0]
        for h in range(1, 4):
            ordered[me_ref[0] ^ (r | 4 * h)] = blocks[3 + h][r]
    outer_forward(f_ref, lambda g: ordered[:, 16 * g : 16 * g + 16, :].reshape(256, LANES), spec)

    def step(k, carry):
        out_ref[k] = dot(forward_table(fc_ref, fs_ref, row_ref, k), pair_of(spec, k)).astype(BF16)
        return carry

    lax.fori_loop(0, 17, step, 0)


def rounded(table):
    return jnp.asarray(np.asarray(table, np.float32).astype(jnp.bfloat16))


def filter_spectrum(me, constants, blocks):
    fc, fs, row, _ = constants
    forward, back = outer_tables()
    return pl.pallas_call(
        filter_kernel,
        in_specs=[SMEM] + [VMEM_SPEC] * 12,
        out_specs=[VMEM_SPEC] * 3,
        out_shape=[
            jax.ShapeDtypeStruct((17, 2 * LANES, LANES), BF16),
            jax.ShapeDtypeStruct((512, 256), BF16),
            jax.ShapeDtypeStruct((256, 512), BF16),
        ],
        scratch_shapes=[pltpu.VMEM((16, 128, LANES), BF16), pltpu.VMEM((34, LANES, LANES), BF16)],
        name="filter_spectrum",
    )(me, fc, fs, row, rounded(forward), rounded(back), *blocks)


def conv_kernel(
    in_ref, h_ref, fc_ref, fs_ref, row_ref, col_ref, f_ref, b_ref, out_ref, cross_ref, spec, turns,
):
    def pick(g):
        if g:
            parts = [in_ref[:, 128 * i + 16 * g : 128 * i + 16 * g + 16, :] for i in range(2)]
        else:
            edges = in_ref[:, 256:272, :].astype(F32)
            nothing = jnp.zeros((1, 8, LANES), F32)
            filtered = edges[:, 0:8] + jnp.concatenate([nothing, edges[:15, 8:16]], axis=0)
            gated = filtered * pltpu.roll(filtered, 6, 1)
            heads = (gated, pltpu.roll(gated, 4, 1))
            rows = iota((16, 16, LANES), 1)
            parts = []
            for i in range(2):
                head = jnp.concatenate([heads[i], heads[i]], axis=1)
                plain = in_ref[:, 128 * i : 128 * i + 16, :].astype(F32)
                parts.append(jnp.where(rows < 2, head, plain).astype(BF16))
        return jnp.concatenate([part.reshape(256, LANES) for part in parts], axis=1)

    outer_forward(f_ref, pick, spec)

    def step(k):
        value = dot(forward_table(fc_ref, fs_ref, row_ref, k), pair_of(spec, k))
        xr, xi = value[:LANES, :LANES], value[LANES:, :LANES]
        gr, gi = value[:LANES, LANES:], value[LANES:, LANES:]
        h = h_ref[k].astype(F32)
        hr, hi = h[:LANES], h[LANES:]
        cross = jnp.concatenate([xr * gr + xi * gi, xr * gi - xi * gr], axis=0)
        cross_ref[k] = cross.astype(BF16)
        real = jnp.concatenate([hr * xr - hi * xi, hr * gr + hi * gi], axis=1)
        imag = jnp.concatenate([hr * xi + hi * xr, hr * gi - hi * gr], axis=1)
        mixed = jnp.concatenate([real, imag], axis=0).astype(BF16)
        put_pair(turns, k, dot(back_table(fc_ref, fs_ref, col_ref, k), mixed))

    inner_loop(step)
    for g in range(8):
        last = outer_back(b_ref, turns, g)
        parts = [last[:, i * LANES : (i + 1) * LANES].reshape(16, 16, LANES) for i in range(2)]
        for i in range(2):
            out_ref[:, 128 * i + 16 * g : 128 * i + 16 * g + 16, :] = parts[i].astype(BF16)
        if g == 0:
            leads = jnp.concatenate([part[1:, 0:8, :] for part in parts], axis=1)
            leads = jnp.concatenate([leads, jnp.zeros((1, 16, LANES), F32)], axis=0)
            out_ref[:, 256:272, :] = leads.astype(BF16)


def conv_both(columns, spectrum, constants):
    h, forward, back = spectrum
    return pl.pallas_call(
        conv_kernel,
        in_specs=[VMEM_SPEC] * 8,
        out_specs=[VMEM_SPEC] * 2,
        out_shape=[
            jax.ShapeDtypeStruct((16, 272, LANES), BF16),
            jax.ShapeDtypeStruct((17, 2 * LANES, LANES), BF16),
        ],
        scratch_shapes=[pltpu.VMEM((34, LANES, 2 * LANES), BF16) for _ in range(2)],
        name="conv_both",
    )(columns, h, *constants, forward, back)


def reversed_bits(j):
    return ((j & 1) << 3) | ((j & 2) << 1) | ((j & 4) >> 1) | ((j & 8) >> 3)


def filter_grad_kernel(ids_ref, cross_ref, fc_ref, fs_ref, col_ref, bh_ref, out_ref, turns):
    def step(k):
        put_pair(turns, k, dot(back_table(fc_ref, fs_ref, col_ref, k), cross_ref[k]))

    inner_loop(step)
    for g in range(8):
        part = outer_back(bh_ref, turns, g).reshape(16, 16, LANES)
        for e in range(2):
            place = reversed_bits((2 * g + e) ^ ids_ref[0])
            for p in range(16):
                out_ref[place, p ^ ids_ref[1]] = part[p, 8 * e : 8 * e + 8].astype(BF16)


def filter_grad(ids, cross, constants, back):
    fc, fs, _, col = constants
    return pl.pallas_call(
        filter_grad_kernel,
        in_specs=[SMEM] + [VMEM_SPEC] * 5,
        out_specs=VMEM_SPEC,
        out_shape=jax.ShapeDtypeStruct((16, 16, 8, LANES), BF16),
        scratch_shapes=[pltpu.VMEM((34, LANES, LANES), BF16)],
        name="filter_grad",
    )(ids, cross, fc, fs, col, back)


def extended(take, streams, xs):
    for s, (ref, prev, after) in enumerate(streams):
        xs[s, 6:8, :] = prev[...].astype(F32)
        xs[s, 8:136, :] = dot(take, ref[...])
        xs[s, 136:144, :] = jnp.zeros((8, xs.shape[2]), F32)
        xs[s, 136:138, :] = after[...].astype(F32)


def hats_kernel(
    k_ref, v_ref, take_ref, pk_ref, pv_ref, nk_ref, nv_ref, ids_ref, w_ref, key_ref, value_ref, xs,
):
    m1, m2 = masks_of(ids_ref)
    extended(take_ref[...], ((k_ref, pk_ref, nk_ref), (v_ref, pv_ref, nv_ref)), xs)
    for s, out_ref in enumerate((key_ref, value_ref)):
        w = w_ref[:, s, :]
        out_ref[...] = (
            w[0:1] * xs[s, 8:144, :] + w[1:2] * (xs[s, 7:143, :] * m1) + w[2:3] * (xs[s, 6:142, :] * m2)
        )


def make_hats(received, take, prev, after, ids, weights):
    channels = weights.shape[2]
    chunks = channels // CHUNK
    return pl.pallas_call(
        hats_kernel,
        grid=(chunks,),
        in_specs=stream_specs(256, chunks)[:2]
        + [whole(128, 256)]
        + stream_specs(2, chunks)[:2]
        + stream_specs(2, chunks)[:2]
        + [whole(144, 1), WEIGHTS],
        out_specs=[column_spec(136)] * 2,
        out_shape=[jax.ShapeDtypeStruct((136, channels), F32)] * 2,
        scratch_shapes=[pltpu.VMEM((2, 144, CHUNK), F32)],
        name="make_hats",
    )(received, received, take, prev, prev, after, after, ids, weights)


def spread_rows(conv_ref, h):
    tail = conv_ref[h, 256:272, :].astype(F32)
    conv = jnp.concatenate([conv_ref[h, 0:128, :].astype(F32), tail[0:8]], axis=0)
    grad_product = jnp.concatenate([conv_ref[h, 128:256, :].astype(F32), tail[8:16]], axis=0)
    return conv, grad_product


def back_kernel(
    key_ref, value_ref, give_ref, ids_ref, w_ref, cot_ref, next_cot_ref, conv_ref, back_ref, one, two,
):
    give = give_ref[...]
    m1, m2 = masks_of(ids_ref)

    def part(h, carry):
        at = pl.ds(pl.multiple_of(h * LANES, LANES), LANES)
        conv, grad_product = spread_rows(conv_ref, h)
        cot = jnp.concatenate([cot_ref[:, at].astype(F32), next_cot_ref[:, at].astype(F32)], axis=0)
        grads = (grad_product * value_ref[:, at], grad_product * key_ref[:, at], cot * conv)
        for s in range(3):
            w = w_ref[:, s, at]
            grad = grads[s]
            one[s] = grad * m1
            two[s] = grad * m2
            rows = w[0:1] * grad[0:128] + w[1:2] * one[s, 1:129] + w[2:3] * two[s, 2:130]
            sent = dot(give, rows.astype(BF16)).astype(BF16)
            back_ref[:, 16 * s : 16 * s + 16, at] = sent.reshape(16, 16, LANES)
        return carry

    lax.fori_loop(0, CHUNK // LANES, part, 0)


def back_rows(hats, give, ids, weights, cot, next_cot, local):
    channels = cot.shape[1]
    chunks = channels // CHUNK
    per = CHUNK // LANES
    return pl.pallas_call(
        back_kernel,
        grid=(chunks,),
        in_specs=[
            column_spec(136),
            column_spec(136),
            whole(256, 128),
            whole(144, 1),
            WEIGHTS,
            column_spec(128),
            column_spec(8),
            pl.BlockSpec((per, 272, LANES), lambda c: (c, 0, 0)),
        ],
        out_specs=pl.BlockSpec((16, 48, CHUNK), lambda c: (0, 0, c)),
        out_shape=jax.ShapeDtypeStruct((16, 48, channels), BF16),
        scratch_shapes=[pltpu.VMEM((3, 136, LANES), F32) for _ in range(2)],
        name="back_rows",
    )(*hats, give, ids, weights, cot, next_cot, local)


def sums_kernel(
    k_ref, v_ref, q_ref, take_ref, pk_ref, pv_ref, pq_ref, key_ref, value_ref, ids_ref, w_ref, cot_ref, conv_ref,
    mixed_ref, taps_ref, xs,
):
    take = take_ref[...]
    m1, m2 = (mask[0:128] for mask in masks_of(ids_ref))
    for s, (ref, prev) in enumerate(((k_ref, pk_ref), (v_ref, pv_ref), (q_ref, pq_ref))):
        xs[s, 6:8, :] = prev[...].astype(F32)
        xs[s, 8:136, :] = dot(take, ref[...])

    def part(h, carry):
        at = pl.ds(pl.multiple_of(h * LANES, LANES), LANES)
        conv = conv_ref[h, 0:128, :].astype(F32)
        grad_product = conv_ref[h, 128:256, :].astype(F32)
        cot = cot_ref[:, at].astype(F32)
        grads = (grad_product * value_ref[0:128, at], grad_product * key_ref[0:128, at], cot * conv)
        for s in range(3):
            parts = (xs[s, 8:136, at], xs[s, 7:135, at] * m1, xs[s, 6:134, at] * m2)
            for k in range(3):
                total = jnp.sum(grads[s] * parts[k], axis=0, keepdims=True)
                taps_ref[3 * s + k, pl.ds((CHUNK // LANES) * pl.program_id(0) + h, 1), :] = total
            if s == 2:
                w = w_ref[:, s, at]
                query = w[0:1] * parts[0] + w[1:2] * parts[1] + w[2:3] * parts[2]
                mixed_ref[:, at] = (query * conv).astype(BF16)
        return carry

    lax.fori_loop(0, CHUNK // LANES, part, 0)


def mixed_and_sums(received, take, prev, hats, ids, weights, cot, local):
    channels = cot.shape[1]
    chunks = channels // CHUNK
    per = CHUNK // LANES
    return pl.pallas_call(
        sums_kernel,
        grid=(chunks,),
        in_specs=stream_specs(256, chunks)
        + [whole(128, 256)]
        + stream_specs(2, chunks)
        + [
            column_spec(136),
            column_spec(136),
            whole(144, 1),
            WEIGHTS,
            column_spec(128),
            pl.BlockSpec((per, 272, LANES), lambda c: (c, 0, 0)),
        ],
        out_specs=[column_spec(128), whole(9, 16, LANES)],
        out_shape=[
            jax.ShapeDtypeStruct((128, channels), BF16),
            jax.ShapeDtypeStruct((9, 16, LANES), F32),
        ],
        scratch_shapes=[pltpu.VMEM((3, 136, CHUNK), F32)],
        name="mixed_and_sums",
    )(received, received, received, take, prev, prev, prev, *hats, ids, weights, cot, local)


def store_kernel(select_ref, in_ref, out_ref):
    width = in_ref.shape[2]
    out_ref[...] = dot_t(select_ref[...], in_ref[...].reshape(256, width)).astype(BF16)


def store_grads(select, returned, channels):
    width = 1024
    chunks = channels // width
    return pl.pallas_call(
        store_kernel,
        grid=(3, chunks),
        in_specs=[
            whole(256, 128),
            pl.BlockSpec((16, 16, width), lambda s, c: (0, s, c)),
        ],
        out_specs=pl.BlockSpec((128, width), lambda s, c: (0, s * chunks + c)),
        out_shape=jax.ShapeDtypeStruct((128, 3 * channels), BF16),
        name="store_grads",
    )(select, returned)


def final_kernel(me_ref, in_ref, grad_ref, taps_ref, total):
    for j in range(16):
        at = pl.multiple_of((j ^ me_ref[0]) * LANES, LANES)
        grad_ref[:, pl.ds(at, LANES)] = in_ref[:, 8 * j : 8 * j + 8, :].astype(F32).reshape(128, LANES)
    total[...] = jnp.sum(in_ref[:, 128:272, :].astype(F32), axis=0).reshape(9, 16, LANES)
    for i in range(3):
        for c in range(16):
            taps_ref[i, :, c * LANES : (c + 1) * LANES] = total[3 * i : 3 * i + 3, c, :]


def final_parts(me, final):
    return pl.pallas_call(
        final_kernel,
        in_specs=[SMEM, VMEM_SPEC],
        out_specs=[VMEM_SPEC] * 2,
        out_shape=[jax.ShapeDtypeStruct((128, 2048), F32), jax.ShapeDtypeStruct((3, 3, 2048), F32)],
        scratch_shapes=[pltpu.VMEM((9, 16, LANES), F32)],
        name="final_parts",
    )(me, final)


def across(value, axis, bit):
    return lax.ppermute(value, axis, [(i, i ^ bit) for i in range(lax.axis_size(axis))])


def halving_sum(value):
    total = value.astype(F32)
    for bit in (1, 2, 4, 8):
        half = total.shape[0] // 2
        total = total[:half] + across(total[half:].astype(BF16), "dp", bit).astype(F32)
    return total[0]


def cube_exchange(value, axis):
    shape = value.shape
    for bit in (1, 2, 4, 8):
        grouped = value.reshape(shape[0] // (2 * bit), 2, bit, *shape[1:])
        other = across(grouped[:, 1], axis, bit)
        value = jnp.stack([grouped[:, 0], other], axis=1).reshape(shape)
    return value


def total_over(value, axis):
    for bit in (1, 2, 4, 8):
        value = value + across(value, axis, bit)
    return value


def shards(stored, source_row, source_span, segments, short_weight, filter_taps, cotangent):
    dp_count = lax.axis_size("dp")
    my_dp = lax.axis_index("dp").astype(jnp.int32)
    my_seq = lax.axis_index("seq").astype(jnp.int32)
    tok_rows = stored.shape[1]
    width = stored.shape[2]
    channels = width // 3
    span_count = source_span.shape[1]
    span_rows = tok_rows // span_count
    sources = source_row[:, :, 0]
    dp_id, seq_id = my_dp[None], my_seq[None]

    sent, select, take, place = pack_rows(dp_id, sources, source_span, stored[0])
    received = exchange(sent.reshape(dp_count, MOST * span_rows, width), "dp")
    received = received.reshape(dp_count * MOST * span_rows, width)

    near = filter_blocks(seq_id, filter_taps)
    near = [near[0]] + [across(near[r], "seq", r) for r in range(1, 4)]
    far = [across(jnp.stack([part[h] for part in near]), "seq", 4 * h) for h in range(1, 4)]

    ids = segments[0] + 1
    outside = jnp.full((6,), -1, jnp.int32)
    ids = jnp.concatenate([outside, shifted(ids[-2:], "seq", 1), ids, shifted(ids[:2], "seq", -1), outside])
    ids = ids.astype(F32)[:, None]
    cot = cotangent[0]
    weights = jnp.transpose(short_weight, (1, 0, 2))
    received, near, far, ids, weights = lax.optimization_barrier((received, near, far, ids, weights))

    columns = exchange(gather_rows(received, take, ids, weights, cot), "seq")
    constants = dft_constants()
    spectrum = filter_spectrum(seq_id, constants, near + far)
    next_cot = jnp.pad(shifted(cot[:2], "seq", -1), ((0, HALO - 2), (0, 0)))
    last = lax.dynamic_slice(received, (place[-1, 0], 0), (span_rows, width))[-2:]
    first = lax.dynamic_slice(received, (place[0, 0], 0), (span_rows, width))[:2]
    prev = shifted(last, "seq", 1)
    after = shifted(first, "seq", -1)
    hats = make_hats(received, take, prev, after, ids, weights)
    give = jnp.transpose(take)
    columns, hats, give, next_cot = lax.optimization_barrier((columns, hats, give, next_cot))

    results, cross = conv_both(columns, spectrum, constants)
    local = exchange(results, "seq")
    lags = halving_sum(filter_grad(jnp.stack([my_dp, my_seq]), cross, constants, spectrum[2]))

    back = back_rows(hats, give, ids, weights, cot, next_cot, local)
    back, local, lags = lax.optimization_barrier((back, local, lags))
    returned = exchange(back, "dp")
    mixed, taps = mixed_and_sums(received, take, prev, hats, ids, weights, cot, local)
    lags = cube_exchange(lags.astype(BF16), "seq")
    taps = total_over(taps, "seq")
    final = jnp.concatenate([lags.reshape(128, LANES), taps.astype(BF16).reshape(144, LANES)], axis=0)
    final = jnp.broadcast_to(final[None], (dp_count, *final.shape))
    returned, final = lax.optimization_barrier((returned, final))
    final = exchange(final, "dp")
    grad_stored = store_grads(select, returned, channels)
    grad_filter, grad_short = final_parts(seq_id, final)
    return (mixed[None], grad_stored[None], grad_filter, grad_short)


def solution(mesh):
    return jax.shard_map(
        shards,
        mesh=mesh,
        in_specs=(
            P("dp", "seq", None),
            P(None, "seq", None),
            P(None, "seq"),
            P("dp", "seq"),
            P(),
            P("seq", None),
            P("dp", "seq", None),
        ),
        out_specs=(P("dp", "seq", None), P("dp", "seq", None), P("seq", None), P()),
        check_vma=False,
    )
```

```python
import functools
import math

import jax
import jax.numpy as jnp
import numpy as np
from jax import lax
from jax.experimental import pallas as pl
from jax.experimental.pallas import tpu as pltpu
from jax.sharding import PartitionSpec as P

MOST = 2
CHUNK = 512
LANES = 128
F32 = jnp.float32
BF16 = jnp.bfloat16


def shifted(value, axis, by):
    length = lax.axis_size(axis)
    pairs = [(i, i + by) for i in range(length) if 0 <= i + by < length]
    return lax.ppermute(value, axis, pairs)


def exchange(value, axis):
    return lax.all_to_all(value, axis, 0, 0, tiled=True)


def dot(left, right):
    return jnp.dot(left, right, preferred_element_type=F32)


def dot_t(left, right):
    return lax.dot_general(left, right, (((0,), (0,)), ((), ())), preferred_element_type=F32)


def iota(shape, axis):
    return lax.broadcasted_iota(jnp.int32, shape, axis)


def whole(*shape):
    return pl.BlockSpec(shape, lambda *ids: (0,) * len(shape))


SMEM = pl.BlockSpec(memory_space=pltpu.SMEM)


def outer_tables():
    blocks = np.arange(16)
    forward = [np.ones(16), np.cos(np.pi * blocks)]
    back = [np.ones(16), np.cos(np.pi * blocks)]
    for k in range(1, 16):
        angle = 2.0 * np.pi * k * blocks / 32.0
        forward += [np.cos(angle), -np.sin(angle)]
        back += [2.0 * np.cos(angle), -2.0 * np.sin(angle)]
    return np.stack(forward), np.stack(back, axis=1) / 4096.0


def spread_in(table, by):
    rows, cols = table.shape
    tall = (iota((rows * by, rows), 0) // by == iota((rows * by, rows), 1)).astype(BF16)
    wide = (iota((cols, cols * by), 0) == iota((cols, cols * by), 1) // by).astype(BF16)
    value = dot(dot(tall, table).astype(BF16), wide)
    shape = (rows * by, cols * by)
    diagonal = iota(shape, 0) % by == iota(shape, 1) % by
    return jnp.where(diagonal, value, 0.0).astype(BF16)


def dft_constants():
    inner = np.arange(LANES)
    turn = 2.0 * np.pi * (inner[:, None] * inner[None, :] % LANES) / LANES
    order = np.asarray([0, 16] + list(range(1, 16)))
    twist = 2.0 * np.pi * order[:, None] * inner[None, :] / 4096.0
    values = (
        np.cos(turn),
        np.sin(turn),
        np.stack([np.cos(twist), np.sin(twist)], axis=1),
        np.stack([np.cos(twist), np.sin(twist)], axis=2),
    )
    return tuple(jnp.asarray(value, F32) for value in values)


def turned(fc_ref, fs_ref, wc, ws):
    fc = fc_ref[...]
    fs = fs_ref[...]
    return fc * wc - fs * ws, fs * wc + fc * ws


def forward_table(fc_ref, fs_ref, row_ref, k):
    row = row_ref[k]
    cos, sin = turned(fc_ref, fs_ref, row[0:1, :], row[1:2, :])
    cos, sin, minus = cos.astype(BF16), sin.astype(BF16), (-sin).astype(BF16)
    return jnp.concatenate(
        [jnp.concatenate([cos, sin], axis=1), jnp.concatenate([minus, cos], axis=1)], axis=0
    )


def back_table(fc_ref, fs_ref, col_ref, k):
    col = col_ref[k]
    cos, sin = turned(fc_ref, fs_ref, col[:, 0:1], col[:, 1:2])
    cos, sin, minus = cos.astype(BF16), sin.astype(BF16), (-sin).astype(BF16)
    return jnp.concatenate(
        [jnp.concatenate([cos, minus], axis=1), jnp.concatenate([sin, cos], axis=1)], axis=0
    )


def pack_kernel(me_ref, source_ref, span_ref, stored_ref, out_ref, select_ref, take_ref, place_ref):
    @pl.when(pl.program_id(0) == 0)
    def _():
        mine = (source_ref[...] == me_ref[0]).astype(F32)
        before = (iota((16, 16), 0) < iota((16, 16), 1)).astype(F32)
        earlier = dot(mine, before)
        tall = (iota((256, 16), 0) // 16 == iota((256, 16), 1)).astype(F32)
        row = iota((256, 16), 0)
        hit = dot(tall, mine) * (dot(tall, earlier) == (row // 8 % 2).astype(F32)).astype(F32)
        start = jnp.sum(hit * (dot(tall, span_ref[...].astype(F32)) * 8.0 + 1.0), axis=1, keepdims=True)
        target = jnp.where(start > 0.5, start - 1.0 + (iota((256, 1), 0) % 8).astype(F32), -1.0)
        select_ref[...] = (iota((256, 128), 1).astype(F32) == target).astype(F32).astype(BF16)

    @pl.when(pl.program_id(0) == pl.num_programs(0) - 1)
    def _():
        sources = source_ref[...].astype(F32)
        row = iota((16, 16), 0)
        col = iota((16, 16), 1)
        ours = jnp.sum(jnp.where(row == me_ref[0], sources, 0.0), axis=0, keepdims=True)
        ours_down = jnp.sum(jnp.where(row == col, ours, 0.0), axis=1, keepdims=True)
        order = jnp.sum(((ours_down == ours) & (col < row)).astype(F32), axis=1, keepdims=True)
        place = (ours_down * MOST + order) * 8.0
        place_ref[...] = place.astype(jnp.int32)
        place_across = jnp.sum(jnp.where(row == col, place, 0.0), axis=0, keepdims=True)
        mine = iota((128, 16), 0) // 8 == iota((128, 16), 1)
        target = jnp.sum(jnp.where(mine, place_across, 0.0), axis=1, keepdims=True)
        target = target + (iota((128, 1), 0) % 8).astype(F32)
        take_ref[...] = (iota((128, 256), 1).astype(F32) == target).astype(F32).astype(BF16)

    out_ref[...] = dot(select_ref[...], stored_ref[...]).astype(BF16)


def pack_rows(me, sources, spans, stored):
    width = 1024
    return pl.pallas_call(
        pack_kernel,
        grid=(stored.shape[1] // width,),
        in_specs=[
            SMEM,
            whole(16, 16),
            whole(16, 16),
            pl.BlockSpec((128, width), lambda c: (0, c)),
        ],
        out_specs=[
            pl.BlockSpec((256, width), lambda c: (0, c)),
            whole(256, 128),
            whole(128, 256),
            whole(16, 1),
        ],
        out_shape=[
            jax.ShapeDtypeStruct((256, stored.shape[1]), BF16),
            jax.ShapeDtypeStruct((256, 128), BF16),
            jax.ShapeDtypeStruct((128, 256), BF16),
            jax.ShapeDtypeStruct((16, 1), jnp.int32),
        ],
        name="pack_rows",
    )(me, sources, spans, stored)


def filter_blocks_kernel(me_ref, taps_ref, *out_refs):
    for r, out_ref in enumerate(out_refs):
        for h in range(4):
            at = pl.multiple_of((me_ref[0] ^ (r | 4 * h)) * LANES, LANES)
            out_ref[h] = taps_ref[:, pl.ds(at, LANES)].astype(BF16)


def filter_blocks(me, filter_taps):
    return pl.pallas_call(
        filter_blocks_kernel,
        in_specs=[SMEM, pl.BlockSpec(memory_space=pltpu.VMEM)],
        out_specs=[pl.BlockSpec(memory_space=pltpu.VMEM)] * 4,
        out_shape=[jax.ShapeDtypeStruct((4, 128, LANES), BF16)] * 4,
        name="filter_blocks",
    )(me, filter_taps)


def masks_of(ids_ref):
    here = ids_ref[8:144, :]
    return (ids_ref[7:143, :] == here).astype(F32), (ids_ref[6:142, :] == here).astype(F32)


def gather_kernel(k_ref, v_ref, q_ref, take_ref, ids_ref, w_ref, cot_ref, out_ref, xs, edge):
    take = take_ref[...]
    m1, m2 = masks_of(ids_ref)
    for s, ref in enumerate((k_ref, v_ref, q_ref)):
        xs[s, 0:8, :] = jnp.zeros((8, CHUNK), F32)
        xs[s, 8:136, :] = dot(take, ref[...])
        xs[s, 136:144, :] = jnp.zeros((8, CHUNK), F32)

    for h in range(CHUNK // LANES):
        at = slice(h * LANES, (h + 1) * LANES)
        hats = []
        for s in range(3):
            w = w_ref[:, s, at]
            hats.append(
                w[0:1] * xs[s, 8:144, at]
                + w[1:2] * (xs[s, 7:143, at] * m1)
                + w[2:3] * (xs[s, 6:142, at] * m2)
            )
            edge[2 * s : 2 * s + 2, :] = hats[s][0:2]
            edge[2 * s + 8 : 2 * s + 10, :] = hats[s][128:130]
        cot = cot_ref[:, at].astype(F32)
        edge[6:8, :] = cot[0:2]
        edge[14:16, :] = jnp.zeros((2, LANES), F32)
        out_ref[h, 0:128, :] = (hats[0] * hats[1])[0:128].astype(BF16)
        out_ref[h, 128:256, :] = (cot * hats[2][0:128]).astype(BF16)
        out_ref[h, 256:272, :] = edge[...].astype(BF16)


def stream_specs(rows, chunks):
    return [pl.BlockSpec((rows, CHUNK), lambda c, s=s: (0, s * chunks + c)) for s in range(3)]


def column_spec(rows):
    return pl.BlockSpec((rows, CHUNK), lambda c: (0, c))


WEIGHTS = pl.BlockSpec((3, 3, CHUNK), lambda c: (0, 0, c))


def gather_rows(received, take, ids, weights, cot):
    chunks = cot.shape[1] // CHUNK
    per = CHUNK // LANES
    return pl.pallas_call(
        gather_kernel,
        grid=(chunks,),
        in_specs=stream_specs(256, chunks)
        + [whole(128, 256), whole(144, 1), WEIGHTS, column_spec(128)],
        out_specs=pl.BlockSpec((per, 272, LANES), lambda c: (c, 0, 0)),
        out_shape=jax.ShapeDtypeStruct((chunks * per, 272, LANES), BF16),
        scratch_shapes=[pltpu.VMEM((3, 144, CHUNK), F32), pltpu.VMEM((16, LANES), F32)],
        name="gather_rows",
    )(received, received, received, take, ids, weights, cot)


def outer_forward(fh_ref, pick, spec):
    nothing = jnp.zeros(spec.shape[1:], BF16)
    for where in (1, 3):
        spec[where] = nothing
    for g in range(8):
        at = slice(16 * g, 16 * g + 16)
        data = pick(g)
        value = dot(fh_ref[...], data).astype(BF16)
        spec[0, at, :] = value[0:16]
        spec[2, at, :] = value[16:32]
        spec[4:34, at, :] = value[32:512].reshape(30, 16, value.shape[1])


def outer_back(bh_ref, turns, g):
    at = slice(16 * g, 16 * g + 16)
    rest = turns[4:34, at, :].reshape(480, turns.shape[2])
    return dot(bh_ref[...], jnp.concatenate([turns[0, at, :], turns[2, at, :], rest], axis=0))


def pair_of(ref, k):
    return ref[pl.ds(2 * k, 2)].reshape(2 * LANES, ref.shape[2])


def put_pair(ref, k, value):
    ref[pl.ds(2 * k, 2)] = value.astype(BF16).reshape(2, LANES, ref.shape[2])


VMEM_SPEC = pl.BlockSpec(memory_space=pltpu.VMEM)


def inner_loop(step):
    def four(i, carry):
        for j in range(4):
            step(4 * i + j)
        return carry

    lax.fori_loop(0, 4, four, 0)
    step(16)


def filter_kernel(me_ref, fc_ref, fs_ref, row_ref, of_ref, ob_ref, *rest):
    blocks, (out_ref, f_ref, b_ref, ordered, spec) = rest[:7], rest[7:]
    f_ref[...] = spread_in(of_ref[...], 16)
    b_ref[...] = spread_in(ob_ref[...], 16)
    for r in range(4):
        ordered[me_ref[0] ^ r] = blocks[r][0]
        for h in range(1, 4):
            ordered[me_ref[0] ^ (r | 4 * h)] = blocks[3 + h][r]
    outer_forward(f_ref, lambda g: ordered[:, 16 * g : 16 * g + 16, :].reshape(256, LANES), spec)

    def step(k, carry):
        out_ref[k] = dot(forward_table(fc_ref, fs_ref, row_ref, k), pair_of(spec, k)).astype(BF16)
        return carry

    lax.fori_loop(0, 17, step, 0)


def rounded(table):
    return jnp.asarray(np.asarray(table, np.float32).astype(jnp.bfloat16))


def filter_spectrum(me, constants, blocks):
    fc, fs, row, _ = constants
    forward, back = outer_tables()
    return pl.pallas_call(
        filter_kernel,
        in_specs=[SMEM] + [VMEM_SPEC] * 12,
        out_specs=[VMEM_SPEC] * 3,
        out_shape=[
            jax.ShapeDtypeStruct((17, 2 * LANES, LANES), BF16),
            jax.ShapeDtypeStruct((512, 256), BF16),
            jax.ShapeDtypeStruct((256, 512), BF16),
        ],
        scratch_shapes=[pltpu.VMEM((16, 128, LANES), BF16), pltpu.VMEM((34, LANES, LANES), BF16)],
        name="filter_spectrum",
    )(me, fc, fs, row, rounded(forward), rounded(back), *blocks)


def conv_kernel(
    in_ref, h_ref, fc_ref, fs_ref, row_ref, col_ref, f_ref, b_ref, out_ref, cross_ref, spec, turns, firsts,
):
    def pick(g):
        if g:
            parts = [in_ref[:, 128 * i + 16 * g : 128 * i + 16 * g + 16, :] for i in range(2)]
        else:
            edges = in_ref[:, 256:272, :].astype(F32)
            nothing = jnp.zeros((1, 8, LANES), F32)
            filtered = edges[:, 0:8] + jnp.concatenate([nothing, edges[:15, 8:16]], axis=0)
            firsts[...] = filtered
            gated = filtered * pltpu.roll(filtered, 6, 1)
            heads = (gated, pltpu.roll(gated, 4, 1))
            rows = iota((16, 16, LANES), 1)
            parts = []
            for i in range(2):
                head = jnp.concatenate([heads[i], heads[i]], axis=1)
                plain = in_ref[:, 128 * i : 128 * i + 16, :].astype(F32)
                parts.append(jnp.where(rows < 2, head, plain).astype(BF16))
        return jnp.concatenate([part.reshape(256, LANES) for part in parts], axis=1)

    outer_forward(f_ref, pick, spec)

    def step(k):
        value = dot(forward_table(fc_ref, fs_ref, row_ref, k), pair_of(spec, k))
        xr, xi = value[:LANES, :LANES], value[LANES:, :LANES]
        gr, gi = value[:LANES, LANES:], value[LANES:, LANES:]
        h = h_ref[k].astype(F32)
        hr, hi = h[:LANES], h[LANES:]
        cross = jnp.concatenate([xr * gr + xi * gi, xr * gi - xi * gr], axis=0)
        cross_ref[k] = cross.astype(BF16)
        real = jnp.concatenate([hr * xr - hi * xi, hr * gr + hi * gi], axis=1)
        imag = jnp.concatenate([hr * xi + hi * xr, hr * gi - hi * gr], axis=1)
        mixed = jnp.concatenate([real, imag], axis=0).astype(BF16)
        put_pair(turns, k, dot(back_table(fc_ref, fs_ref, col_ref, k), mixed))

    inner_loop(step)
    for g in range(8):
        last = outer_back(b_ref, turns, g)
        parts = [last[:, i * LANES : (i + 1) * LANES].reshape(16, 16, LANES) for i in range(2)]
        for i in range(2):
            out_ref[:, 128 * i + 16 * g : 128 * i + 16 * g + 16, :] = parts[i].astype(BF16)
        if g == 0:
            own = firsts[...]
            nothing = jnp.zeros((1, 8, LANES), F32)
            conv, grad, following = (
                jnp.concatenate([part[1:, 0:8], nothing], axis=0) for part in (*parts, own)
            )
            row = iota((16, 8, LANES), 1)
            following = jnp.where((row == 4) | (row == 5), pltpu.roll(conv, 4, 1), following)
            own = jnp.where(row >= 6, pltpu.roll(grad, 6, 1), own)
            out_ref[:, 256:272, :] = jnp.concatenate([following, own], axis=1).astype(BF16)


def conv_both(columns, spectrum, constants):
    h, forward, back = spectrum
    return pl.pallas_call(
        conv_kernel,
        in_specs=[VMEM_SPEC] * 8,
        out_specs=[VMEM_SPEC] * 2,
        out_shape=[
            jax.ShapeDtypeStruct((16, 272, LANES), BF16),
            jax.ShapeDtypeStruct((17, 2 * LANES, LANES), BF16),
        ],
        scratch_shapes=[pltpu.VMEM((34, LANES, 2 * LANES), BF16) for _ in range(2)]
        + [pltpu.VMEM((16, 8, LANES), F32)],
        name="conv_both",
    )(columns, h, *constants, forward, back)


def reversed_bits(j):
    return ((j & 1) << 3) | ((j & 2) << 1) | ((j & 4) >> 1) | ((j & 8) >> 3)


def filter_grad_kernel(ids_ref, cross_ref, fc_ref, fs_ref, col_ref, bh_ref, out_ref, turns):
    def step(k):
        put_pair(turns, k, dot(back_table(fc_ref, fs_ref, col_ref, k), cross_ref[k]))

    inner_loop(step)
    for g in range(8):
        part = outer_back(bh_ref, turns, g).reshape(16, 16, LANES)
        for e in range(2):
            place = reversed_bits((2 * g + e) ^ ids_ref[0])
            for p in range(16):
                out_ref[place, p ^ ids_ref[1]] = part[p, 8 * e : 8 * e + 8].astype(BF16)


def filter_grad(ids, cross, constants, back):
    fc, fs, _, col = constants
    return pl.pallas_call(
        filter_grad_kernel,
        in_specs=[SMEM] + [VMEM_SPEC] * 5,
        out_specs=VMEM_SPEC,
        out_shape=jax.ShapeDtypeStruct((16, 16, 8, LANES), BF16),
        scratch_shapes=[pltpu.VMEM((34, LANES, LANES), BF16)],
        name="filter_grad",
    )(ids, cross, fc, fs, col, back)


def hats_kernel(k_ref, v_ref, take_ref, ids_ref, w_ref, key_ref, value_ref, xs):
    m1, m2 = (mask[0:128] for mask in masks_of(ids_ref))
    take = take_ref[...]
    for s, ref in enumerate((k_ref, v_ref)):
        xs[s, 0:8, :] = jnp.zeros((8, CHUNK), F32)
        xs[s, 8:136, :] = dot(take, ref[...])

    def part(h, carry):
        at = pl.ds(pl.multiple_of(h * LANES, LANES), LANES)
        for s, out_ref in enumerate((key_ref, value_ref)):
            w = w_ref[:, s, at]
            out_ref[:, at] = (
                w[0:1] * xs[s, 8:136, at] + w[1:2] * (xs[s, 7:135, at] * m1) + w[2:3] * (xs[s, 6:134, at] * m2)
            )
        return carry

    lax.fori_loop(0, CHUNK // LANES, part, 0)


def make_hats(received, take, ids, weights):
    channels = weights.shape[2]
    chunks = channels // CHUNK
    return pl.pallas_call(
        hats_kernel,
        grid=(chunks,),
        in_specs=stream_specs(256, chunks)[:2] + [whole(128, 256), whole(144, 1), WEIGHTS],
        out_specs=[column_spec(128)] * 2,
        out_shape=[jax.ShapeDtypeStruct((128, channels), F32)] * 2,
        scratch_shapes=[pltpu.VMEM((2, 136, CHUNK), F32)],
        name="make_hats",
    )(received, received, take, ids, weights)


def edges_of(conv_ref, h):
    edges = conv_ref[h, 256:272, :].astype(F32)
    return edges[0:8], edges[8:16]


def patched(ref, at, own, shift):
    own = pltpu.roll(own, shift, 0) if shift else own
    head = jnp.where(iota((8, LANES), 0) < 2, own, ref[0:8, at])
    return head, ref[8:128, at]


def back_kernel(key_ref, value_ref, give_ref, ids_ref, w_ref, cot_ref, conv_ref, back_ref, one, two):
    give = give_ref[...]
    m1, m2 = masks_of(ids_ref)

    for h in range(CHUNK // LANES):
        at = slice(h * LANES, (h + 1) * LANES)
        following, own = edges_of(conv_ref, h)
        conv = jnp.concatenate([conv_ref[h, 0:128, :].astype(F32), pltpu.roll(following, 4, 0)], axis=0)
        grad_product = jnp.concatenate([conv_ref[h, 128:256, :].astype(F32), pltpu.roll(own, 2, 0)], axis=0)
        cot = jnp.concatenate([cot_ref[:, at].astype(F32), pltpu.roll(following, 2, 0)], axis=0)
        key = jnp.concatenate([*patched(key_ref, at, own, 0), following], axis=0)
        value = jnp.concatenate([*patched(value_ref, at, own, 6), pltpu.roll(following, 6, 0)], axis=0)
        grads = (grad_product * value, grad_product * key, cot * conv)
        for s in range(3):
            w = w_ref[:, s, at]
            grad = grads[s]
            one[s] = grad * m1
            two[s] = grad * m2
            rows = w[0:1] * grad[0:128] + w[1:2] * one[s, 1:129] + w[2:3] * two[s, 2:130]
            sent = dot(give, rows.astype(BF16)).astype(BF16)
            back_ref[:, 16 * s : 16 * s + 16, at] = sent.reshape(16, 16, LANES)


def back_rows(hats, give, ids, weights, cot, local):
    channels = cot.shape[1]
    chunks = channels // CHUNK
    per = CHUNK // LANES
    return pl.pallas_call(
        back_kernel,
        grid=(chunks,),
        in_specs=[
            column_spec(128),
            column_spec(128),
            whole(256, 128),
            whole(144, 1),
            WEIGHTS,
            column_spec(128),
            pl.BlockSpec((per, 272, LANES), lambda c: (c, 0, 0)),
        ],
        out_specs=pl.BlockSpec((16, 48, CHUNK), lambda c: (0, 0, c)),
        out_shape=jax.ShapeDtypeStruct((16, 48, channels), BF16),
        scratch_shapes=[pltpu.VMEM((3, 136, LANES), F32) for _ in range(2)],
        name="back_rows",
    )(*hats, give, ids, weights, cot, local)


def sums_kernel(
    k_ref, v_ref, q_ref, take_ref, pk_ref, pv_ref, pq_ref, key_ref, value_ref, ids_ref, w_ref, cot_ref, conv_ref,
    mixed_ref, taps_ref, xs,
):
    take = take_ref[...]
    m1, m2 = (mask[0:128] for mask in masks_of(ids_ref))
    for s, (ref, prev) in enumerate(((k_ref, pk_ref), (v_ref, pv_ref), (q_ref, pq_ref))):
        xs[s, 6:8, :] = prev[...].astype(F32)
        xs[s, 8:136, :] = dot(take, ref[...])

    def part(h, carry):
        at = pl.ds(pl.multiple_of(h * LANES, LANES), LANES)
        conv = conv_ref[h, 0:128, :].astype(F32)
        grad_product = conv_ref[h, 128:256, :].astype(F32)
        cot = cot_ref[:, at].astype(F32)
        own = edges_of(conv_ref, h)[1]
        key = jnp.concatenate(patched(key_ref, at, own, 0), axis=0)
        value = jnp.concatenate(patched(value_ref, at, own, 6), axis=0)
        grads = (grad_product * value, grad_product * key, cot * conv)
        for s in range(3):
            parts = (xs[s, 8:136, at], xs[s, 7:135, at] * m1, xs[s, 6:134, at] * m2)
            for k in range(3):
                total = jnp.sum(grads[s] * parts[k], axis=0, keepdims=True)
                taps_ref[3 * s + k, pl.ds((CHUNK // LANES) * pl.program_id(0) + h, 1), :] = total
            if s == 2:
                w = w_ref[:, s, at]
                query = w[0:1] * parts[0] + w[1:2] * parts[1] + w[2:3] * parts[2]
                mixed_ref[:, at] = (query * conv).astype(BF16)
        return carry

    lax.fori_loop(0, CHUNK // LANES, part, 0)


def mixed_and_sums(received, take, prev, hats, ids, weights, cot, local):
    channels = cot.shape[1]
    chunks = channels // CHUNK
    per = CHUNK // LANES
    return pl.pallas_call(
        sums_kernel,
        grid=(chunks,),
        in_specs=stream_specs(256, chunks)
        + [whole(128, 256)]
        + stream_specs(2, chunks)
        + [
            column_spec(128),
            column_spec(128),
            whole(144, 1),
            WEIGHTS,
            column_spec(128),
            pl.BlockSpec((per, 272, LANES), lambda c: (c, 0, 0)),
        ],
        out_specs=[column_spec(128), whole(9, 16, LANES)],
        out_shape=[
            jax.ShapeDtypeStruct((128, channels), BF16),
            jax.ShapeDtypeStruct((9, 16, LANES), F32),
        ],
        scratch_shapes=[pltpu.VMEM((3, 136, CHUNK), F32)],
        name="mixed_and_sums",
    )(received, received, received, take, prev, prev, prev, *hats, ids, weights, cot, local)


def store_kernel(select_ref, in_ref, out_ref):
    width = in_ref.shape[2]
    out_ref[...] = dot_t(select_ref[...], in_ref[...].reshape(256, width)).astype(BF16)


def store_grads(select, returned, channels):
    width = 1024
    chunks = channels // width
    return pl.pallas_call(
        store_kernel,
        grid=(3, chunks),
        in_specs=[
            whole(256, 128),
            pl.BlockSpec((16, 16, width), lambda s, c: (0, s, c)),
        ],
        out_specs=pl.BlockSpec((128, width), lambda s, c: (0, s * chunks + c)),
        out_shape=jax.ShapeDtypeStruct((128, 3 * channels), BF16),
        name="store_grads",
    )(select, returned)


def final_kernel(me_ref, in_ref, grad_ref, taps_ref, total):
    for j in range(16):
        at = pl.multiple_of((j ^ me_ref[0]) * LANES, LANES)
        grad_ref[:, pl.ds(at, LANES)] = in_ref[:, 8 * j : 8 * j + 8, :].astype(F32).reshape(128, LANES)
    total[...] = jnp.sum(in_ref[:, 128:272, :].astype(F32), axis=0).reshape(9, 16, LANES)
    for i in range(3):
        for c in range(16):
            taps_ref[i, :, c * LANES : (c + 1) * LANES] = total[3 * i : 3 * i + 3, c, :]


def final_parts(me, final):
    return pl.pallas_call(
        final_kernel,
        in_specs=[SMEM, VMEM_SPEC],
        out_specs=[VMEM_SPEC] * 2,
        out_shape=[jax.ShapeDtypeStruct((128, 2048), F32), jax.ShapeDtypeStruct((3, 3, 2048), F32)],
        scratch_shapes=[pltpu.VMEM((9, 16, LANES), F32)],
        name="final_parts",
    )(me, final)


def across(value, axis, bit):
    return lax.ppermute(value, axis, [(i, i ^ bit) for i in range(lax.axis_size(axis))])


def halving_sum(value):
    total = value.astype(F32)
    for bit in (1, 2, 4, 8):
        half = total.shape[0] // 2
        total = total[:half] + across(total[half:].astype(BF16), "dp", bit).astype(F32)
    return total[0]


def cube_exchange(value, axis):
    shape = value.shape
    for bit in (1, 2, 4, 8):
        grouped = value.reshape(shape[0] // (2 * bit), 2, bit, *shape[1:])
        other = across(grouped[:, 1], axis, bit)
        value = jnp.stack([grouped[:, 0], other], axis=1).reshape(shape)
    return value


def total_over(value, axis):
    for bit in (1, 2, 4, 8):
        value = value + across(value, axis, bit)
    return value


def shards(stored, source_row, source_span, segments, short_weight, filter_taps, cotangent):
    dp_count = lax.axis_size("dp")
    my_dp = lax.axis_index("dp").astype(jnp.int32)
    my_seq = lax.axis_index("seq").astype(jnp.int32)
    tok_rows = stored.shape[1]
    width = stored.shape[2]
    channels = width // 3
    span_count = source_span.shape[1]
    span_rows = tok_rows // span_count
    sources = source_row[:, :, 0]
    dp_id, seq_id = my_dp[None], my_seq[None]

    sent, select, take, place = pack_rows(dp_id, sources, source_span, stored[0])
    received = exchange(sent.reshape(dp_count, MOST * span_rows, width), "dp")
    received = received.reshape(dp_count * MOST * span_rows, width)

    near = filter_blocks(seq_id, filter_taps)
    near = [near[0]] + [across(near[r], "seq", r) for r in range(1, 4)]
    far = [across(jnp.stack([part[h] for part in near]), "seq", 4 * h) for h in range(1, 4)]

    ids = segments[0] + 1
    outside = jnp.full((6,), -1, jnp.int32)
    ids = jnp.concatenate([outside, shifted(ids[-2:], "seq", 1), ids, shifted(ids[:2], "seq", -1), outside])
    ids = ids.astype(F32)[:, None]
    cot = cotangent[0]
    weights = jnp.transpose(short_weight, (1, 0, 2))
    received, near, far, ids, weights = lax.optimization_barrier((received, near, far, ids, weights))

    columns = exchange(gather_rows(received, take, ids, weights, cot), "seq")
    constants = dft_constants()
    spectrum = filter_spectrum(seq_id, constants, near + far)
    hats = make_hats(received, take, ids, weights)
    give = jnp.transpose(take)
    columns, spectrum, hats, give = lax.optimization_barrier((columns, spectrum, hats, give))
    last = lax.dynamic_slice(received, (place[-1, 0], 0), (span_rows, width))[-2:]
    prev = shifted(last, "seq", 1)

    results, cross = conv_both(columns, spectrum, constants)
    local = exchange(results, "seq")
    lags = halving_sum(filter_grad(jnp.stack([my_dp, my_seq]), cross, constants, spectrum[2]))

    back = back_rows(hats, give, ids, weights, cot, local)
    back, local, lags, prev = lax.optimization_barrier((back, local, lags, prev))
    returned = exchange(back, "dp")
    mixed, taps = mixed_and_sums(received, take, prev, hats, ids, weights, cot, local)
    lags = cube_exchange(lags.astype(BF16), "seq")
    taps = total_over(taps, "seq")
    final = jnp.concatenate([lags.reshape(128, LANES), taps.astype(BF16).reshape(144, LANES)], axis=0)
    final = jnp.broadcast_to(final[None], (dp_count, *final.shape))
    returned, final = lax.optimization_barrier((returned, final))
    final = exchange(final, "dp")
    grad_stored = store_grads(select, returned, channels)
    grad_filter, grad_short = final_parts(seq_id, final)
    return (mixed[None], grad_stored[None], grad_filter, grad_short)


def solution(mesh):
    return jax.shard_map(
        shards,
        mesh=mesh,
        in_specs=(
            P("dp", "seq", None),
            P(None, "seq", None),
            P(None, "seq"),
            P("dp", "seq"),
            P(),
            P("seq", None),
            P("dp", "seq", None),
        ),
        out_specs=(P("dp", "seq", None), P("dp", "seq", None), P("seq", None), P()),
        check_vma=False,
    )
```

```python
import functools
import math

import jax
import jax.numpy as jnp
import numpy as np
from jax import lax
from jax.experimental import pallas as pl
from jax.experimental.pallas import tpu as pltpu
from jax.sharding import PartitionSpec as P

MOST = 2
CHUNK = 512
LANES = 128
F32 = jnp.float32
BF16 = jnp.bfloat16


def shifted(value, axis, by):
    length = lax.axis_size(axis)
    pairs = [(i, i + by) for i in range(length) if 0 <= i + by < length]
    return lax.ppermute(value, axis, pairs)


def exchange(value, axis):
    return lax.all_to_all(value, axis, 0, 0, tiled=True)


def dot(left, right):
    return jnp.dot(left, right, preferred_element_type=F32)


def dot_t(left, right):
    return lax.dot_general(left, right, (((0,), (0,)), ((), ())), preferred_element_type=F32)


def iota(shape, axis):
    return lax.broadcasted_iota(jnp.int32, shape, axis)


def whole(*shape):
    return pl.BlockSpec(shape, lambda *ids: (0,) * len(shape))


SMEM = pl.BlockSpec(memory_space=pltpu.SMEM)


def outer_tables():
    blocks = np.arange(16)
    forward = [np.ones(16), np.cos(np.pi * blocks)]
    back = [np.ones(16), np.cos(np.pi * blocks)]
    for k in range(1, 16):
        angle = 2.0 * np.pi * k * blocks / 32.0
        forward += [np.cos(angle), -np.sin(angle)]
        back += [2.0 * np.cos(angle), -2.0 * np.sin(angle)]
    return np.stack(forward), np.stack(back, axis=1) / 4096.0


def spread_in(table, by):
    rows, cols = table.shape
    tall = (iota((rows * by, rows), 0) // by == iota((rows * by, rows), 1)).astype(BF16)
    wide = (iota((cols, cols * by), 0) == iota((cols, cols * by), 1) // by).astype(BF16)
    value = dot(dot(tall, table).astype(BF16), wide)
    shape = (rows * by, cols * by)
    diagonal = iota(shape, 0) % by == iota(shape, 1) % by
    return jnp.where(diagonal, value, 0.0).astype(BF16)


def dft_constants():
    inner = np.arange(LANES)
    turn = 2.0 * np.pi * (inner[:, None] * inner[None, :] % LANES) / LANES
    order = np.asarray([0, 16] + list(range(1, 16)))
    twist = 2.0 * np.pi * order[:, None] * inner[None, :] / 4096.0
    values = (
        np.cos(turn),
        np.sin(turn),
        np.stack([np.cos(twist), np.sin(twist)], axis=1),
        np.stack([np.cos(twist), np.sin(twist)], axis=2),
    )
    return tuple(jnp.asarray(value, F32) for value in values)


def turned(fc_ref, fs_ref, wc, ws):
    fc = fc_ref[...]
    fs = fs_ref[...]
    return fc * wc - fs * ws, fs * wc + fc * ws


def forward_table(fc_ref, fs_ref, row_ref, k):
    row = row_ref[k]
    cos, sin = turned(fc_ref, fs_ref, row[0:1, :], row[1:2, :])
    cos, sin, minus = cos.astype(BF16), sin.astype(BF16), (-sin).astype(BF16)
    return jnp.concatenate(
        [jnp.concatenate([cos, sin], axis=1), jnp.concatenate([minus, cos], axis=1)], axis=0
    )


def back_table(fc_ref, fs_ref, col_ref, k):
    col = col_ref[k]
    cos, sin = turned(fc_ref, fs_ref, col[:, 0:1], col[:, 1:2])
    cos, sin, minus = cos.astype(BF16), sin.astype(BF16), (-sin).astype(BF16)
    return jnp.concatenate(
        [jnp.concatenate([cos, minus], axis=1), jnp.concatenate([sin, cos], axis=1)], axis=0
    )


def pack_kernel(me_ref, source_ref, span_ref, stored_ref, out_ref, select_ref, take_ref, place_ref):
    @pl.when(pl.program_id(0) == 0)
    def _():
        mine = (source_ref[...] == me_ref[0]).astype(F32)
        before = (iota((16, 16), 0) < iota((16, 16), 1)).astype(F32)
        earlier = dot(mine, before)
        tall = (iota((256, 16), 0) // 16 == iota((256, 16), 1)).astype(F32)
        row = iota((256, 16), 0)
        hit = dot(tall, mine) * (dot(tall, earlier) == (row // 8 % 2).astype(F32)).astype(F32)
        start = jnp.sum(hit * (dot(tall, span_ref[...].astype(F32)) * 8.0 + 1.0), axis=1, keepdims=True)
        target = jnp.where(start > 0.5, start - 1.0 + (iota((256, 1), 0) % 8).astype(F32), -1.0)
        select_ref[...] = (iota((256, 128), 1).astype(F32) == target).astype(F32).astype(BF16)

    @pl.when(pl.program_id(0) == pl.num_programs(0) - 1)
    def _():
        sources = source_ref[...].astype(F32)
        row = iota((16, 16), 0)
        col = iota((16, 16), 1)
        ours = jnp.sum(jnp.where(row == me_ref[0], sources, 0.0), axis=0, keepdims=True)
        ours_down = jnp.sum(jnp.where(row == col, ours, 0.0), axis=1, keepdims=True)
        order = jnp.sum(((ours_down == ours) & (col < row)).astype(F32), axis=1, keepdims=True)
        place = (ours_down * MOST + order) * 8.0
        place_ref[...] = place.astype(jnp.int32)
        place_across = jnp.sum(jnp.where(row == col, place, 0.0), axis=0, keepdims=True)
        mine = iota((128, 16), 0) // 8 == iota((128, 16), 1)
        target = jnp.sum(jnp.where(mine, place_across, 0.0), axis=1, keepdims=True)
        target = target + (iota((128, 1), 0) % 8).astype(F32)
        take_ref[...] = (iota((128, 256), 1).astype(F32) == target).astype(F32).astype(BF16)

    out_ref[...] = dot(select_ref[...], stored_ref[...]).astype(BF16)


def pack_rows(me, sources, spans, stored):
    width = 1024
    return pl.pallas_call(
        pack_kernel,
        grid=(stored.shape[1] // width,),
        in_specs=[
            SMEM,
            whole(16, 16),
            whole(16, 16),
            pl.BlockSpec((128, width), lambda c: (0, c)),
        ],
        out_specs=[
            pl.BlockSpec((256, width), lambda c: (0, c)),
            whole(256, 128),
            whole(128, 256),
            whole(16, 1),
        ],
        out_shape=[
            jax.ShapeDtypeStruct((256, stored.shape[1]), BF16),
            jax.ShapeDtypeStruct((256, 128), BF16),
            jax.ShapeDtypeStruct((128, 256), BF16),
            jax.ShapeDtypeStruct((16, 1), jnp.int32),
        ],
        name="pack_rows",
    )(me, sources, spans, stored)


def filter_blocks_kernel(me_ref, taps_ref, *out_refs):
    for r, out_ref in enumerate(out_refs):
        for h in range(4):
            at = pl.multiple_of((me_ref[0] ^ (r | 4 * h)) * LANES, LANES)
            out_ref[h] = taps_ref[:, pl.ds(at, LANES)].astype(BF16)


def filter_blocks(me, filter_taps):
    return pl.pallas_call(
        filter_blocks_kernel,
        in_specs=[SMEM, pl.BlockSpec(memory_space=pltpu.VMEM)],
        out_specs=[pl.BlockSpec(memory_space=pltpu.VMEM)] * 4,
        out_shape=[jax.ShapeDtypeStruct((4, 128, LANES), BF16)] * 4,
        name="filter_blocks",
    )(me, filter_taps)


def masks_of(ids_ref):
    here = ids_ref[8:144, :]
    return (ids_ref[7:143, :] == here).astype(F32), (ids_ref[6:142, :] == here).astype(F32)


def gather_kernel(k_ref, v_ref, q_ref, take_ref, ids_ref, w_ref, cot_ref, out_ref, xs, edge):
    take = take_ref[...]
    m1, m2 = masks_of(ids_ref)
    for s, ref in enumerate((k_ref, v_ref, q_ref)):
        xs[s, 0:8, :] = jnp.zeros((8, CHUNK), F32)
        xs[s, 8:136, :] = dot(take, ref[...])
        xs[s, 136:144, :] = jnp.zeros((8, CHUNK), F32)

    for h in range(CHUNK // LANES):
        at = slice(h * LANES, (h + 1) * LANES)
        hats = []
        for s in range(3):
            w = w_ref[:, s, at]
            hats.append(
                w[0:1] * xs[s, 8:144, at]
                + w[1:2] * (xs[s, 7:143, at] * m1)
                + w[2:3] * (xs[s, 6:142, at] * m2)
            )
            edge[2 * s : 2 * s + 2, :] = hats[s][0:2]
            edge[2 * s + 8 : 2 * s + 10, :] = hats[s][128:130]
        cot = cot_ref[:, at].astype(F32)
        edge[6:8, :] = cot[0:2]
        edge[14:16, :] = jnp.zeros((2, LANES), F32)
        out_ref[h, 0:128, :] = (hats[0] * hats[1])[0:128].astype(BF16)
        out_ref[h, 128:256, :] = (cot * hats[2][0:128]).astype(BF16)
        out_ref[h, 256:272, :] = edge[...].astype(BF16)


def stream_specs(rows, chunks):
    return [pl.BlockSpec((rows, CHUNK), lambda c, s=s: (0, s * chunks + c)) for s in range(3)]


def column_spec(rows):
    return pl.BlockSpec((rows, CHUNK), lambda c: (0, c))


WEIGHTS = pl.BlockSpec((3, 3, CHUNK), lambda c: (0, 0, c))


def gather_rows(received, take, ids, weights, cot):
    chunks = cot.shape[1] // CHUNK
    per = CHUNK // LANES
    return pl.pallas_call(
        gather_kernel,
        grid=(chunks,),
        in_specs=stream_specs(256, chunks)
        + [whole(128, 256), whole(144, 1), WEIGHTS, column_spec(128)],
        out_specs=pl.BlockSpec((per, 272, LANES), lambda c: (c, 0, 0)),
        out_shape=jax.ShapeDtypeStruct((chunks * per, 272, LANES), BF16),
        scratch_shapes=[pltpu.VMEM((3, 144, CHUNK), F32), pltpu.VMEM((16, LANES), F32)],
        name="gather_rows",
    )(received, received, received, take, ids, weights, cot)


def outer_forward(fh_ref, pick, spec):
    nothing = jnp.zeros(spec.shape[1:], BF16)
    for where in (1, 3):
        spec[where] = nothing
    for g in range(8):
        at = slice(16 * g, 16 * g + 16)
        data = pick(g)
        value = dot(fh_ref[...], data).astype(BF16)
        spec[0, at, :] = value[0:16]
        spec[2, at, :] = value[16:32]
        spec[4:34, at, :] = value[32:512].reshape(30, 16, value.shape[1])


def outer_back(bh_ref, turns, g):
    at = slice(16 * g, 16 * g + 16)
    rest = turns[4:34, at, :].reshape(480, turns.shape[2])
    return dot(bh_ref[...], jnp.concatenate([turns[0, at, :], turns[2, at, :], rest], axis=0))


def pair_of(ref, k):
    return ref[pl.ds(2 * k, 2)].reshape(2 * LANES, ref.shape[2])


def put_pair(ref, k, value):
    ref[pl.ds(2 * k, 2)] = value.astype(BF16).reshape(2, LANES, ref.shape[2])


VMEM_SPEC = pl.BlockSpec(memory_space=pltpu.VMEM)


def inner_loop(step):
    def four(i, carry):
        for j in range(4):
            step(4 * i + j)
        return carry

    lax.fori_loop(0, 4, four, 0)
    step(16)


def filter_kernel(me_ref, fc_ref, fs_ref, row_ref, of_ref, ob_ref, *rest):
    blocks, (out_ref, f_ref, b_ref, ordered, spec) = rest[:7], rest[7:]
    f_ref[...] = spread_in(of_ref[...], 16)
    b_ref[...] = spread_in(ob_ref[...], 16)
    for r in range(4):
        ordered[me_ref[0] ^ r] = blocks[r][0]
        for h in range(1, 4):
            ordered[me_ref[0] ^ (r | 4 * h)] = blocks[3 + h][r]
    outer_forward(f_ref, lambda g: ordered[:, 16 * g : 16 * g + 16, :].reshape(256, LANES), spec)

    def step(k, carry):
        out_ref[k] = dot(forward_table(fc_ref, fs_ref, row_ref, k), pair_of(spec, k)).astype(BF16)
        return carry

    lax.fori_loop(0, 17, step, 0)


def rounded(table):
    return jnp.asarray(np.asarray(table, np.float32).astype(jnp.bfloat16))


def filter_spectrum(me, constants, blocks):
    fc, fs, row, _ = constants
    forward, back = outer_tables()
    return pl.pallas_call(
        filter_kernel,
        in_specs=[SMEM] + [VMEM_SPEC] * 12,
        out_specs=[VMEM_SPEC] * 3,
        out_shape=[
            jax.ShapeDtypeStruct((17, 2 * LANES, LANES), BF16),
            jax.ShapeDtypeStruct((512, 256), BF16),
            jax.ShapeDtypeStruct((256, 512), BF16),
        ],
        scratch_shapes=[pltpu.VMEM((16, 128, LANES), BF16), pltpu.VMEM((34, LANES, LANES), BF16)],
        name="filter_spectrum",
    )(me, fc, fs, row, rounded(forward), rounded(back), *blocks)


def conv_kernel(
    in_ref, h_ref, fc_ref, fs_ref, row_ref, col_ref, f_ref, b_ref, out_ref, cross_ref, spec, turns, firsts,
):
    def pick(g):
        if g:
            parts = [in_ref[:, 128 * i + 16 * g : 128 * i + 16 * g + 16, :] for i in range(2)]
        else:
            edges = in_ref[:, 256:272, :].astype(F32)
            nothing = jnp.zeros((1, 8, LANES), F32)
            filtered = edges[:, 0:8] + jnp.concatenate([nothing, edges[:15, 8:16]], axis=0)
            firsts[...] = filtered
            gated = filtered * pltpu.roll(filtered, 6, 1)
            heads = (gated, pltpu.roll(gated, 4, 1))
            rows = iota((16, 16, LANES), 1)
            parts = []
            for i in range(2):
                head = jnp.concatenate([heads[i], heads[i]], axis=1)
                plain = in_ref[:, 128 * i : 128 * i + 16, :].astype(F32)
                parts.append(jnp.where(rows < 2, head, plain).astype(BF16))
        return jnp.concatenate([part.reshape(256, LANES) for part in parts], axis=1)

    outer_forward(f_ref, pick, spec)

    def step(k):
        value = dot(forward_table(fc_ref, fs_ref, row_ref, k), pair_of(spec, k))
        xr, xi = value[:LANES, :LANES], value[LANES:, :LANES]
        gr, gi = value[:LANES, LANES:], value[LANES:, LANES:]
        h = h_ref[k].astype(F32)
        hr, hi = h[:LANES], h[LANES:]
        cross = jnp.concatenate([xr * gr + xi * gi, xr * gi - xi * gr], axis=0)
        cross_ref[k] = cross.astype(BF16)
        real = jnp.concatenate([hr * xr - hi * xi, hr * gr + hi * gi], axis=1)
        imag = jnp.concatenate([hr * xi + hi * xr, hr * gi - hi * gr], axis=1)
        mixed = jnp.concatenate([real, imag], axis=0).astype(BF16)
        put_pair(turns, k, dot(back_table(fc_ref, fs_ref, col_ref, k), mixed))

    inner_loop(step)
    for g in range(8):
        last = outer_back(b_ref, turns, g)
        parts = [last[:, i * LANES : (i + 1) * LANES].reshape(16, 16, LANES) for i in range(2)]
        for i in range(2):
            out_ref[:, 128 * i + 16 * g : 128 * i + 16 * g + 16, :] = parts[i].astype(BF16)
        if g == 0:
            own = firsts[...]
            nothing = jnp.zeros((1, 8, LANES), F32)
            conv, grad, following = (
                jnp.concatenate([part[1:, 0:8], nothing], axis=0) for part in (*parts, own)
            )
            row = iota((16, 8, LANES), 1)
            following = jnp.where((row == 4) | (row == 5), pltpu.roll(conv, 4, 1), following)
            own = jnp.where(row >= 6, pltpu.roll(grad, 6, 1), own)
            out_ref[:, 256:272, :] = jnp.concatenate([following, own], axis=1).astype(BF16)


def conv_both(columns, spectrum, constants):
    h, forward, back = spectrum
    return pl.pallas_call(
        conv_kernel,
        in_specs=[VMEM_SPEC] * 8,
        out_specs=[VMEM_SPEC] * 2,
        out_shape=[
            jax.ShapeDtypeStruct((16, 272, LANES), BF16),
            jax.ShapeDtypeStruct((17, 2 * LANES, LANES), BF16),
        ],
        scratch_shapes=[pltpu.VMEM((34, LANES, 2 * LANES), BF16) for _ in range(2)]
        + [pltpu.VMEM((16, 8, LANES), F32)],
        name="conv_both",
    )(columns, h, *constants, forward, back)


def reversed_bits(j):
    return ((j & 1) << 3) | ((j & 2) << 1) | ((j & 4) >> 1) | ((j & 8) >> 3)


def filter_grad_kernel(ids_ref, cross_ref, fc_ref, fs_ref, col_ref, bh_ref, out_ref, turns):
    def step(k):
        put_pair(turns, k, dot(back_table(fc_ref, fs_ref, col_ref, k), cross_ref[k]))

    inner_loop(step)
    for g in range(8):
        part = outer_back(bh_ref, turns, g).reshape(16, 16, LANES)
        for e in range(2):
            place = reversed_bits((2 * g + e) ^ ids_ref[0])
            for p in range(16):
                out_ref[place, p ^ ids_ref[1]] = part[p, 8 * e : 8 * e + 8].astype(BF16)


def filter_grad(ids, cross, constants, back):
    fc, fs, _, col = constants
    return pl.pallas_call(
        filter_grad_kernel,
        in_specs=[SMEM] + [VMEM_SPEC] * 5,
        out_specs=VMEM_SPEC,
        out_shape=jax.ShapeDtypeStruct((16, 16, 8, LANES), BF16),
        scratch_shapes=[pltpu.VMEM((34, LANES, LANES), BF16)],
        name="filter_grad",
    )(ids, cross, fc, fs, col, back)


def hats_kernel(k_ref, v_ref, take_ref, ids_ref, w_ref, key_ref, value_ref, xs):
    m1, m2 = (mask[0:128] for mask in masks_of(ids_ref))
    take = take_ref[...]
    for s, ref in enumerate((k_ref, v_ref)):
        xs[s, 0:8, :] = jnp.zeros((8, CHUNK), F32)
        xs[s, 8:136, :] = dot(take, ref[...])

    def part(h, carry):
        at = pl.ds(pl.multiple_of(h * LANES, LANES), LANES)
        for s, out_ref in enumerate((key_ref, value_ref)):
            w = w_ref[:, s, at]
            out_ref[:, at] = (
                w[0:1] * xs[s, 8:136, at] + w[1:2] * (xs[s, 7:135, at] * m1) + w[2:3] * (xs[s, 6:134, at] * m2)
            )
        return carry

    lax.fori_loop(0, CHUNK // LANES, part, 0)


def make_hats(received, take, ids, weights):
    channels = weights.shape[2]
    chunks = channels // CHUNK
    return pl.pallas_call(
        hats_kernel,
        grid=(chunks,),
        in_specs=stream_specs(256, chunks)[:2] + [whole(128, 256), whole(144, 1), WEIGHTS],
        out_specs=[column_spec(128)] * 2,
        out_shape=[jax.ShapeDtypeStruct((128, channels), F32)] * 2,
        scratch_shapes=[pltpu.VMEM((2, 136, CHUNK), F32)],
        name="make_hats",
    )(received, received, take, ids, weights)


def edges_of(conv_ref, h):
    edges = conv_ref[h, 256:272, :].astype(F32)
    return edges[0:8], edges[8:16]


def patched(ref, at, own, shift):
    own = pltpu.roll(own, shift, 0) if shift else own
    head = jnp.where(iota((8, LANES), 0) < 2, own, ref[0:8, at])
    return head, ref[8:128, at]


def back_kernel(key_ref, value_ref, give_ref, ids_ref, w_ref, cot_ref, conv_ref, back_ref, one, two):
    give = give_ref[...]
    m1, m2 = masks_of(ids_ref)

    for h in range(CHUNK // LANES):
        at = slice(h * LANES, (h + 1) * LANES)
        following, own = edges_of(conv_ref, h)
        conv = jnp.concatenate([conv_ref[h, 0:128, :].astype(F32), pltpu.roll(following, 4, 0)], axis=0)
        grad_product = jnp.concatenate([conv_ref[h, 128:256, :].astype(F32), pltpu.roll(own, 2, 0)], axis=0)
        cot = jnp.concatenate([cot_ref[:, at].astype(F32), pltpu.roll(following, 2, 0)], axis=0)
        key = jnp.concatenate([*patched(key_ref, at, own, 0), following], axis=0)
        value = jnp.concatenate([*patched(value_ref, at, own, 6), pltpu.roll(following, 6, 0)], axis=0)
        grads = (grad_product * value, grad_product * key, cot * conv)
        for s in range(3):
            w = w_ref[:, s, at]
            grad = grads[s]
            one[s] = grad * m1
            two[s] = grad * m2
            rows = w[0:1] * grad[0:128] + w[1:2] * one[s, 1:129] + w[2:3] * two[s, 2:130]
            sent = dot(give, rows.astype(BF16)).astype(BF16)
            back_ref[:, 16 * s : 16 * s + 16, at] = sent.reshape(16, 16, LANES)


def back_rows(hats, give, ids, weights, cot, local):
    channels = cot.shape[1]
    chunks = channels // CHUNK
    per = CHUNK // LANES
    return pl.pallas_call(
        back_kernel,
        grid=(chunks,),
        in_specs=[
            column_spec(128),
            column_spec(128),
            whole(256, 128),
            whole(144, 1),
            WEIGHTS,
            column_spec(128),
            pl.BlockSpec((per, 272, LANES), lambda c: (c, 0, 0)),
        ],
        out_specs=pl.BlockSpec((16, 48, CHUNK), lambda c: (0, 0, c)),
        out_shape=jax.ShapeDtypeStruct((16, 48, channels), BF16),
        scratch_shapes=[pltpu.VMEM((3, 136, LANES), F32) for _ in range(2)],
        name="back_rows",
    )(*hats, give, ids, weights, cot, local)


def sums_kernel(
    me_ref, k_ref, v_ref, q_ref, take_ref, pk_ref, pv_ref, pq_ref, key_ref, value_ref, ids_ref, w_ref, cot_ref, conv_ref,
    mixed_ref, taps_ref, xs,
):
    take = take_ref[...]
    m1, m2 = (mask[0:128] for mask in masks_of(ids_ref))
    for s, (ref, prev) in enumerate(((k_ref, pk_ref), (v_ref, pv_ref), (q_ref, pq_ref))):
        xs[s, 6:8, :] = prev[...].astype(F32)
        xs[s, 8:136, :] = dot(take, ref[...])

    def part(h, carry):
        at = pl.ds(pl.multiple_of(h * LANES, LANES), LANES)
        block = (CHUNK // LANES) * pl.program_id(0) + h
        side = (block // 8) ^ (me_ref[0] % 2)
        conv = conv_ref[h, 0:128, :].astype(F32)
        grad_product = conv_ref[h, 128:256, :].astype(F32)
        cot = cot_ref[:, at].astype(F32)
        own = edges_of(conv_ref, h)[1]
        key = jnp.concatenate(patched(key_ref, at, own, 0), axis=0)
        value = jnp.concatenate(patched(value_ref, at, own, 6), axis=0)
        grads = (grad_product * value, grad_product * key, cot * conv)
        for s in range(3):
            parts = (xs[s, 8:136, at], xs[s, 7:135, at] * m1, xs[s, 6:134, at] * m2)
            for k in range(3):
                total = jnp.sum(grads[s] * parts[k], axis=0, keepdims=True)
                taps_ref[side, 3 * s + k, pl.ds(block % 8, 1), :] = total
            if s == 2:
                w = w_ref[:, s, at]
                query = w[0:1] * parts[0] + w[1:2] * parts[1] + w[2:3] * parts[2]
                mixed_ref[:, at] = (query * conv).astype(BF16)
        return carry

    lax.fori_loop(0, CHUNK // LANES, part, 0)


def mixed_and_sums(me, received, take, prev, hats, ids, weights, cot, local):
    channels = cot.shape[1]
    chunks = channels // CHUNK
    per = CHUNK // LANES
    return pl.pallas_call(
        sums_kernel,
        grid=(chunks,),
        in_specs=[SMEM]
        + stream_specs(256, chunks)
        + [whole(128, 256)]
        + stream_specs(2, chunks)
        + [
            column_spec(128),
            column_spec(128),
            whole(144, 1),
            WEIGHTS,
            column_spec(128),
            pl.BlockSpec((per, 272, LANES), lambda c: (c, 0, 0)),
        ],
        out_specs=[column_spec(128), whole(2, 9, 8, LANES)],
        out_shape=[
            jax.ShapeDtypeStruct((128, channels), BF16),
            jax.ShapeDtypeStruct((2, 9, 8, LANES), F32),
        ],
        scratch_shapes=[pltpu.VMEM((3, 136, CHUNK), F32)],
        name="mixed_and_sums",
    )(me, received, received, received, take, prev, prev, prev, *hats, ids, weights, cot, local)


def store_kernel(select_ref, in_ref, out_ref):
    width = in_ref.shape[2]
    out_ref[...] = dot_t(select_ref[...], in_ref[...].reshape(256, width)).astype(BF16)


def store_grads(select, returned, channels):
    width = 1024
    chunks = channels // width
    return pl.pallas_call(
        store_kernel,
        grid=(3, chunks),
        in_specs=[
            whole(256, 128),
            pl.BlockSpec((16, 16, width), lambda s, c: (0, s, c)),
        ],
        out_specs=pl.BlockSpec((128, width), lambda s, c: (0, s * chunks + c)),
        out_shape=jax.ShapeDtypeStruct((128, 3 * channels), BF16),
        name="store_grads",
    )(select, returned)


def final_kernel(me_ref, in_ref, grad_ref, taps_ref, total):
    for j in range(16):
        at = pl.multiple_of((j ^ me_ref[0]) * LANES, LANES)
        grad_ref[:, pl.ds(at, LANES)] = in_ref[:, 8 * j : 8 * j + 8, :].astype(F32).reshape(128, LANES)
    for side in range(2):
        parts = [in_ref[d, 128:200, :].astype(F32) for d in range(side, 16, 2)]
        total[side] = sum(parts[1:], parts[0]).reshape(9, 8, LANES)
    for i in range(3):
        for c in range(16):
            taps_ref[i, :, c * LANES : (c + 1) * LANES] = total[c // 8, 3 * i : 3 * i + 3, c % 8, :]


def final_parts(me, final):
    return pl.pallas_call(
        final_kernel,
        in_specs=[SMEM, VMEM_SPEC],
        out_specs=[VMEM_SPEC] * 2,
        out_shape=[jax.ShapeDtypeStruct((128, 2048), F32), jax.ShapeDtypeStruct((3, 3, 2048), F32)],
        scratch_shapes=[pltpu.VMEM((2, 9, 8, LANES), F32)],
        name="final_parts",
    )(me, final)


def across(value, axis, bit):
    return lax.ppermute(value, axis, [(i, i ^ bit) for i in range(lax.axis_size(axis))])


def halving_sum(value):
    total = value.astype(F32)
    for bit in (1, 2, 4, 8):
        half = total.shape[0] // 2
        total = total[:half] + across(total[half:].astype(BF16), "dp", bit).astype(F32)
    return total[0]


def cube_exchange(value, axis):
    shape = value.shape
    for bit in (1, 2, 4, 8):
        grouped = value.reshape(shape[0] // (2 * bit), 2, bit, *shape[1:])
        other = across(grouped[:, 1], axis, bit)
        value = jnp.stack([grouped[:, 0], other], axis=1).reshape(shape)
    return value


def total_over(value, axis):
    for bit in (1, 2, 4, 8):
        value = value + across(value, axis, bit)
    return value


def shards(stored, source_row, source_span, segments, short_weight, filter_taps, cotangent):
    dp_count = lax.axis_size("dp")
    my_dp = lax.axis_index("dp").astype(jnp.int32)
    my_seq = lax.axis_index("seq").astype(jnp.int32)
    tok_rows = stored.shape[1]
    width = stored.shape[2]
    channels = width // 3
    span_count = source_span.shape[1]
    span_rows = tok_rows // span_count
    sources = source_row[:, :, 0]
    dp_id, seq_id = my_dp[None], my_seq[None]

    sent, select, take, place = pack_rows(dp_id, sources, source_span, stored[0])
    received = exchange(sent.reshape(dp_count, MOST * span_rows, width), "dp")
    received = received.reshape(dp_count * MOST * span_rows, width)

    near = filter_blocks(seq_id, filter_taps)
    near = [near[0]] + [across(near[r], "seq", r) for r in range(1, 4)]
    ids = segments[0] + 1
    outside = jnp.full((6,), -1, jnp.int32)
    ids = jnp.concatenate([outside, shifted(ids[-2:], "seq", 1), ids, shifted(ids[:2], "seq", -1), outside])
    ids = ids.astype(F32)[:, None]
    near, ids = lax.optimization_barrier((near, ids))
    far = [across(jnp.stack([part[h] for part in near]), "seq", 4 * h) for h in range(1, 4)]

    cot = cotangent[0]
    weights = jnp.transpose(short_weight, (1, 0, 2))
    received, near, far, ids, weights = lax.optimization_barrier((received, near, far, ids, weights))

    columns = exchange(gather_rows(received, take, ids, weights, cot), "seq")
    constants = dft_constants()
    spectrum = filter_spectrum(seq_id, constants, near + far)
    hats = make_hats(received, take, ids, weights)
    give = jnp.transpose(take)
    last = lax.dynamic_slice(received, (place[-1, 0], 0), (span_rows, width))[-2:]
    prev = shifted(last, "seq", 1)
    columns, spectrum, hats, give, prev = lax.optimization_barrier((columns, spectrum, hats, give, prev))
    results, cross = conv_both(columns, spectrum, constants)
    local = exchange(results, "seq")
    lags = halving_sum(filter_grad(jnp.stack([my_dp, my_seq]), cross, constants, spectrum[2]))

    back = back_rows(hats, give, ids, weights, cot, local)
    back, local, lags = lax.optimization_barrier((back, local, lags))
    returned = exchange(back, "dp")
    mixed, taps = mixed_and_sums(dp_id, received, take, prev, hats, ids, weights, cot, local)
    lags = cube_exchange(lags.astype(BF16), "seq")
    taps = total_over(taps[0] + across(taps[1], "dp", 1), "seq")
    final = jnp.concatenate([lags.reshape(128, LANES), taps.astype(BF16).reshape(72, LANES)], axis=0)
    final = jnp.broadcast_to(final[None], (dp_count, *final.shape))
    returned, final = lax.optimization_barrier((returned, final))
    final = exchange(final, "dp")
    grad_stored = store_grads(select, returned, channels)
    grad_filter, grad_short = final_parts(seq_id, final)
    return (mixed[None], grad_stored[None], grad_filter, grad_short)


def solution(mesh):
    return jax.shard_map(
        shards,
        mesh=mesh,
        in_specs=(
            P("dp", "seq", None),
            P(None, "seq", None),
            P(None, "seq"),
            P("dp", "seq"),
            P(),
            P("seq", None),
            P("dp", "seq", None),
        ),
        out_specs=(P("dp", "seq", None), P("dp", "seq", None), P("seq", None), P()),
        check_vma=False,
    )
```

```python
import functools
import math

import jax
import jax.numpy as jnp
import numpy as np
from jax import lax
from jax.experimental import pallas as pl
from jax.experimental.pallas import tpu as pltpu
from jax.sharding import PartitionSpec as P

MOST = 2
CHUNK = 512
LANES = 128
F32 = jnp.float32
BF16 = jnp.bfloat16


def shifted(value, axis, by):
    length = lax.axis_size(axis)
    pairs = [(i, i + by) for i in range(length) if 0 <= i + by < length]
    return lax.ppermute(value, axis, pairs)


def exchange(value, axis):
    return lax.all_to_all(value, axis, 0, 0, tiled=True)


def dot(left, right):
    return jnp.dot(left, right, preferred_element_type=F32)


def dot_t(left, right):
    return lax.dot_general(left, right, (((0,), (0,)), ((), ())), preferred_element_type=F32)


def iota(shape, axis):
    return lax.broadcasted_iota(jnp.int32, shape, axis)


def whole(*shape):
    return pl.BlockSpec(shape, lambda *ids: (0,) * len(shape))


SMEM = pl.BlockSpec(memory_space=pltpu.SMEM)


def outer_tables():
    blocks = np.arange(16)
    forward = [np.ones(16), np.cos(np.pi * blocks)]
    back = [np.ones(16), np.cos(np.pi * blocks)]
    for k in range(1, 16):
        angle = 2.0 * np.pi * k * blocks / 32.0
        forward += [np.cos(angle), -np.sin(angle)]
        back += [2.0 * np.cos(angle), -2.0 * np.sin(angle)]
    return np.stack(forward), np.stack(back, axis=1) / 4096.0


def spread_in(table, by):
    rows, cols = table.shape
    tall = (iota((rows * by, rows), 0) // by == iota((rows * by, rows), 1)).astype(BF16)
    wide = (iota((cols, cols * by), 0) == iota((cols, cols * by), 1) // by).astype(BF16)
    value = dot(dot(tall, table).astype(BF16), wide)
    shape = (rows * by, cols * by)
    diagonal = iota(shape, 0) % by == iota(shape, 1) % by
    return jnp.where(diagonal, value, 0.0).astype(BF16)


def dft_constants():
    inner = np.arange(LANES)
    turn = 2.0 * np.pi * (inner[:, None] * inner[None, :] % LANES) / LANES
    order = np.asarray([0, 16] + list(range(1, 16)))
    twist = 2.0 * np.pi * order[:, None] * inner[None, :] / 4096.0
    values = (
        np.cos(turn),
        np.sin(turn),
        np.stack([np.cos(twist), np.sin(twist)], axis=1),
        np.stack([np.cos(twist), np.sin(twist)], axis=2),
    )
    return tuple(jnp.asarray(value, F32) for value in values)


def turned(fc_ref, fs_ref, wc, ws):
    fc = fc_ref[...]
    fs = fs_ref[...]
    return fc * wc - fs * ws, fs * wc + fc * ws


def forward_table(fc_ref, fs_ref, row_ref, k):
    row = row_ref[k]
    cos, sin = turned(fc_ref, fs_ref, row[0:1, :], row[1:2, :])
    cos, sin, minus = cos.astype(BF16), sin.astype(BF16), (-sin).astype(BF16)
    return jnp.concatenate(
        [jnp.concatenate([cos, sin], axis=1), jnp.concatenate([minus, cos], axis=1)], axis=0
    )


def back_table(fc_ref, fs_ref, col_ref, k):
    col = col_ref[k]
    cos, sin = turned(fc_ref, fs_ref, col[:, 0:1], col[:, 1:2])
    cos, sin, minus = cos.astype(BF16), sin.astype(BF16), (-sin).astype(BF16)
    return jnp.concatenate(
        [jnp.concatenate([cos, minus], axis=1), jnp.concatenate([sin, cos], axis=1)], axis=0
    )


def route_kernel(me_ref, source_ref, span_ref, select_ref, take_ref, place_ref):
    sources = source_ref[...].astype(F32)
    mine = (source_ref[...] == me_ref[0]).astype(F32)
    before = (iota((16, 16), 0) < iota((16, 16), 1)).astype(F32)
    earlier = dot(mine, before)
    tall = (iota((256, 16), 0) // 16 == iota((256, 16), 1)).astype(F32)
    slot = iota((256, 16), 0) // 8 % 2
    hit = dot(tall, mine) * (dot(tall, earlier) == slot.astype(F32)).astype(F32)
    start = jnp.sum(hit * (dot(tall, span_ref[...].astype(F32)) * 8.0 + 1.0), axis=1, keepdims=True)
    target = jnp.where(start > 0.5, start - 1.0 + (iota((256, 1), 0) % 8).astype(F32), -1.0)
    select_ref[...] = (iota((256, 128), 1).astype(F32) == target).astype(F32).astype(BF16)

    row = iota((16, 16), 0)
    col = iota((16, 16), 1)
    ours = jnp.sum(jnp.where(row == me_ref[0], sources, 0.0), axis=0, keepdims=True)
    ours_down = jnp.sum(jnp.where(row == col, ours, 0.0), axis=1, keepdims=True)
    order = jnp.sum(((ours_down == ours) & (col < row)).astype(F32), axis=1, keepdims=True)
    place = (ours_down * MOST + order) * 8.0
    place_ref[...] = place.astype(jnp.int32)
    place_across = jnp.sum(jnp.where(row == col, place, 0.0), axis=0, keepdims=True)
    slots = iota((128, 16), 0) // 8 == iota((128, 16), 1)
    target = jnp.sum(jnp.where(slots, place_across, 0.0), axis=1, keepdims=True)
    target = target + (iota((128, 1), 0) % 8).astype(F32)
    take_ref[...] = (iota((128, 256), 1).astype(F32) == target).astype(F32).astype(BF16)


def route(me, sources, spans):
    return pl.pallas_call(
        route_kernel,
        in_specs=[SMEM] + [pl.BlockSpec(memory_space=pltpu.VMEM)] * 2,
        out_specs=[pl.BlockSpec(memory_space=pltpu.VMEM)] * 3,
        out_shape=[
            jax.ShapeDtypeStruct((256, 128), BF16),
            jax.ShapeDtypeStruct((128, 256), BF16),
            jax.ShapeDtypeStruct((16, 1), jnp.int32),
        ],
        name="route",
    )(me, sources, spans)


def filter_blocks_kernel(me_ref, taps_ref, *out_refs):
    for r, out_ref in enumerate(out_refs):
        for h in range(4):
            at = pl.multiple_of((me_ref[0] ^ (r | 4 * h)) * LANES, LANES)
            out_ref[h] = taps_ref[:, pl.ds(at, LANES)].astype(BF16)


def filter_blocks(me, filter_taps):
    return pl.pallas_call(
        filter_blocks_kernel,
        in_specs=[SMEM, pl.BlockSpec(memory_space=pltpu.VMEM)],
        out_specs=[pl.BlockSpec(memory_space=pltpu.VMEM)] * 4,
        out_shape=[jax.ShapeDtypeStruct((4, 128, LANES), BF16)] * 4,
        name="filter_blocks",
    )(me, filter_taps)


def masks_of(ids_ref):
    here = ids_ref[8:144, :]
    return (ids_ref[7:143, :] == here).astype(F32), (ids_ref[6:142, :] == here).astype(F32)


def gather_kernel(k_ref, v_ref, q_ref, take_ref, ids_ref, w_ref, cot_ref, out_ref, xs, edge):
    take = take_ref[...]
    m1, m2 = masks_of(ids_ref)
    for s, ref in enumerate((k_ref, v_ref, q_ref)):
        xs[s, 0:8, :] = jnp.zeros((8, CHUNK), F32)
        xs[s, 8:136, :] = dot(take, ref[...])
        xs[s, 136:144, :] = jnp.zeros((8, CHUNK), F32)

    for h in range(CHUNK // LANES):
        at = slice(h * LANES, (h + 1) * LANES)
        hats = []
        for s in range(3):
            w = w_ref[:, s, at]
            hats.append(
                w[0:1] * xs[s, 8:144, at]
                + w[1:2] * (xs[s, 7:143, at] * m1)
                + w[2:3] * (xs[s, 6:142, at] * m2)
            )
            edge[2 * s : 2 * s + 2, :] = hats[s][0:2]
            edge[2 * s + 8 : 2 * s + 10, :] = hats[s][128:130]
        cot = cot_ref[:, at].astype(F32)
        edge[6:8, :] = cot[0:2]
        edge[14:16, :] = jnp.zeros((2, LANES), F32)
        out_ref[h, 0:128, :] = (hats[0] * hats[1])[0:128].astype(BF16)
        out_ref[h, 128:256, :] = (cot * hats[2][0:128]).astype(BF16)
        out_ref[h, 256:272, :] = edge[...].astype(BF16)


def stream_specs(rows, chunks):
    return [pl.BlockSpec((rows, CHUNK), lambda c, s=s: (0, s * chunks + c)) for s in range(3)]


def column_spec(rows):
    return pl.BlockSpec((rows, CHUNK), lambda c: (0, c))


WEIGHTS = pl.BlockSpec((3, 3, CHUNK), lambda c: (0, 0, c))


def gather_rows(received, take, ids, weights, cot):
    chunks = cot.shape[1] // CHUNK
    per = CHUNK // LANES
    return pl.pallas_call(
        gather_kernel,
        grid=(chunks,),
        in_specs=stream_specs(256, chunks)
        + [whole(128, 256), whole(144, 1), WEIGHTS, column_spec(128)],
        out_specs=pl.BlockSpec((per, 272, LANES), lambda c: (c, 0, 0)),
        out_shape=jax.ShapeDtypeStruct((chunks * per, 272, LANES), BF16),
        scratch_shapes=[pltpu.VMEM((3, 144, CHUNK), F32), pltpu.VMEM((16, LANES), F32)],
        name="gather_rows",
    )(received, received, received, take, ids, weights, cot)


def outer_forward(fh_ref, pick, spec):
    nothing = jnp.zeros(spec.shape[1:], BF16)
    for where in (1, 3):
        spec[where] = nothing
    for g in range(8):
        at = slice(16 * g, 16 * g + 16)
        data = pick(g)
        value = dot(fh_ref[...], data).astype(BF16)
        spec[0, at, :] = value[0:16]
        spec[2, at, :] = value[16:32]
        spec[4:34, at, :] = value[32:512].reshape(30, 16, value.shape[1])


def outer_back(bh_ref, turns, g):
    at = slice(16 * g, 16 * g + 16)
    rest = turns[4:34, at, :].reshape(480, turns.shape[2])
    return dot(bh_ref[...], jnp.concatenate([turns[0, at, :], turns[2, at, :], rest], axis=0))


def pair_of(ref, k):
    return ref[pl.ds(2 * k, 2)].reshape(2 * LANES, ref.shape[2])


def put_pair(ref, k, value):
    ref[pl.ds(2 * k, 2)] = value.astype(BF16).reshape(2, LANES, ref.shape[2])


VMEM_SPEC = pl.BlockSpec(memory_space=pltpu.VMEM)


def inner_loop(step):
    def four(i, carry):
        for j in range(4):
            step(4 * i + j)
        return carry

    lax.fori_loop(0, 4, four, 0)
    step(16)


def filter_kernel(me_ref, fc_ref, fs_ref, row_ref, of_ref, ob_ref, *rest):
    blocks, (out_ref, f_ref, b_ref, ordered, spec) = rest[:7], rest[7:]
    f_ref[...] = spread_in(of_ref[...], 16)
    b_ref[...] = spread_in(ob_ref[...], 16)
    for r in range(4):
        ordered[me_ref[0] ^ r] = blocks[r][0]
        for h in range(1, 4):
            ordered[me_ref[0] ^ (r | 4 * h)] = blocks[3 + h][r]
    outer_forward(f_ref, lambda g: ordered[:, 16 * g : 16 * g + 16, :].reshape(256, LANES), spec)

    def step(k, carry):
        out_ref[k] = dot(forward_table(fc_ref, fs_ref, row_ref, k), pair_of(spec, k)).astype(BF16)
        return carry

    lax.fori_loop(0, 17, step, 0)


def rounded(table):
    return jnp.asarray(np.asarray(table, np.float32).astype(jnp.bfloat16))


def filter_spectrum(me, constants, blocks):
    fc, fs, row, _ = constants
    forward, back = outer_tables()
    return pl.pallas_call(
        filter_kernel,
        in_specs=[SMEM] + [VMEM_SPEC] * 12,
        out_specs=[VMEM_SPEC] * 3,
        out_shape=[
            jax.ShapeDtypeStruct((17, 2 * LANES, LANES), BF16),
            jax.ShapeDtypeStruct((512, 256), BF16),
            jax.ShapeDtypeStruct((256, 512), BF16),
        ],
        scratch_shapes=[pltpu.VMEM((16, 128, LANES), BF16), pltpu.VMEM((34, LANES, LANES), BF16)],
        name="filter_spectrum",
    )(me, fc, fs, row, rounded(forward), rounded(back), *blocks)


def conv_kernel(
    in_ref, h_ref, fc_ref, fs_ref, row_ref, col_ref, f_ref, b_ref, out_ref, cross_ref, spec, turns, firsts,
):
    def pick(g):
        if g:
            parts = [in_ref[:, 128 * i + 16 * g : 128 * i + 16 * g + 16, :] for i in range(2)]
        else:
            edges = in_ref[:, 256:272, :].astype(F32)
            nothing = jnp.zeros((1, 8, LANES), F32)
            filtered = edges[:, 0:8] + jnp.concatenate([nothing, edges[:15, 8:16]], axis=0)
            firsts[...] = filtered
            gated = filtered * pltpu.roll(filtered, 6, 1)
            heads = (gated, pltpu.roll(gated, 4, 1))
            rows = iota((16, 16, LANES), 1)
            parts = []
            for i in range(2):
                head = jnp.concatenate([heads[i], heads[i]], axis=1)
                plain = in_ref[:, 128 * i : 128 * i + 16, :].astype(F32)
                parts.append(jnp.where(rows < 2, head, plain).astype(BF16))
        return jnp.concatenate([part.reshape(256, LANES) for part in parts], axis=1)

    outer_forward(f_ref, pick, spec)

    def step(k):
        value = dot(forward_table(fc_ref, fs_ref, row_ref, k), pair_of(spec, k))
        xr, xi = value[:LANES, :LANES], value[LANES:, :LANES]
        gr, gi = value[:LANES, LANES:], value[LANES:, LANES:]
        h = h_ref[k].astype(F32)
        hr, hi = h[:LANES], h[LANES:]
        cross = jnp.concatenate([xr * gr + xi * gi, xr * gi - xi * gr], axis=0)
        cross_ref[k] = cross.astype(BF16)
        real = jnp.concatenate([hr * xr - hi * xi, hr * gr + hi * gi], axis=1)
        imag = jnp.concatenate([hr * xi + hi * xr, hr * gi - hi * gr], axis=1)
        mixed = jnp.concatenate([real, imag], axis=0).astype(BF16)
        put_pair(turns, k, dot(back_table(fc_ref, fs_ref, col_ref, k), mixed))

    inner_loop(step)
    for g in range(8):
        last = outer_back(b_ref, turns, g)
        parts = [last[:, i * LANES : (i + 1) * LANES].reshape(16, 16, LANES) for i in range(2)]
        for i in range(2):
            out_ref[:, 128 * i + 16 * g : 128 * i + 16 * g + 16, :] = parts[i].astype(BF16)
        if g == 0:
            own = firsts[...]
            nothing = jnp.zeros((1, 8, LANES), F32)
            conv, grad, following = (
                jnp.concatenate([part[1:, 0:8], nothing], axis=0) for part in (*parts, own)
            )
            row = iota((16, 8, LANES), 1)
            following = jnp.where((row == 4) | (row == 5), pltpu.roll(conv, 4, 1), following)
            own = jnp.where(row >= 6, pltpu.roll(grad, 6, 1), own)
            out_ref[:, 256:272, :] = jnp.concatenate([following, own], axis=1).astype(BF16)


def conv_both(columns, spectrum, constants):
    h, forward, back = spectrum
    return pl.pallas_call(
        conv_kernel,
        in_specs=[VMEM_SPEC] * 8,
        out_specs=[VMEM_SPEC] * 2,
        out_shape=[
            jax.ShapeDtypeStruct((16, 272, LANES), BF16),
            jax.ShapeDtypeStruct((17, 2 * LANES, LANES), BF16),
        ],
        scratch_shapes=[pltpu.VMEM((34, LANES, 2 * LANES), BF16) for _ in range(2)]
        + [pltpu.VMEM((16, 8, LANES), F32)],
        name="conv_both",
    )(columns, h, *constants, forward, back)


def halving_place(j):
    return ((j & 1) << 3) | (j & 4) | ((j & 8) >> 2) | ((j & 2) >> 1)


def filter_grad_kernel(ids_ref, cross_ref, fc_ref, fs_ref, col_ref, bh_ref, out_ref, turns):
    def step(k):
        put_pair(turns, k, dot(back_table(fc_ref, fs_ref, col_ref, k), cross_ref[k]))

    inner_loop(step)
    for g in range(8):
        part = outer_back(bh_ref, turns, g).reshape(16, 16, LANES)
        for e in range(2):
            place = halving_place((2 * g + e) ^ ids_ref[0])
            for p in range(16):
                out_ref[place, p ^ ids_ref[1]] = part[p, 8 * e : 8 * e + 8].astype(BF16)


def filter_grad(ids, cross, constants, back):
    fc, fs, _, col = constants
    return pl.pallas_call(
        filter_grad_kernel,
        in_specs=[SMEM] + [VMEM_SPEC] * 5,
        out_specs=VMEM_SPEC,
        out_shape=jax.ShapeDtypeStruct((16, 16, 8, LANES), BF16),
        scratch_shapes=[pltpu.VMEM((34, LANES, LANES), BF16)],
        name="filter_grad",
    )(ids, cross, fc, fs, col, back)


def hats_kernel(k_ref, v_ref, take_ref, ids_ref, w_ref, key_ref, value_ref, xs):
    m1, m2 = (mask[0:128] for mask in masks_of(ids_ref))
    take = take_ref[...]
    for s, ref in enumerate((k_ref, v_ref)):
        xs[s, 0:8, :] = jnp.zeros((8, CHUNK), F32)
        xs[s, 8:136, :] = dot(take, ref[...])

    def part(h, carry):
        at = pl.ds(pl.multiple_of(h * LANES, LANES), LANES)
        for s, out_ref in enumerate((key_ref, value_ref)):
            w = w_ref[:, s, at]
            out_ref[:, at] = (
                w[0:1] * xs[s, 8:136, at] + w[1:2] * (xs[s, 7:135, at] * m1) + w[2:3] * (xs[s, 6:134, at] * m2)
            )
        return carry

    lax.fori_loop(0, CHUNK // LANES, part, 0)


def make_hats(received, take, ids, weights):
    channels = weights.shape[2]
    chunks = channels // CHUNK
    return pl.pallas_call(
        hats_kernel,
        grid=(chunks,),
        in_specs=stream_specs(256, chunks)[:2] + [whole(128, 256), whole(144, 1), WEIGHTS],
        out_specs=[column_spec(128)] * 2,
        out_shape=[jax.ShapeDtypeStruct((128, channels), F32)] * 2,
        scratch_shapes=[pltpu.VMEM((2, 136, CHUNK), F32)],
        name="make_hats",
    )(received, received, take, ids, weights)


def edges_of(conv_ref, h):
    edges = conv_ref[h, 256:272, :].astype(F32)
    return edges[0:8], edges[8:16]


def patched(ref, at, own, shift):
    own = pltpu.roll(own, shift, 0) if shift else own
    head = jnp.where(iota((8, LANES), 0) < 2, own, ref[0:8, at])
    return head, ref[8:128, at]


def back_kernel(key_ref, value_ref, give_ref, ids_ref, w_ref, cot_ref, conv_ref, back_ref, one, two):
    give = give_ref[...]
    m1, m2 = masks_of(ids_ref)

    for h in range(CHUNK // LANES):
        at = slice(h * LANES, (h + 1) * LANES)
        following, own = edges_of(conv_ref, h)
        conv = jnp.concatenate([conv_ref[h, 0:128, :].astype(F32), pltpu.roll(following, 4, 0)], axis=0)
        grad_product = jnp.concatenate([conv_ref[h, 128:256, :].astype(F32), pltpu.roll(own, 2, 0)], axis=0)
        cot = jnp.concatenate([cot_ref[:, at].astype(F32), pltpu.roll(following, 2, 0)], axis=0)
        key = jnp.concatenate([*patched(key_ref, at, own, 0), following], axis=0)
        value = jnp.concatenate([*patched(value_ref, at, own, 6), pltpu.roll(following, 6, 0)], axis=0)
        grads = (grad_product * value, grad_product * key, cot * conv)
        for s in range(3):
            w = w_ref[:, s, at]
            grad = grads[s]
            one[s] = grad * m1
            two[s] = grad * m2
            rows = w[0:1] * grad[0:128] + w[1:2] * one[s, 1:129] + w[2:3] * two[s, 2:130]
            sent = dot(give, rows.astype(BF16)).astype(BF16)
            back_ref[:, 16 * s : 16 * s + 16, at] = sent.reshape(16, 16, LANES)


def back_rows(hats, give, ids, weights, cot, local):
    channels = cot.shape[1]
    chunks = channels // CHUNK
    per = CHUNK // LANES
    return pl.pallas_call(
        back_kernel,
        grid=(chunks,),
        in_specs=[
            column_spec(128),
            column_spec(128),
            whole(256, 128),
            whole(144, 1),
            WEIGHTS,
            column_spec(128),
            pl.BlockSpec((per, 272, LANES), lambda c: (c, 0, 0)),
        ],
        out_specs=pl.BlockSpec((16, 48, CHUNK), lambda c: (0, 0, c)),
        out_shape=jax.ShapeDtypeStruct((16, 48, channels), BF16),
        scratch_shapes=[pltpu.VMEM((3, 136, LANES), F32) for _ in range(2)],
        name="back_rows",
    )(*hats, give, ids, weights, cot, local)


def sums_kernel(
    me_ref, k_ref, v_ref, q_ref, take_ref, pk_ref, pv_ref, pq_ref, key_ref, value_ref, ids_ref, w_ref, cot_ref, conv_ref,
    mixed_ref, taps_ref, xs,
):
    take = take_ref[...]
    m1, m2 = (mask[0:128] for mask in masks_of(ids_ref))
    for s, (ref, prev) in enumerate(((k_ref, pk_ref), (v_ref, pv_ref), (q_ref, pq_ref))):
        xs[s, 6:8, :] = prev[...].astype(F32)
        xs[s, 8:136, :] = dot(take, ref[...])

    def part(h, carry):
        at = pl.ds(pl.multiple_of(h * LANES, LANES), LANES)
        block = (CHUNK // LANES) * pl.program_id(0) + h
        side = (block // 8) ^ (me_ref[0] % 2)
        conv = conv_ref[h, 0:128, :].astype(F32)
        grad_product = conv_ref[h, 128:256, :].astype(F32)
        cot = cot_ref[:, at].astype(F32)
        own = edges_of(conv_ref, h)[1]
        key = jnp.concatenate(patched(key_ref, at, own, 0), axis=0)
        value = jnp.concatenate(patched(value_ref, at, own, 6), axis=0)
        grads = (grad_product * value, grad_product * key, cot * conv)
        for s in range(3):
            parts = (xs[s, 8:136, at], xs[s, 7:135, at] * m1, xs[s, 6:134, at] * m2)
            for k in range(3):
                total = jnp.sum(grads[s] * parts[k], axis=0, keepdims=True)
                taps_ref[side, 3 * s + k, pl.ds(block % 8, 1), :] = total
            if s == 2:
                w = w_ref[:, s, at]
                query = w[0:1] * parts[0] + w[1:2] * parts[1] + w[2:3] * parts[2]
                mixed_ref[:, at] = (query * conv).astype(BF16)
        return carry

    lax.fori_loop(0, CHUNK // LANES, part, 0)


def mixed_and_sums(me, received, take, prev, hats, ids, weights, cot, local):
    channels = cot.shape[1]
    chunks = channels // CHUNK
    per = CHUNK // LANES
    return pl.pallas_call(
        sums_kernel,
        grid=(chunks,),
        in_specs=[SMEM]
        + stream_specs(256, chunks)
        + [whole(128, 256)]
        + stream_specs(2, chunks)
        + [
            column_spec(128),
            column_spec(128),
            whole(144, 1),
            WEIGHTS,
            column_spec(128),
            pl.BlockSpec((per, 272, LANES), lambda c: (c, 0, 0)),
        ],
        out_specs=[column_spec(128), whole(2, 9, 8, LANES)],
        out_shape=[
            jax.ShapeDtypeStruct((128, channels), BF16),
            jax.ShapeDtypeStruct((2, 9, 8, LANES), F32),
        ],
        scratch_shapes=[pltpu.VMEM((3, 136, CHUNK), F32)],
        name="mixed_and_sums",
    )(me, received, received, received, take, prev, prev, prev, *hats, ids, weights, cot, local)


def store_kernel(select_ref, in_ref, out_ref):
    width = in_ref.shape[2]
    out_ref[...] = dot_t(select_ref[...], in_ref[...].reshape(256, width)).astype(BF16)


def store_grads(select, returned, channels):
    width = 1024
    chunks = channels // width
    return pl.pallas_call(
        store_kernel,
        grid=(3, chunks),
        in_specs=[
            whole(256, 128),
            pl.BlockSpec((16, 16, width), lambda s, c: (0, s, c)),
        ],
        out_specs=pl.BlockSpec((128, width), lambda s, c: (0, s * chunks + c)),
        out_shape=jax.ShapeDtypeStruct((128, 3 * channels), BF16),
        name="store_grads",
    )(select, returned)


def final_kernel(me_ref, in_ref, grad_ref, taps_ref, total):
    for j in range(16):
        at = pl.multiple_of((j ^ me_ref[0]) * LANES, LANES)
        grad_ref[:, pl.ds(at, LANES)] = in_ref[:, 8 * j : 8 * j + 8, :].astype(F32).reshape(128, LANES)
    for side in range(2):
        parts = [in_ref[d, 128:200, :].astype(F32) for d in range(side, 16, 2)]
        total[side] = sum(parts[1:], parts[0]).reshape(9, 8, LANES)
    for i in range(3):
        for c in range(16):
            taps_ref[i, :, c * LANES : (c + 1) * LANES] = total[c // 8, 3 * i : 3 * i + 3, c % 8, :]


def final_parts(me, final):
    return pl.pallas_call(
        final_kernel,
        in_specs=[SMEM, VMEM_SPEC],
        out_specs=[VMEM_SPEC] * 2,
        out_shape=[jax.ShapeDtypeStruct((128, 2048), F32), jax.ShapeDtypeStruct((3, 3, 2048), F32)],
        scratch_shapes=[pltpu.VMEM((2, 9, 8, LANES), F32)],
        name="final_parts",
    )(me, final)


def across(value, axis, bit):
    return lax.ppermute(value, axis, [(i, i ^ bit) for i in range(lax.axis_size(axis))])


def halving_sum(value):
    total = value.astype(F32)
    for bit in (1, 4, 8, 2):
        half = total.shape[0] // 2
        total = total[:half] + across(total[half:].astype(BF16), "dp", bit).astype(F32)
    return total[0]


def cube_exchange(value, axis):
    shape = value.shape
    for bit in (1, 2, 4, 8):
        grouped = value.reshape(shape[0] // (2 * bit), 2, bit, *shape[1:])
        other = across(grouped[:, 1], axis, bit)
        value = jnp.stack([grouped[:, 0], other], axis=1).reshape(shape)
    return value


def total_over(value, axis):
    for bit in (1, 2, 4, 8):
        value = value + across(value, axis, bit)
    return value


def shards(stored, source_row, source_span, segments, short_weight, filter_taps, cotangent):
    dp_count = lax.axis_size("dp")
    my_dp = lax.axis_index("dp").astype(jnp.int32)
    my_seq = lax.axis_index("seq").astype(jnp.int32)
    tok_rows = stored.shape[1]
    width = stored.shape[2]
    channels = width // 3
    span_count = source_span.shape[1]
    span_rows = tok_rows // span_count
    sources = source_row[:, :, 0]
    dp_id, seq_id = my_dp[None], my_seq[None]

    select, take, place = route(dp_id, sources, source_span)
    sent = dot(select, stored[0]).astype(BF16)
    received = exchange(sent.reshape(dp_count, MOST * span_rows, width), "dp")
    received = received.reshape(dp_count * MOST * span_rows, width)

    near = filter_blocks(seq_id, filter_taps)
    near = [near[0]] + [across(near[r], "seq", r) for r in range(1, 4)]
    ids = segments[0] + 1
    outside = jnp.full((6,), -1, jnp.int32)
    ids = jnp.concatenate([outside, shifted(ids[-2:], "seq", 1), ids, shifted(ids[:2], "seq", -1), outside])
    ids = ids.astype(F32)[:, None]
    near, ids = lax.optimization_barrier((near, ids))
    far = [across(jnp.stack([part[h] for part in near]), "seq", 4 * h) for h in range(1, 4)]

    cot = cotangent[0]
    weights = jnp.transpose(short_weight, (1, 0, 2))
    received, near, far, ids, weights = lax.optimization_barrier((received, near, far, ids, weights))

    columns = exchange(gather_rows(received, take, ids, weights, cot), "seq")
    constants = dft_constants()
    spectrum = filter_spectrum(seq_id, constants, near + far)
    hats = make_hats(received, take, ids, weights)
    give = jnp.transpose(take)
    last = lax.dynamic_slice(received, (place[-1, 0], 0), (span_rows, width))[-2:]
    prev = shifted(last, "seq", 1)
    columns, spectrum, hats, give, prev = lax.optimization_barrier((columns, spectrum, hats, give, prev))
    results, cross = conv_both(columns, spectrum, constants)
    local = exchange(results, "seq")
    lags = halving_sum(filter_grad(jnp.stack([my_dp, my_seq]), cross, constants, spectrum[2]))

    back = back_rows(hats, give, ids, weights, cot, local)
    back, local, lags = lax.optimization_barrier((back, local, lags))
    returned = exchange(back, "dp")
    mixed, taps = mixed_and_sums(dp_id, received, take, prev, hats, ids, weights, cot, local)
    lags = cube_exchange(lags.astype(BF16), "seq")
    taps = total_over(taps[0] + across(taps[1], "dp", 1), "seq")
    final = jnp.concatenate([lags.reshape(128, LANES), taps.astype(BF16).reshape(72, LANES)], axis=0)
    final = jnp.broadcast_to(final[None], (dp_count, *final.shape))
    returned, final = lax.optimization_barrier((returned, final))
    final = exchange(final, "dp")
    grad_stored = store_grads(select, returned, channels)
    grad_filter, grad_short = final_parts(seq_id, final)
    return (mixed[None], grad_stored[None], grad_filter, grad_short)


def solution(mesh):
    return jax.shard_map(
        shards,
        mesh=mesh,
        in_specs=(
            P("dp", "seq", None),
            P(None, "seq", None),
            P(None, "seq"),
            P("dp", "seq"),
            P(),
            P("seq", None),
            P("dp", "seq", None),
        ),
        out_specs=(P("dp", "seq", None), P("dp", "seq", None), P("seq", None), P()),
        check_vma=False,
    )
```

```python
import functools
import math

import jax
import jax.numpy as jnp
import numpy as np
from jax import lax
from jax.experimental import pallas as pl
from jax.experimental.pallas import tpu as pltpu
from jax.sharding import PartitionSpec as P

MOST = 2
CHUNK = 512
LANES = 128
F32 = jnp.float32
BF16 = jnp.bfloat16


def shifted(value, axis, by):
    length = lax.axis_size(axis)
    pairs = [(i, i + by) for i in range(length) if 0 <= i + by < length]
    return lax.ppermute(value, axis, pairs)


def exchange(value, axis):
    return lax.all_to_all(value, axis, 0, 0, tiled=True)


def dot(left, right):
    return jnp.dot(left, right, preferred_element_type=F32)


def dot_t(left, right):
    return lax.dot_general(left, right, (((0,), (0,)), ((), ())), preferred_element_type=F32)


def iota(shape, axis):
    return lax.broadcasted_iota(jnp.int32, shape, axis)


def whole(*shape):
    return pl.BlockSpec(shape, lambda *ids: (0,) * len(shape))


SMEM = pl.BlockSpec(memory_space=pltpu.SMEM)


def outer_tables():
    blocks = np.arange(16)
    forward = [np.ones(16), np.cos(np.pi * blocks)]
    back = [np.ones(16), np.cos(np.pi * blocks)]
    for k in range(1, 16):
        angle = 2.0 * np.pi * k * blocks / 32.0
        forward += [np.cos(angle), -np.sin(angle)]
        back += [2.0 * np.cos(angle), -2.0 * np.sin(angle)]
    return np.stack(forward), np.stack(back, axis=1) / 4096.0


def spread_in(table, by):
    rows, cols = table.shape
    tall = (iota((rows * by, rows), 0) // by == iota((rows * by, rows), 1)).astype(BF16)
    wide = (iota((cols, cols * by), 0) == iota((cols, cols * by), 1) // by).astype(BF16)
    value = dot(dot(tall, table).astype(BF16), wide)
    shape = (rows * by, cols * by)
    diagonal = iota(shape, 0) % by == iota(shape, 1) % by
    return jnp.where(diagonal, value, 0.0).astype(BF16)


def dft_constants():
    inner = np.arange(LANES)
    turn = 2.0 * np.pi * (inner[:, None] * inner[None, :] % LANES) / LANES
    order = np.asarray([0, 16] + list(range(1, 16)))
    twist = 2.0 * np.pi * order[:, None] * inner[None, :] / 4096.0
    values = (
        np.cos(turn),
        np.sin(turn),
        np.stack([np.cos(twist), np.sin(twist)], axis=1),
        np.stack([np.cos(twist), np.sin(twist)], axis=2),
    )
    return tuple(jnp.asarray(value, F32) for value in values)


def turned(fc_ref, fs_ref, wc, ws):
    fc = fc_ref[...]
    fs = fs_ref[...]
    return fc * wc - fs * ws, fs * wc + fc * ws


def forward_table(fc_ref, fs_ref, row_ref, k):
    row = row_ref[k]
    cos, sin = turned(fc_ref, fs_ref, row[0:1, :], row[1:2, :])
    cos, sin, minus = cos.astype(BF16), sin.astype(BF16), (-sin).astype(BF16)
    return jnp.concatenate(
        [jnp.concatenate([cos, sin], axis=1), jnp.concatenate([minus, cos], axis=1)], axis=0
    )


def back_table(fc_ref, fs_ref, col_ref, k):
    col = col_ref[k]
    cos, sin = turned(fc_ref, fs_ref, col[:, 0:1], col[:, 1:2])
    cos, sin, minus = cos.astype(BF16), sin.astype(BF16), (-sin).astype(BF16)
    return jnp.concatenate(
        [jnp.concatenate([cos, minus], axis=1), jnp.concatenate([sin, cos], axis=1)], axis=0
    )


def route_kernel(me_ref, source_ref, span_ref, select_ref, take_ref, place_ref):
    sources = source_ref[...].astype(F32)
    mine = (source_ref[...] == me_ref[0]).astype(F32)
    before = (iota((16, 16), 0) < iota((16, 16), 1)).astype(F32)
    earlier = dot(mine, before)
    tall = (iota((256, 16), 0) // 16 == iota((256, 16), 1)).astype(F32)
    slot = iota((256, 16), 0) // 8 % 2
    hit = dot(tall, mine) * (dot(tall, earlier) == slot.astype(F32)).astype(F32)
    start = jnp.sum(hit * (dot(tall, span_ref[...].astype(F32)) * 8.0 + 1.0), axis=1, keepdims=True)
    target = jnp.where(start > 0.5, start - 1.0 + (iota((256, 1), 0) % 8).astype(F32), -1.0)
    select_ref[...] = (iota((256, 128), 1).astype(F32) == target).astype(F32).astype(BF16)

    row = iota((16, 16), 0)
    col = iota((16, 16), 1)
    ours = jnp.sum(jnp.where(row == me_ref[0], sources, 0.0), axis=0, keepdims=True)
    ours_down = jnp.sum(jnp.where(row == col, ours, 0.0), axis=1, keepdims=True)
    order = jnp.sum(((ours_down == ours) & (col < row)).astype(F32), axis=1, keepdims=True)
    place = (ours_down * MOST + order) * 8.0
    place_ref[...] = place.astype(jnp.int32)
    place_across = jnp.sum(jnp.where(row == col, place, 0.0), axis=0, keepdims=True)
    slots = iota((128, 16), 0) // 8 == iota((128, 16), 1)
    target = jnp.sum(jnp.where(slots, place_across, 0.0), axis=1, keepdims=True)
    target = target + (iota((128, 1), 0) % 8).astype(F32)
    take_ref[...] = (iota((128, 256), 1).astype(F32) == target).astype(F32).astype(BF16)


def route(me, sources, spans):
    return pl.pallas_call(
        route_kernel,
        in_specs=[SMEM] + [pl.BlockSpec(memory_space=pltpu.VMEM)] * 2,
        out_specs=[pl.BlockSpec(memory_space=pltpu.VMEM)] * 3,
        out_shape=[
            jax.ShapeDtypeStruct((256, 128), BF16),
            jax.ShapeDtypeStruct((128, 256), BF16),
            jax.ShapeDtypeStruct((16, 1), jnp.int32),
        ],
        name="route",
    )(me, sources, spans)


def filter_blocks_kernel(me_ref, taps_ref, *out_refs):
    for r, out_ref in enumerate(out_refs):
        for h in range(2):
            at = pl.multiple_of((me_ref[0] ^ (r | 8 * h)) * LANES, LANES)
            out_ref[h] = taps_ref[:, pl.ds(at, LANES)].astype(BF16)


def filter_blocks(me, filter_taps):
    return pl.pallas_call(
        filter_blocks_kernel,
        in_specs=[SMEM, pl.BlockSpec(memory_space=pltpu.VMEM)],
        out_specs=[pl.BlockSpec(memory_space=pltpu.VMEM)] * 8,
        out_shape=[jax.ShapeDtypeStruct((2, 128, LANES), BF16)] * 8,
        name="filter_blocks",
    )(me, filter_taps)


def masks_of(ids_ref):
    here = ids_ref[8:144, :]
    return (ids_ref[7:143, :] == here).astype(F32), (ids_ref[6:142, :] == here).astype(F32)


def gather_kernel(k_ref, v_ref, q_ref, take_ref, ids_ref, w_ref, cot_ref, out_ref, xs, edge):
    take = take_ref[...]
    m1, m2 = masks_of(ids_ref)
    for s, ref in enumerate((k_ref, v_ref, q_ref)):
        xs[s, 0:8, :] = jnp.zeros((8, CHUNK), F32)
        xs[s, 8:136, :] = dot(take, ref[...])
        xs[s, 136:144, :] = jnp.zeros((8, CHUNK), F32)

    for h in range(CHUNK // LANES):
        at = slice(h * LANES, (h + 1) * LANES)
        hats = []
        for s in range(3):
            w = w_ref[:, s, at]
            hats.append(
                w[0:1] * xs[s, 8:144, at]
                + w[1:2] * (xs[s, 7:143, at] * m1)
                + w[2:3] * (xs[s, 6:142, at] * m2)
            )
            edge[2 * s : 2 * s + 2, :] = hats[s][0:2]
            edge[2 * s + 8 : 2 * s + 10, :] = hats[s][128:130]
        cot = cot_ref[:, at].astype(F32)
        edge[6:8, :] = cot[0:2]
        edge[14:16, :] = jnp.zeros((2, LANES), F32)
        out_ref[h, 0:128, :] = (hats[0] * hats[1])[0:128].astype(BF16)
        out_ref[h, 128:256, :] = (cot * hats[2][0:128]).astype(BF16)
        out_ref[h, 256:272, :] = edge[...].astype(BF16)


def stream_specs(rows, chunks):
    return [pl.BlockSpec((rows, CHUNK), lambda c, s=s: (0, s * chunks + c)) for s in range(3)]


def column_spec(rows):
    return pl.BlockSpec((rows, CHUNK), lambda c: (0, c))


WEIGHTS = pl.BlockSpec((3, 3, CHUNK), lambda c: (0, 0, c))


def gather_rows(received, take, ids, weights, cot):
    chunks = cot.shape[1] // CHUNK
    per = CHUNK // LANES
    return pl.pallas_call(
        gather_kernel,
        grid=(chunks,),
        in_specs=stream_specs(256, chunks)
        + [whole(128, 256), whole(144, 1), WEIGHTS, column_spec(128)],
        out_specs=pl.BlockSpec((per, 272, LANES), lambda c: (c, 0, 0)),
        out_shape=jax.ShapeDtypeStruct((chunks * per, 272, LANES), BF16),
        scratch_shapes=[pltpu.VMEM((3, 144, CHUNK), F32), pltpu.VMEM((16, LANES), F32)],
        name="gather_rows",
    )(received, received, received, take, ids, weights, cot)


def outer_forward(fh_ref, pick, spec):
    nothing = jnp.zeros(spec.shape[1:], BF16)
    for where in (1, 3):
        spec[where] = nothing
    for g in range(8):
        at = slice(16 * g, 16 * g + 16)
        data = pick(g)
        value = dot(fh_ref[...], data).astype(BF16)
        spec[0, at, :] = value[0:16]
        spec[2, at, :] = value[16:32]
        spec[4:34, at, :] = value[32:512].reshape(30, 16, value.shape[1])


def outer_back(bh_ref, turns, g):
    at = slice(16 * g, 16 * g + 16)
    rest = turns[4:34, at, :].reshape(480, turns.shape[2])
    return dot(bh_ref[...], jnp.concatenate([turns[0, at, :], turns[2, at, :], rest], axis=0))


def pair_of(ref, k):
    return ref[pl.ds(2 * k, 2)].reshape(2 * LANES, ref.shape[2])


def put_pair(ref, k, value):
    ref[pl.ds(2 * k, 2)] = value.astype(BF16).reshape(2, LANES, ref.shape[2])


VMEM_SPEC = pl.BlockSpec(memory_space=pltpu.VMEM)


def inner_loop(step):
    def four(i, carry):
        for j in range(4):
            step(4 * i + j)
        return carry

    lax.fori_loop(0, 4, four, 0)
    step(16)


def filter_kernel(me_ref, fc_ref, fs_ref, row_ref, of_ref, ob_ref, *rest):
    blocks, (out_ref, f_ref, b_ref, ordered, spec) = rest[:9], rest[9:]
    f_ref[...] = spread_in(of_ref[...], 16)
    b_ref[...] = spread_in(ob_ref[...], 16)
    for r in range(8):
        ordered[me_ref[0] ^ r] = blocks[r][0]
        ordered[me_ref[0] ^ (r | 8)] = blocks[8][r]
    outer_forward(f_ref, lambda g: ordered[:, 16 * g : 16 * g + 16, :].reshape(256, LANES), spec)

    def step(k, carry):
        out_ref[k] = dot(forward_table(fc_ref, fs_ref, row_ref, k), pair_of(spec, k)).astype(BF16)
        return carry

    lax.fori_loop(0, 17, step, 0)


def rounded(table):
    return jnp.asarray(np.asarray(table, np.float32).astype(jnp.bfloat16))


def filter_spectrum(me, constants, blocks):
    fc, fs, row, _ = constants
    forward, back = outer_tables()
    return pl.pallas_call(
        filter_kernel,
        in_specs=[SMEM] + [VMEM_SPEC] * 14,
        out_specs=[VMEM_SPEC] * 3,
        out_shape=[
            jax.ShapeDtypeStruct((17, 2 * LANES, LANES), BF16),
            jax.ShapeDtypeStruct((512, 256), BF16),
            jax.ShapeDtypeStruct((256, 512), BF16),
        ],
        scratch_shapes=[pltpu.VMEM((16, 128, LANES), BF16), pltpu.VMEM((34, LANES, LANES), BF16)],
        name="filter_spectrum",
    )(me, fc, fs, row, rounded(forward), rounded(back), *blocks)


def conv_kernel(
    in_ref, h_ref, fc_ref, fs_ref, row_ref, col_ref, f_ref, b_ref, out_ref, cross_ref, spec, turns, firsts,
):
    def pick(g):
        if g:
            parts = [in_ref[:, 128 * i + 16 * g : 128 * i + 16 * g + 16, :] for i in range(2)]
        else:
            edges = in_ref[:, 256:272, :].astype(F32)
            nothing = jnp.zeros((1, 8, LANES), F32)
            filtered = edges[:, 0:8] + jnp.concatenate([nothing, edges[:15, 8:16]], axis=0)
            firsts[...] = filtered
            gated = filtered * pltpu.roll(filtered, 6, 1)
            heads = (gated, pltpu.roll(gated, 4, 1))
            rows = iota((16, 16, LANES), 1)
            parts = []
            for i in range(2):
                head = jnp.concatenate([heads[i], heads[i]], axis=1)
                plain = in_ref[:, 128 * i : 128 * i + 16, :].astype(F32)
                parts.append(jnp.where(rows < 2, head, plain).astype(BF16))
        return jnp.concatenate([part.reshape(256, LANES) for part in parts], axis=1)

    outer_forward(f_ref, pick, spec)

    def step(k):
        value = dot(forward_table(fc_ref, fs_ref, row_ref, k), pair_of(spec, k))
        xr, xi = value[:LANES, :LANES], value[LANES:, :LANES]
        gr, gi = value[:LANES, LANES:], value[LANES:, LANES:]
        h = h_ref[k].astype(F32)
        hr, hi = h[:LANES], h[LANES:]
        cross = jnp.concatenate([xr * gr + xi * gi, xr * gi - xi * gr], axis=0)
        cross_ref[k] = cross.astype(BF16)
        real = jnp.concatenate([hr * xr - hi * xi, hr * gr + hi * gi], axis=1)
        imag = jnp.concatenate([hr * xi + hi * xr, hr * gi - hi * gr], axis=1)
        mixed = jnp.concatenate([real, imag], axis=0).astype(BF16)
        put_pair(turns, k, dot(back_table(fc_ref, fs_ref, col_ref, k), mixed))

    inner_loop(step)
    for g in range(8):
        last = outer_back(b_ref, turns, g)
        parts = [last[:, i * LANES : (i + 1) * LANES].reshape(16, 16, LANES) for i in range(2)]
        for i in range(2):
            out_ref[:, 128 * i + 16 * g : 128 * i + 16 * g + 16, :] = parts[i].astype(BF16)
        if g == 0:
            own = firsts[...]
            nothing = jnp.zeros((1, 8, LANES), F32)
            conv, grad, following = (
                jnp.concatenate([part[1:, 0:8], nothing], axis=0) for part in (*parts, own)
            )
            row = iota((16, 8, LANES), 1)
            following = jnp.where((row == 4) | (row == 5), pltpu.roll(conv, 4, 1), following)
            own = jnp.where(row >= 6, pltpu.roll(grad, 6, 1), own)
            out_ref[:, 256:272, :] = jnp.concatenate([following, own], axis=1).astype(BF16)


def conv_both(columns, spectrum, constants):
    h, forward, back = spectrum
    return pl.pallas_call(
        conv_kernel,
        in_specs=[VMEM_SPEC] * 8,
        out_specs=[VMEM_SPEC] * 2,
        out_shape=[
            jax.ShapeDtypeStruct((16, 272, LANES), BF16),
            jax.ShapeDtypeStruct((17, 2 * LANES, LANES), BF16),
        ],
        scratch_shapes=[pltpu.VMEM((34, LANES, 2 * LANES), BF16) for _ in range(2)]
        + [pltpu.VMEM((16, 8, LANES), F32)],
        name="conv_both",
    )(columns, h, *constants, forward, back)


def halving_place(j):
    return ((j & 1) << 3) | (j & 4) | ((j & 8) >> 2) | ((j & 2) >> 1)


def filter_grad_kernel(ids_ref, cross_ref, fc_ref, fs_ref, col_ref, bh_ref, out_ref, turns):
    def step(k):
        put_pair(turns, k, dot(back_table(fc_ref, fs_ref, col_ref, k), cross_ref[k]))

    inner_loop(step)
    for g in range(8):
        part = outer_back(bh_ref, turns, g).reshape(16, 16, LANES)
        for e in range(2):
            place = halving_place((2 * g + e) ^ ids_ref[0])
            for p in range(16):
                out_ref[place, p ^ ids_ref[1]] = part[p, 8 * e : 8 * e + 8].astype(BF16)


def filter_grad(ids, cross, constants, back):
    fc, fs, _, col = constants
    return pl.pallas_call(
        filter_grad_kernel,
        in_specs=[SMEM] + [VMEM_SPEC] * 5,
        out_specs=VMEM_SPEC,
        out_shape=jax.ShapeDtypeStruct((16, 16, 8, LANES), BF16),
        scratch_shapes=[pltpu.VMEM((34, LANES, LANES), BF16)],
        name="filter_grad",
    )(ids, cross, fc, fs, col, back)


def hats_kernel(k_ref, v_ref, take_ref, ids_ref, w_ref, key_ref, value_ref, xs):
    m1, m2 = (mask[0:128] for mask in masks_of(ids_ref))
    take = take_ref[...]
    for s, ref in enumerate((k_ref, v_ref)):
        xs[s, 0:8, :] = jnp.zeros((8, CHUNK), F32)
        xs[s, 8:136, :] = dot(take, ref[...])

    def part(h, carry):
        at = pl.ds(pl.multiple_of(h * LANES, LANES), LANES)
        for s, out_ref in enumerate((key_ref, value_ref)):
            w = w_ref[:, s, at]
            out_ref[:, at] = (
                w[0:1] * xs[s, 8:136, at] + w[1:2] * (xs[s, 7:135, at] * m1) + w[2:3] * (xs[s, 6:134, at] * m2)
            )
        return carry

    lax.fori_loop(0, CHUNK // LANES, part, 0)


def make_hats(received, take, ids, weights):
    channels = weights.shape[2]
    chunks = channels // CHUNK
    return pl.pallas_call(
        hats_kernel,
        grid=(chunks,),
        in_specs=stream_specs(256, chunks)[:2] + [whole(128, 256), whole(144, 1), WEIGHTS],
        out_specs=[column_spec(128)] * 2,
        out_shape=[jax.ShapeDtypeStruct((128, channels), F32)] * 2,
        scratch_shapes=[pltpu.VMEM((2, 136, CHUNK), F32)],
        name="make_hats",
    )(received, received, take, ids, weights)


def edges_of(conv_ref, h):
    edges = conv_ref[h, 256:272, :].astype(F32)
    return edges[0:8], edges[8:16]


def patched(ref, at, own, shift):
    own = pltpu.roll(own, shift, 0) if shift else own
    head = jnp.where(iota((8, LANES), 0) < 2, own, ref[0:8, at])
    return head, ref[8:128, at]


def back_kernel(key_ref, value_ref, give_ref, ids_ref, w_ref, cot_ref, conv_ref, back_ref, one, two):
    give = give_ref[...]
    m1, m2 = masks_of(ids_ref)

    for h in range(CHUNK // LANES):
        at = slice(h * LANES, (h + 1) * LANES)
        following, own = edges_of(conv_ref, h)
        conv = jnp.concatenate([conv_ref[h, 0:128, :].astype(F32), pltpu.roll(following, 4, 0)], axis=0)
        grad_product = jnp.concatenate([conv_ref[h, 128:256, :].astype(F32), pltpu.roll(own, 2, 0)], axis=0)
        cot = jnp.concatenate([cot_ref[:, at].astype(F32), pltpu.roll(following, 2, 0)], axis=0)
        key = jnp.concatenate([*patched(key_ref, at, own, 0), following], axis=0)
        value = jnp.concatenate([*patched(value_ref, at, own, 6), pltpu.roll(following, 6, 0)], axis=0)
        grads = (grad_product * value, grad_product * key, cot * conv)
        for s in range(3):
            w = w_ref[:, s, at]
            grad = grads[s]
            one[s] = grad * m1
            two[s] = grad * m2
            rows = w[0:1] * grad[0:128] + w[1:2] * one[s, 1:129] + w[2:3] * two[s, 2:130]
            sent = dot(give, rows.astype(BF16)).astype(BF16)
            back_ref[:, 16 * s : 16 * s + 16, at] = sent.reshape(16, 16, LANES)


def back_rows(hats, give, ids, weights, cot, local):
    channels = cot.shape[1]
    chunks = channels // CHUNK
    per = CHUNK // LANES
    return pl.pallas_call(
        back_kernel,
        grid=(chunks,),
        in_specs=[
            column_spec(128),
            column_spec(128),
            whole(256, 128),
            whole(144, 1),
            WEIGHTS,
            column_spec(128),
            pl.BlockSpec((per, 272, LANES), lambda c: (c, 0, 0)),
        ],
        out_specs=pl.BlockSpec((16, 48, CHUNK), lambda c: (0, 0, c)),
        out_shape=jax.ShapeDtypeStruct((16, 48, channels), BF16),
        scratch_shapes=[pltpu.VMEM((3, 136, LANES), F32) for _ in range(2)],
        name="back_rows",
    )(*hats, give, ids, weights, cot, local)


def sums_kernel(
    me_ref, k_ref, v_ref, q_ref, take_ref, pk_ref, pv_ref, pq_ref, key_ref, value_ref, ids_ref, w_ref, cot_ref, conv_ref,
    mixed_ref, taps_ref, xs,
):
    take = take_ref[...]
    m1, m2 = (mask[0:128] for mask in masks_of(ids_ref))
    for s, (ref, prev) in enumerate(((k_ref, pk_ref), (v_ref, pv_ref), (q_ref, pq_ref))):
        xs[s, 6:8, :] = prev[...].astype(F32)
        xs[s, 8:136, :] = dot(take, ref[...])

    def part(h, carry):
        at = pl.ds(pl.multiple_of(h * LANES, LANES), LANES)
        block = (CHUNK // LANES) * pl.program_id(0) + h
        side = (block // 8) ^ (me_ref[0] % 2)
        conv = conv_ref[h, 0:128, :].astype(F32)
        grad_product = conv_ref[h, 128:256, :].astype(F32)
        cot = cot_ref[:, at].astype(F32)
        own = edges_of(conv_ref, h)[1]
        key = jnp.concatenate(patched(key_ref, at, own, 0), axis=0)
        value = jnp.concatenate(patched(value_ref, at, own, 6), axis=0)
        grads = (grad_product * value, grad_product * key, cot * conv)
        for s in range(3):
            parts = (xs[s, 8:136, at], xs[s, 7:135, at] * m1, xs[s, 6:134, at] * m2)
            for k in range(3):
                total = jnp.sum(grads[s] * parts[k], axis=0, keepdims=True)
                taps_ref[side, 3 * s + k, pl.ds(block % 8, 1), :] = total
            if s == 2:
                w = w_ref[:, s, at]
                query = w[0:1] * parts[0] + w[1:2] * parts[1] + w[2:3] * parts[2]
                mixed_ref[:, at] = (query * conv).astype(BF16)
        return carry

    lax.fori_loop(0, CHUNK // LANES, part, 0)


def mixed_and_sums(me, received, take, prev, hats, ids, weights, cot, local):
    channels = cot.shape[1]
    chunks = channels // CHUNK
    per = CHUNK // LANES
    return pl.pallas_call(
        sums_kernel,
        grid=(chunks,),
        in_specs=[SMEM]
        + stream_specs(256, chunks)
        + [whole(128, 256)]
        + stream_specs(2, chunks)
        + [
            column_spec(128),
            column_spec(128),
            whole(144, 1),
            WEIGHTS,
            column_spec(128),
            pl.BlockSpec((per, 272, LANES), lambda c: (c, 0, 0)),
        ],
        out_specs=[column_spec(128), whole(2, 9, 8, LANES)],
        out_shape=[
            jax.ShapeDtypeStruct((128, channels), BF16),
            jax.ShapeDtypeStruct((2, 9, 8, LANES), F32),
        ],
        scratch_shapes=[pltpu.VMEM((3, 136, CHUNK), F32)],
        name="mixed_and_sums",
    )(me, received, received, received, take, prev, prev, prev, *hats, ids, weights, cot, local)


def store_kernel(select_ref, in_ref, out_ref):
    width = in_ref.shape[2]
    out_ref[...] = dot_t(select_ref[...], in_ref[...].reshape(256, width)).astype(BF16)


def store_grads(select, returned, channels):
    width = 1024
    chunks = channels // width
    return pl.pallas_call(
        store_kernel,
        grid=(3, chunks),
        in_specs=[
            whole(256, 128),
            pl.BlockSpec((16, 16, width), lambda s, c: (0, s, c)),
        ],
        out_specs=pl.BlockSpec((128, width), lambda s, c: (0, s * chunks + c)),
        out_shape=jax.ShapeDtypeStruct((128, 3 * channels), BF16),
        name="store_grads",
    )(select, returned)


def pack_final_kernel(lags_ref, taps_ref, out_ref):
    lags = lags_ref[...].astype(F32).reshape(128, LANES)
    rows = jnp.concatenate([lags, taps_ref[...].reshape(72, LANES)], axis=0).astype(BF16)
    for d in range(out_ref.shape[0]):
        out_ref[d] = rows


def pack_final(lags, taps, count):
    return pl.pallas_call(
        pack_final_kernel,
        in_specs=[VMEM_SPEC] * 2,
        out_specs=VMEM_SPEC,
        out_shape=jax.ShapeDtypeStruct((count, 200, LANES), BF16),
        name="pack_final",
    )(lags, taps)


def final_kernel(me_ref, in_ref, grad_ref, taps_ref, total):
    for j in range(16):
        at = pl.multiple_of((j ^ me_ref[0]) * LANES, LANES)
        grad_ref[:, pl.ds(at, LANES)] = in_ref[:, 8 * j : 8 * j + 8, :].astype(F32).reshape(128, LANES)
    for side in range(2):
        parts = [in_ref[d, 128:200, :].astype(F32) for d in range(side, 16, 2)]
        total[side] = sum(parts[1:], parts[0]).reshape(9, 8, LANES)
    for i in range(3):
        for c in range(16):
            taps_ref[i, :, c * LANES : (c + 1) * LANES] = total[c // 8, 3 * i : 3 * i + 3, c % 8, :]


def final_parts(me, final):
    return pl.pallas_call(
        final_kernel,
        in_specs=[SMEM, VMEM_SPEC],
        out_specs=[VMEM_SPEC] * 2,
        out_shape=[jax.ShapeDtypeStruct((128, 2048), F32), jax.ShapeDtypeStruct((3, 3, 2048), F32)],
        scratch_shapes=[pltpu.VMEM((2, 9, 8, LANES), F32)],
        name="final_parts",
    )(me, final)


def across(value, axis, bit):
    return lax.ppermute(value, axis, [(i, i ^ bit) for i in range(lax.axis_size(axis))])


def halving_sum(value):
    total = value.astype(F32)
    for bit in (1, 4, 8, 2):
        half = total.shape[0] // 2
        total = total[:half] + across(total[half:].astype(BF16), "dp", bit).astype(F32)
    return total[0]


def cube_exchange(value, axis):
    shape = value.shape
    for bit in (1, 2, 4, 8):
        grouped = value.reshape(shape[0] // (2 * bit), 2, bit, *shape[1:])
        other = across(grouped[:, 1], axis, bit)
        value = jnp.stack([grouped[:, 0], other], axis=1).reshape(shape)
    return value


def total_over(value, axis):
    for bit in (1, 2, 4, 8):
        value = value + across(value, axis, bit)
    return value


def shards(stored, source_row, source_span, segments, short_weight, filter_taps, cotangent):
    dp_count = lax.axis_size("dp")
    my_dp = lax.axis_index("dp").astype(jnp.int32)
    my_seq = lax.axis_index("seq").astype(jnp.int32)
    tok_rows = stored.shape[1]
    width = stored.shape[2]
    channels = width // 3
    span_count = source_span.shape[1]
    span_rows = tok_rows // span_count
    sources = source_row[:, :, 0]
    dp_id, seq_id = my_dp[None], my_seq[None]

    select, take, place = route(dp_id, sources, source_span)
    sent = dot(select, stored[0]).astype(BF16)
    received = exchange(sent.reshape(dp_count, MOST * span_rows, width), "dp")
    received = received.reshape(dp_count * MOST * span_rows, width)

    near = filter_blocks(seq_id, filter_taps)
    near = [near[0]] + [across(near[r], "seq", r) for r in range(1, 8)]
    ids = segments[0] + 1
    outside = jnp.full((6,), -1, jnp.int32)
    ids = jnp.concatenate([outside, shifted(ids[-2:], "seq", 1), ids, shifted(ids[:2], "seq", -1), outside])
    ids = ids.astype(F32)[:, None]

    cot = cotangent[0]
    weights = jnp.transpose(short_weight, (1, 0, 2))
    far = jnp.stack([part[1] for part in near])
    received, near, far, ids, weights = lax.optimization_barrier((received, near, far, ids, weights))

    columns = exchange(gather_rows(received, take, ids, weights, cot), "seq")
    constants = dft_constants()
    spectrum = filter_spectrum(seq_id, constants, [*near, across(far, "seq", 8)])
    hats = make_hats(received, take, ids, weights)
    give = jnp.transpose(take)
    last = lax.dynamic_slice(received, (place[-1, 0], 0), (span_rows, width))[-2:]
    prev = shifted(last, "seq", 1)
    columns, spectrum, hats, give, prev = lax.optimization_barrier((columns, spectrum, hats, give, prev))
    results, cross = conv_both(columns, spectrum, constants)
    local = exchange(results, "seq")
    lags = halving_sum(filter_grad(jnp.stack([my_dp, my_seq]), cross, constants, spectrum[2]))

    back = back_rows(hats, give, ids, weights, cot, local)
    back, local, lags = lax.optimization_barrier((back, local, lags))
    returned = exchange(back, "dp")
    mixed, taps = mixed_and_sums(dp_id, received, take, prev, hats, ids, weights, cot, local)
    lags = cube_exchange(lags.astype(BF16), "seq")
    taps = total_over(taps[0] + across(taps[1], "dp", 1), "seq")
    final = pack_final(lags, taps, dp_count)
    returned, final = lax.optimization_barrier((returned, final))
    final = exchange(final, "dp")
    grad_stored = store_grads(select, returned, channels)
    grad_filter, grad_short = final_parts(seq_id, final)
    return (mixed[None], grad_stored[None], grad_filter, grad_short)


def solution(mesh):
    return jax.shard_map(
        shards,
        mesh=mesh,
        in_specs=(
            P("dp", "seq", None),
            P(None, "seq", None),
            P(None, "seq"),
            P("dp", "seq"),
            P(),
            P("seq", None),
            P("dp", "seq", None),
        ),
        out_specs=(P("dp", "seq", None), P("dp", "seq", None), P("seq", None), P()),
        check_vma=False,
    )
```

```python
import functools
import math

import jax
import jax.numpy as jnp
import numpy as np
from jax import lax
from jax.experimental import pallas as pl
from jax.experimental.pallas import tpu as pltpu
from jax.sharding import PartitionSpec as P

MOST = 2
CHUNK = 512
LANES = 128
F32 = jnp.float32
BF16 = jnp.bfloat16


def shifted(value, axis, by):
    length = lax.axis_size(axis)
    pairs = [(i, i + by) for i in range(length) if 0 <= i + by < length]
    return lax.ppermute(value, axis, pairs)


def exchange(value, axis):
    return lax.all_to_all(value, axis, 0, 0, tiled=True)


def dot(left, right):
    return jnp.dot(left, right, preferred_element_type=F32)


def dot_t(left, right):
    return lax.dot_general(left, right, (((0,), (0,)), ((), ())), preferred_element_type=F32)


def iota(shape, axis):
    return lax.broadcasted_iota(jnp.int32, shape, axis)


def whole(*shape):
    return pl.BlockSpec(shape, lambda *ids: (0,) * len(shape))


SMEM = pl.BlockSpec(memory_space=pltpu.SMEM)


def outer_tables():
    blocks = np.arange(16)
    forward = [np.ones(16), np.cos(np.pi * blocks)]
    back = [np.ones(16), np.cos(np.pi * blocks)]
    for k in range(1, 16):
        angle = 2.0 * np.pi * k * blocks / 32.0
        forward += [np.cos(angle), -np.sin(angle)]
        back += [2.0 * np.cos(angle), -2.0 * np.sin(angle)]
    return np.stack(forward), np.stack(back, axis=1) / 4096.0


def spread_in(table, by):
    rows, cols = table.shape
    tall = (iota((rows * by, rows), 0) // by == iota((rows * by, rows), 1)).astype(BF16)
    wide = (iota((cols, cols * by), 0) == iota((cols, cols * by), 1) // by).astype(BF16)
    value = dot(dot(tall, table).astype(BF16), wide)
    shape = (rows * by, cols * by)
    diagonal = iota(shape, 0) % by == iota(shape, 1) % by
    return jnp.where(diagonal, value, 0.0).astype(BF16)


def dft_constants():
    inner = np.arange(LANES)
    turn = 2.0 * np.pi * (inner[:, None] * inner[None, :] % LANES) / LANES
    order = np.asarray([0, 16] + list(range(1, 16)))
    twist = 2.0 * np.pi * order[:, None] * inner[None, :] / 4096.0
    values = (
        np.cos(turn),
        np.sin(turn),
        np.stack([np.cos(twist), np.sin(twist)], axis=1),
        np.stack([np.cos(twist), np.sin(twist)], axis=2),
    )
    return tuple(jnp.asarray(value, F32) for value in values)


def turned(fc_ref, fs_ref, wc, ws):
    fc = fc_ref[...]
    fs = fs_ref[...]
    return fc * wc - fs * ws, fs * wc + fc * ws


def forward_table(fc_ref, fs_ref, row_ref, k):
    row = row_ref[k]
    cos, sin = turned(fc_ref, fs_ref, row[0:1, :], row[1:2, :])
    cos, sin, minus = cos.astype(BF16), sin.astype(BF16), (-sin).astype(BF16)
    return jnp.concatenate(
        [jnp.concatenate([cos, sin], axis=1), jnp.concatenate([minus, cos], axis=1)], axis=0
    )


def back_table(fc_ref, fs_ref, col_ref, k):
    col = col_ref[k]
    cos, sin = turned(fc_ref, fs_ref, col[:, 0:1], col[:, 1:2])
    cos, sin, minus = cos.astype(BF16), sin.astype(BF16), (-sin).astype(BF16)
    return jnp.concatenate(
        [jnp.concatenate([cos, minus], axis=1), jnp.concatenate([sin, cos], axis=1)], axis=0
    )


def route_kernel(me_ref, source_ref, span_ref, select_ref, take_ref, place_ref):
    sources = source_ref[...].astype(F32)
    mine = (source_ref[...] == me_ref[0]).astype(F32)
    before = (iota((16, 16), 0) < iota((16, 16), 1)).astype(F32)
    earlier = dot(mine, before)
    tall = (iota((256, 16), 0) // 16 == iota((256, 16), 1)).astype(F32)
    slot = iota((256, 16), 0) // 8 % 2
    hit = dot(tall, mine) * (dot(tall, earlier) == slot.astype(F32)).astype(F32)
    start = jnp.sum(hit * (dot(tall, span_ref[...].astype(F32)) * 8.0 + 1.0), axis=1, keepdims=True)
    target = jnp.where(start > 0.5, start - 1.0 + (iota((256, 1), 0) % 8).astype(F32), -1.0)
    select_ref[...] = (iota((256, 128), 1).astype(F32) == target).astype(F32).astype(BF16)

    row = iota((16, 16), 0)
    col = iota((16, 16), 1)
    ours = jnp.sum(jnp.where(row == me_ref[0], sources, 0.0), axis=0, keepdims=True)
    ours_down = jnp.sum(jnp.where(row == col, ours, 0.0), axis=1, keepdims=True)
    order = jnp.sum(((ours_down == ours) & (col < row)).astype(F32), axis=1, keepdims=True)
    place = (ours_down * MOST + order) * 8.0
    place_ref[...] = place.astype(jnp.int32)
    place_across = jnp.sum(jnp.where(row == col, place, 0.0), axis=0, keepdims=True)
    slots = iota((128, 16), 0) // 8 == iota((128, 16), 1)
    target = jnp.sum(jnp.where(slots, place_across, 0.0), axis=1, keepdims=True)
    target = target + (iota((128, 1), 0) % 8).astype(F32)
    take_ref[...] = (iota((128, 256), 1).astype(F32) == target).astype(F32).astype(BF16)


def route(me, sources, spans):
    return pl.pallas_call(
        route_kernel,
        in_specs=[SMEM] + [pl.BlockSpec(memory_space=pltpu.VMEM)] * 2,
        out_specs=[pl.BlockSpec(memory_space=pltpu.VMEM)] * 3,
        out_shape=[
            jax.ShapeDtypeStruct((256, 128), BF16),
            jax.ShapeDtypeStruct((128, 256), BF16),
            jax.ShapeDtypeStruct((16, 1), jnp.int32),
        ],
        name="route",
    )(me, sources, spans)


def filter_blocks_kernel(me_ref, taps_ref, *out_refs):
    for r, out_ref in enumerate(out_refs):
        for h in range(2):
            at = pl.multiple_of((me_ref[0] ^ (r | 8 * h)) * LANES, LANES)
            out_ref[h] = taps_ref[:, pl.ds(at, LANES)].astype(BF16)


def filter_blocks(me, filter_taps):
    return pl.pallas_call(
        filter_blocks_kernel,
        in_specs=[SMEM, pl.BlockSpec(memory_space=pltpu.VMEM)],
        out_specs=[pl.BlockSpec(memory_space=pltpu.VMEM)] * 8,
        out_shape=[jax.ShapeDtypeStruct((2, 128, LANES), BF16)] * 8,
        name="filter_blocks",
    )(me, filter_taps)


def masks_of(ids_ref):
    here = ids_ref[8:144, :]
    return (ids_ref[7:143, :] == here).astype(F32), (ids_ref[6:142, :] == here).astype(F32)


def lags_kernel(take_ref, ids_ref, out_ref, rows):
    rows[0:8, :] = jnp.zeros((8, 256), F32)
    rows[8:136, :] = take_ref[...].astype(F32)
    rows[136:144, :] = jnp.zeros((8, 256), F32)
    m1, m2 = masks_of(ids_ref)
    parts = [rows[8:144, :], rows[7:143, :] * m1, rows[6:142, :] * m2]
    out_ref[...] = jnp.concatenate(parts, axis=0).astype(BF16)


def masked_lags(take, ids):
    return pl.pallas_call(
        lags_kernel,
        in_specs=[VMEM_SPEC] * 2,
        out_specs=VMEM_SPEC,
        out_shape=jax.ShapeDtypeStruct((408, 256), BF16),
        scratch_shapes=[pltpu.VMEM((144, 256), F32)],
        name="masked_lags",
    )(take, ids)


def gather_kernel(k_ref, v_ref, q_ref, lags_ref, w_ref, cot_ref, out_ref, xs, edge):
    lags = lags_ref[...]
    for s, ref in enumerate((k_ref, v_ref, q_ref)):
        xs[s] = dot(lags, ref[...])
    for h in range(CHUNK // LANES):
        at = slice(h * LANES, (h + 1) * LANES)
        hats = []
        for s in range(3):
            w = w_ref[:, s, at]
            hats.append(
                w[0:1] * xs[s, 0:136, at] + w[1:2] * xs[s, 136:272, at] + w[2:3] * xs[s, 272:408, at]
            )
            edge[2 * s : 2 * s + 2, :] = hats[s][0:2]
            edge[2 * s + 8 : 2 * s + 10, :] = hats[s][128:130]
        cot = cot_ref[:, at].astype(F32)
        edge[6:8, :] = cot[0:2]
        edge[14:16, :] = jnp.zeros((2, LANES), F32)
        out_ref[h, 0:128, :] = (hats[0] * hats[1])[0:128].astype(BF16)
        out_ref[h, 128:256, :] = (cot * hats[2][0:128]).astype(BF16)
        out_ref[h, 256:272, :] = edge[...].astype(BF16)


def stream_specs(rows, chunks):
    return [pl.BlockSpec((rows, CHUNK), lambda c, s=s: (0, s * chunks + c)) for s in range(3)]


def column_spec(rows):
    return pl.BlockSpec((rows, CHUNK), lambda c: (0, c))


WEIGHTS = pl.BlockSpec((3, 3, CHUNK), lambda c: (0, 0, c))


def gather_rows(received, lags, weights, cot):
    chunks = cot.shape[1] // CHUNK
    per = CHUNK // LANES
    return pl.pallas_call(
        gather_kernel,
        grid=(chunks,),
        in_specs=stream_specs(256, chunks)
        + [whole(408, 256), WEIGHTS, column_spec(128)],
        out_specs=pl.BlockSpec((per, 272, LANES), lambda c: (c, 0, 0)),
        out_shape=jax.ShapeDtypeStruct((chunks * per, 272, LANES), BF16),
        scratch_shapes=[pltpu.VMEM((3, 408, CHUNK), F32), pltpu.VMEM((16, LANES), F32)],
        name="gather_rows",
    )(received, received, received, lags, weights, cot)


def outer_forward(fh_ref, pick, spec):
    nothing = jnp.zeros(spec.shape[1:], BF16)
    for where in (1, 3):
        spec[where] = nothing
    for g in range(8):
        at = slice(16 * g, 16 * g + 16)
        data = pick(g)
        value = dot(fh_ref[...], data).astype(BF16)
        spec[0, at, :] = value[0:16]
        spec[2, at, :] = value[16:32]
        spec[4:34, at, :] = value[32:512].reshape(30, 16, value.shape[1])


def outer_back(bh_ref, turns, g):
    at = slice(16 * g, 16 * g + 16)
    rest = turns[4:34, at, :].reshape(480, turns.shape[2])
    return dot(bh_ref[...], jnp.concatenate([turns[0, at, :], turns[2, at, :], rest], axis=0))


def pair_of(ref, k):
    return ref[pl.ds(2 * k, 2)].reshape(2 * LANES, ref.shape[2])


def put_pair(ref, k, value):
    ref[pl.ds(2 * k, 2)] = value.astype(BF16).reshape(2, LANES, ref.shape[2])


VMEM_SPEC = pl.BlockSpec(memory_space=pltpu.VMEM)


def inner_loop(step):
    def four(i, carry):
        for j in range(4):
            step(4 * i + j)
        return carry

    lax.fori_loop(0, 4, four, 0)
    step(16)


def filter_kernel(me_ref, fc_ref, fs_ref, row_ref, of_ref, ob_ref, *rest):
    blocks, (out_ref, f_ref, b_ref, ordered, spec) = rest[:9], rest[9:]
    f_ref[...] = spread_in(of_ref[...], 16)
    b_ref[...] = spread_in(ob_ref[...], 16)
    for r in range(8):
        ordered[me_ref[0] ^ r] = blocks[r][0]
        ordered[me_ref[0] ^ (r | 8)] = blocks[8][r]
    outer_forward(f_ref, lambda g: ordered[:, 16 * g : 16 * g + 16, :].reshape(256, LANES), spec)

    def step(k, carry):
        out_ref[k] = dot(forward_table(fc_ref, fs_ref, row_ref, k), pair_of(spec, k)).astype(BF16)
        return carry

    lax.fori_loop(0, 17, step, 0)


def rounded(table):
    return jnp.asarray(np.asarray(table, np.float32).astype(jnp.bfloat16))


def filter_spectrum(me, constants, blocks):
    fc, fs, row, _ = constants
    forward, back = outer_tables()
    return pl.pallas_call(
        filter_kernel,
        in_specs=[SMEM] + [VMEM_SPEC] * 14,
        out_specs=[VMEM_SPEC] * 3,
        out_shape=[
            jax.ShapeDtypeStruct((17, 2 * LANES, LANES), BF16),
            jax.ShapeDtypeStruct((512, 256), BF16),
            jax.ShapeDtypeStruct((256, 512), BF16),
        ],
        scratch_shapes=[pltpu.VMEM((16, 128, LANES), BF16), pltpu.VMEM((34, LANES, LANES), BF16)],
        name="filter_spectrum",
    )(me, fc, fs, row, rounded(forward), rounded(back), *blocks)


def conv_kernel(
    in_ref, h_ref, fc_ref, fs_ref, row_ref, col_ref, f_ref, b_ref, out_ref, cross_ref, spec, turns, firsts,
):
    def pick(g):
        if g:
            parts = [in_ref[:, 128 * i + 16 * g : 128 * i + 16 * g + 16, :] for i in range(2)]
        else:
            edges = in_ref[:, 256:272, :].astype(F32)
            nothing = jnp.zeros((1, 8, LANES), F32)
            filtered = edges[:, 0:8] + jnp.concatenate([nothing, edges[:15, 8:16]], axis=0)
            firsts[...] = filtered
            gated = filtered * pltpu.roll(filtered, 6, 1)
            heads = (gated, pltpu.roll(gated, 4, 1))
            rows = iota((16, 16, LANES), 1)
            parts = []
            for i in range(2):
                head = jnp.concatenate([heads[i], heads[i]], axis=1)
                plain = in_ref[:, 128 * i : 128 * i + 16, :].astype(F32)
                parts.append(jnp.where(rows < 2, head, plain).astype(BF16))
        return jnp.concatenate([part.reshape(256, LANES) for part in parts], axis=1)

    outer_forward(f_ref, pick, spec)

    def step(k):
        value = dot(forward_table(fc_ref, fs_ref, row_ref, k), pair_of(spec, k))
        xr, xi = value[:LANES, :LANES], value[LANES:, :LANES]
        gr, gi = value[:LANES, LANES:], value[LANES:, LANES:]
        h = h_ref[k].astype(F32)
        hr, hi = h[:LANES], h[LANES:]
        cross = jnp.concatenate([xr * gr + xi * gi, xr * gi - xi * gr], axis=0)
        cross_ref[k] = cross.astype(BF16)
        real = jnp.concatenate([hr * xr - hi * xi, hr * gr + hi * gi], axis=1)
        imag = jnp.concatenate([hr * xi + hi * xr, hr * gi - hi * gr], axis=1)
        mixed = jnp.concatenate([real, imag], axis=0).astype(BF16)
        put_pair(turns, k, dot(back_table(fc_ref, fs_ref, col_ref, k), mixed))

    inner_loop(step)
    for g in range(8):
        last = outer_back(b_ref, turns, g)
        parts = [last[:, i * LANES : (i + 1) * LANES].reshape(16, 16, LANES) for i in range(2)]
        for i in range(2):
            out_ref[:, 128 * i + 16 * g : 128 * i + 16 * g + 16, :] = parts[i].astype(BF16)
        if g == 0:
            own = firsts[...]
            nothing = jnp.zeros((1, 8, LANES), F32)
            conv, grad, following = (
                jnp.concatenate([part[1:, 0:8], nothing], axis=0) for part in (*parts, own)
            )
            row = iota((16, 8, LANES), 1)
            following = jnp.where((row == 4) | (row == 5), pltpu.roll(conv, 4, 1), following)
            own = jnp.where(row >= 6, pltpu.roll(grad, 6, 1), own)
            out_ref[:, 256:272, :] = jnp.concatenate([following, own], axis=1).astype(BF16)


def conv_both(columns, spectrum, constants):
    h, forward, back = spectrum
    return pl.pallas_call(
        conv_kernel,
        in_specs=[VMEM_SPEC] * 8,
        out_specs=[VMEM_SPEC] * 2,
        out_shape=[
            jax.ShapeDtypeStruct((16, 272, LANES), BF16),
            jax.ShapeDtypeStruct((17, 2 * LANES, LANES), BF16),
        ],
        scratch_shapes=[pltpu.VMEM((34, LANES, 2 * LANES), BF16) for _ in range(2)]
        + [pltpu.VMEM((16, 8, LANES), F32)],
        name="conv_both",
    )(columns, h, *constants, forward, back)


def halving_place(j):
    return ((j & 1) << 3) | (j & 4) | ((j & 8) >> 2) | ((j & 2) >> 1)


def filter_grad_kernel(ids_ref, cross_ref, fc_ref, fs_ref, col_ref, bh_ref, out_ref, turns):
    def step(k):
        put_pair(turns, k, dot(back_table(fc_ref, fs_ref, col_ref, k), cross_ref[k]))

    inner_loop(step)
    for g in range(8):
        part = outer_back(bh_ref, turns, g).reshape(16, 16, LANES)
        for e in range(2):
            place = halving_place((2 * g + e) ^ ids_ref[0])
            for p in range(16):
                out_ref[place, p ^ ids_ref[1]] = part[p, 8 * e : 8 * e + 8].astype(BF16)


def filter_grad(ids, cross, constants, back):
    fc, fs, _, col = constants
    return pl.pallas_call(
        filter_grad_kernel,
        in_specs=[SMEM] + [VMEM_SPEC] * 5,
        out_specs=VMEM_SPEC,
        out_shape=jax.ShapeDtypeStruct((16, 16, 8, LANES), BF16),
        scratch_shapes=[pltpu.VMEM((34, LANES, LANES), BF16)],
        name="filter_grad",
    )(ids, cross, fc, fs, col, back)


def hats_kernel(k_ref, v_ref, take_ref, ids_ref, w_ref, key_ref, value_ref, xs):
    m1, m2 = (mask[0:128] for mask in masks_of(ids_ref))
    take = take_ref[...]
    for s, ref in enumerate((k_ref, v_ref)):
        xs[s, 0:8, :] = jnp.zeros((8, CHUNK), F32)
        xs[s, 8:136, :] = dot(take, ref[...])

    def part(h, carry):
        at = pl.ds(pl.multiple_of(h * LANES, LANES), LANES)
        for s, out_ref in enumerate((key_ref, value_ref)):
            w = w_ref[:, s, at]
            out_ref[:, at] = (
                w[0:1] * xs[s, 8:136, at] + w[1:2] * (xs[s, 7:135, at] * m1) + w[2:3] * (xs[s, 6:134, at] * m2)
            )
        return carry

    lax.fori_loop(0, CHUNK // LANES, part, 0)


def make_hats(received, take, ids, weights):
    channels = weights.shape[2]
    chunks = channels // CHUNK
    return pl.pallas_call(
        hats_kernel,
        grid=(chunks,),
        in_specs=stream_specs(256, chunks)[:2] + [whole(128, 256), whole(144, 1), WEIGHTS],
        out_specs=[column_spec(128)] * 2,
        out_shape=[jax.ShapeDtypeStruct((128, channels), F32)] * 2,
        scratch_shapes=[pltpu.VMEM((2, 136, CHUNK), F32)],
        name="make_hats",
    )(received, received, take, ids, weights)


def edges_of(conv_ref, h):
    edges = conv_ref[h, 256:272, :].astype(F32)
    return edges[0:8], edges[8:16]


def patched(ref, at, own, shift):
    own = pltpu.roll(own, shift, 0) if shift else own
    head = jnp.where(iota((8, LANES), 0) < 2, own, ref[0:8, at])
    return head, ref[8:128, at]


def back_kernel(key_ref, value_ref, give_ref, ids_ref, w_ref, cot_ref, conv_ref, back_ref, one, two):
    give = give_ref[...]
    m1, m2 = masks_of(ids_ref)

    for h in range(CHUNK // LANES):
        at = slice(h * LANES, (h + 1) * LANES)
        following, own = edges_of(conv_ref, h)
        conv = jnp.concatenate([conv_ref[h, 0:128, :].astype(F32), pltpu.roll(following, 4, 0)], axis=0)
        grad_product = jnp.concatenate([conv_ref[h, 128:256, :].astype(F32), pltpu.roll(own, 2, 0)], axis=0)
        cot = jnp.concatenate([cot_ref[:, at].astype(F32), pltpu.roll(following, 2, 0)], axis=0)
        key = jnp.concatenate([*patched(key_ref, at, own, 0), following], axis=0)
        value = jnp.concatenate([*patched(value_ref, at, own, 6), pltpu.roll(following, 6, 0)], axis=0)
        grads = (grad_product * value, grad_product * key, cot * conv)
        for s in range(3):
            w = w_ref[:, s, at]
            grad = grads[s]
            one[s] = grad * m1
            two[s] = grad * m2
            rows = w[0:1] * grad[0:128] + w[1:2] * one[s, 1:129] + w[2:3] * two[s, 2:130]
            sent = dot(give, rows.astype(BF16)).astype(BF16)
            back_ref[:, 16 * s : 16 * s + 16, at] = sent.reshape(16, 16, LANES)


def back_rows(hats, give, ids, weights, cot, local):
    channels = cot.shape[1]
    chunks = channels // CHUNK
    per = CHUNK // LANES
    return pl.pallas_call(
        back_kernel,
        grid=(chunks,),
        in_specs=[
            column_spec(128),
            column_spec(128),
            whole(256, 128),
            whole(144, 1),
            WEIGHTS,
            column_spec(128),
            pl.BlockSpec((per, 272, LANES), lambda c: (c, 0, 0)),
        ],
        out_specs=pl.BlockSpec((16, 48, CHUNK), lambda c: (0, 0, c)),
        out_shape=jax.ShapeDtypeStruct((16, 48, channels), BF16),
        scratch_shapes=[pltpu.VMEM((3, 136, LANES), F32) for _ in range(2)],
        name="back_rows",
    )(*hats, give, ids, weights, cot, local)


def sums_kernel(
    me_ref, k_ref, v_ref, q_ref, take_ref, pk_ref, pv_ref, pq_ref, key_ref, value_ref, ids_ref, w_ref, cot_ref, conv_ref,
    mixed_ref, taps_ref, xs,
):
    take = take_ref[...]
    m1, m2 = (mask[0:128] for mask in masks_of(ids_ref))
    for s, (ref, prev) in enumerate(((k_ref, pk_ref), (v_ref, pv_ref), (q_ref, pq_ref))):
        xs[s, 6:8, :] = prev[...].astype(F32)
        xs[s, 8:136, :] = dot(take, ref[...])

    def part(h, carry):
        at = pl.ds(pl.multiple_of(h * LANES, LANES), LANES)
        block = (CHUNK // LANES) * pl.program_id(0) + h
        side = (block // 8) ^ (me_ref[0] % 2)
        conv = conv_ref[h, 0:128, :].astype(F32)
        grad_product = conv_ref[h, 128:256, :].astype(F32)
        cot = cot_ref[:, at].astype(F32)
        own = edges_of(conv_ref, h)[1]
        key = jnp.concatenate(patched(key_ref, at, own, 0), axis=0)
        value = jnp.concatenate(patched(value_ref, at, own, 6), axis=0)
        grads = (grad_product * value, grad_product * key, cot * conv)
        for s in range(3):
            parts = (xs[s, 8:136, at], xs[s, 7:135, at] * m1, xs[s, 6:134, at] * m2)
            for k in range(3):
                total = jnp.sum(grads[s] * parts[k], axis=0, keepdims=True)
                taps_ref[side, 3 * s + k, pl.ds(block % 8, 1), :] = total
            if s == 2:
                w = w_ref[:, s, at]
                query = w[0:1] * parts[0] + w[1:2] * parts[1] + w[2:3] * parts[2]
                mixed_ref[:, at] = (query * conv).astype(BF16)
        return carry

    lax.fori_loop(0, CHUNK // LANES, part, 0)


def mixed_and_sums(me, received, take, prev, hats, ids, weights, cot, local):
    channels = cot.shape[1]
    chunks = channels // CHUNK
    per = CHUNK // LANES
    return pl.pallas_call(
        sums_kernel,
        grid=(chunks,),
        in_specs=[SMEM]
        + stream_specs(256, chunks)
        + [whole(128, 256)]
        + stream_specs(2, chunks)
        + [
            column_spec(128),
            column_spec(128),
            whole(144, 1),
            WEIGHTS,
            column_spec(128),
            pl.BlockSpec((per, 272, LANES), lambda c: (c, 0, 0)),
        ],
        out_specs=[column_spec(128), whole(2, 9, 8, LANES)],
        out_shape=[
            jax.ShapeDtypeStruct((128, channels), BF16),
            jax.ShapeDtypeStruct((2, 9, 8, LANES), F32),
        ],
        scratch_shapes=[pltpu.VMEM((3, 136, CHUNK), F32)],
        name="mixed_and_sums",
    )(me, received, received, received, take, prev, prev, prev, *hats, ids, weights, cot, local)


def store_kernel(select_ref, in_ref, out_ref):
    width = in_ref.shape[2]
    out_ref[...] = dot_t(select_ref[...], in_ref[...].reshape(256, width)).astype(BF16)


def store_grads(select, returned, channels):
    width = 1024
    chunks = channels // width
    return pl.pallas_call(
        store_kernel,
        grid=(3, chunks),
        in_specs=[
            whole(256, 128),
            pl.BlockSpec((16, 16, width), lambda s, c: (0, s, c)),
        ],
        out_specs=pl.BlockSpec((128, width), lambda s, c: (0, s * chunks + c)),
        out_shape=jax.ShapeDtypeStruct((128, 3 * channels), BF16),
        name="store_grads",
    )(select, returned)


def pack_final_kernel(lags_ref, taps_ref, out_ref):
    lags = lags_ref[...].astype(F32).reshape(128, LANES)
    rows = jnp.concatenate([lags, taps_ref[...].reshape(72, LANES)], axis=0).astype(BF16)
    for d in range(out_ref.shape[0]):
        out_ref[d] = rows


def pack_final(lags, taps, count):
    return pl.pallas_call(
        pack_final_kernel,
        in_specs=[VMEM_SPEC] * 2,
        out_specs=VMEM_SPEC,
        out_shape=jax.ShapeDtypeStruct((count, 200, LANES), BF16),
        name="pack_final",
    )(lags, taps)


def final_kernel(me_ref, in_ref, grad_ref, taps_ref, total):
    for j in range(16):
        at = pl.multiple_of((j ^ me_ref[0]) * LANES, LANES)
        grad_ref[:, pl.ds(at, LANES)] = in_ref[:, 8 * j : 8 * j + 8, :].astype(F32).reshape(128, LANES)
    for side in range(2):
        parts = [in_ref[d, 128:200, :].astype(F32) for d in range(side, 16, 2)]
        total[side] = sum(parts[1:], parts[0]).reshape(9, 8, LANES)
    for i in range(3):
        for c in range(16):
            taps_ref[i, :, c * LANES : (c + 1) * LANES] = total[c // 8, 3 * i : 3 * i + 3, c % 8, :]


def final_parts(me, final):
    return pl.pallas_call(
        final_kernel,
        in_specs=[SMEM, VMEM_SPEC],
        out_specs=[VMEM_SPEC] * 2,
        out_shape=[jax.ShapeDtypeStruct((128, 2048), F32), jax.ShapeDtypeStruct((3, 3, 2048), F32)],
        scratch_shapes=[pltpu.VMEM((2, 9, 8, LANES), F32)],
        name="final_parts",
    )(me, final)


def across(value, axis, bit):
    return lax.ppermute(value, axis, [(i, i ^ bit) for i in range(lax.axis_size(axis))])


def halving_sum(value):
    total = value.astype(F32)
    for bit in (1, 4, 8, 2):
        half = total.shape[0] // 2
        total = total[:half] + across(total[half:].astype(BF16), "dp", bit).astype(F32)
    return total[0]


def cube_exchange(value, axis):
    shape = value.shape
    for bit in (1, 2, 4, 8):
        grouped = value.reshape(shape[0] // (2 * bit), 2, bit, *shape[1:])
        other = across(grouped[:, 1], axis, bit)
        value = jnp.stack([grouped[:, 0], other], axis=1).reshape(shape)
    return value


def total_over(value, axis):
    for bit in (1, 2, 4, 8):
        value = value + across(value, axis, bit)
    return value


def shards(stored, source_row, source_span, segments, short_weight, filter_taps, cotangent):
    dp_count = lax.axis_size("dp")
    my_dp = lax.axis_index("dp").astype(jnp.int32)
    my_seq = lax.axis_index("seq").astype(jnp.int32)
    tok_rows = stored.shape[1]
    width = stored.shape[2]
    channels = width // 3
    span_count = source_span.shape[1]
    span_rows = tok_rows // span_count
    sources = source_row[:, :, 0]
    dp_id, seq_id = my_dp[None], my_seq[None]

    select, take, place = route(dp_id, sources, source_span)
    sent = dot(select, stored[0]).astype(BF16)
    received = exchange(sent.reshape(dp_count, MOST * span_rows, width), "dp")
    received = received.reshape(dp_count * MOST * span_rows, width)

    near = filter_blocks(seq_id, filter_taps)
    near = [near[0]] + [across(near[r], "seq", r) for r in range(1, 8)]
    ids = segments[0] + 1
    outside = jnp.full((6,), -1, jnp.int32)
    ids = jnp.concatenate([outside, shifted(ids[-2:], "seq", 1), ids, shifted(ids[:2], "seq", -1), outside])
    ids = ids.astype(F32)[:, None]

    cot = cotangent[0]
    weights = jnp.transpose(short_weight, (1, 0, 2))
    lag_rows = masked_lags(take, ids)
    far = jnp.stack([part[1] for part in near])
    received, near, far, ids, weights, lag_rows = lax.optimization_barrier(
        (received, near, far, ids, weights, lag_rows)
    )

    columns = exchange(gather_rows(received, lag_rows, weights, cot), "seq")
    constants = dft_constants()
    spectrum = filter_spectrum(seq_id, constants, [*near, across(far, "seq", 8)])
    hats = make_hats(received, take, ids, weights)
    give = jnp.transpose(take)
    last = lax.dynamic_slice(received, (place[-1, 0], 0), (span_rows, width))[-2:]
    prev = shifted(last, "seq", 1)
    columns, spectrum, hats, give, prev = lax.optimization_barrier((columns, spectrum, hats, give, prev))
    results, cross = conv_both(columns, spectrum, constants)
    local = exchange(results, "seq")
    lags = halving_sum(filter_grad(jnp.stack([my_dp, my_seq]), cross, constants, spectrum[2]))

    back = back_rows(hats, give, ids, weights, cot, local)
    back, local, lags = lax.optimization_barrier((back, local, lags))
    returned = exchange(back, "dp")
    mixed, taps = mixed_and_sums(dp_id, received, take, prev, hats, ids, weights, cot, local)
    lags = cube_exchange(lags.astype(BF16), "seq")
    taps = total_over(taps[0] + across(taps[1], "dp", 1), "seq")
    final = pack_final(lags, taps, dp_count)
    returned, final = lax.optimization_barrier((returned, final))
    final = exchange(final, "dp")
    grad_stored = store_grads(select, returned, channels)
    grad_filter, grad_short = final_parts(seq_id, final)
    return (mixed[None], grad_stored[None], grad_filter, grad_short)


def solution(mesh):
    return jax.shard_map(
        shards,
        mesh=mesh,
        in_specs=(
            P("dp", "seq", None),
            P(None, "seq", None),
            P(None, "seq"),
            P("dp", "seq"),
            P(),
            P("seq", None),
            P("dp", "seq", None),
        ),
        out_specs=(P("dp", "seq", None), P("dp", "seq", None), P("seq", None), P()),
        check_vma=False,
    )
```
